32 devices in a mesh: rep: 4 (over z), fsdp: 8 (over y, x, core).
Axes of the slice: x: 2, y: 2, z: 4, core: 2. Of those that a mesh axis runs over, the one named last changes fastest.
Arguments:
- tokens: bfloat16 [4, 2, 512, 2048], P('rep', None, 'fsdp'), may hold values from -6 to 6
- cotangent: bfloat16 [4, 2, 512, 2048], P('rep', None, 'fsdp'), may hold values from -6 to 6
- mixer_gain: bfloat16 [2048], replicated, may hold values from 0.5 to 1.5
- query_weight: bfloat16 [2048, 2048], P('fsdp'), may hold values from -0.125 to 0.125
- key_weight: bfloat16 [2048, 256], P('fsdp'), may hold values from -0.125 to 0.125
- value_weight: bfloat16 [2048, 256], P('fsdp'), may hold values from -0.125 to 0.125
- output_weight: bfloat16 [2048, 2048], P('fsdp'), may hold values from -1.5 to 1.5
- feed_gain: bfloat16 [2048], replicated, may hold values from 0.5 to 1.5
- gate_weight: bfloat16 [2048, 5632], P('fsdp'), may hold values from -0.125 to 0.125
- up_weight: bfloat16 [2048, 5632], P('fsdp'), may hold values from -0.125 to 0.125
- down_weight: bfloat16 [5632, 2048], P('fsdp'), may hold values from -0.078125 to 0.078125
- doc_ids: int32 [4, 2, 512], P('rep'), may hold values from 0 to 2, never falling along the last dimension, each value on 1 to 256 neighbouring positions
- prefix_len: int32 [4, 2, 3], P('rep'), may hold values from 13 to 128
- block_order: int32 [4, 2, 16], P('rep'), may hold values from 0 to 15, each once within a row
Outputs:
- layer_out: bfloat16 [4, 2, 512, 2048], P('rep', None, 'fsdp')
- input_grad: bfloat16 [4, 2, 512, 2048], P('rep', None, 'fsdp')
- mixer_grad: float32 [2048], replicated
- query_grad: float32 [2048, 2048], P('fsdp')
- key_grad: float32 [2048, 256], P('fsdp')
- value_grad: float32 [2048, 256], P('fsdp')
- output_grad: float32 [2048, 2048], P('fsdp')
- feed_grad: float32 [2048], replicated
- gate_grad: float32 [2048, 5632], P('fsdp')
- up_grad: float32 [2048, 5632], P('fsdp')
- down_grad: float32 [5632, 2048], P('fsdp')
The draws below stay inside these ranges and needn't reach their ends.
Inputs may be any that keep to these rules, and one draw needn't show every extreme that they name: `doc_ids`: in each packed row the document numbers never fall, each of 0 to 2 occurs, and one document has exactly 256 tokens. `block_order`: each row names every block exactly once.
All inputs are finite; a program needn't handle non-finite values.
Results may differ from the reference program's by a relative error of at most 0.015.
Values may be sent and summed in bfloat16 or wider, within the bound.
No kernel may reach another device: no remote copies, remote signals or barrier semaphores. Data moves between devices by JAX's collectives and lax.ppermute only.
A program may use at most 896 MiB of HBM per device.

```python
import math
import jax
import jax.numpy as jnp
import numpy as np
from jax import lax

D = 2048
HEADS = 32
KV_HEADS = 4
HEAD_DIM = 64
FF = 5632
MICRO = 2
SEGS = 3
KVD = 256
LEN = 512
BLOCKS = 16
GROUPS = 4


def set_ends(drawn, rng, least, top_value):
    longest = drawn.shape.index(max(drawn.shape))
    spots = []
    for shift in (0, 1):
        where = [jax.random.randint(jax.random.fold_in(rng, axis), (), 0, length) for axis, length in enumerate(drawn.shape)]
        where[longest] = (where[longest] + shift) % drawn.shape[longest]
        spots.append(tuple(where))
    return drawn.at[spots[0]].set(least).at[spots[1]].set(top_value)


def level_of(key, dims, split, low, top_value):
    def one(dim, parts):
        draws = jax.random.uniform(jax.random.fold_in(jax.random.fold_in(key, 6), dim), (parts,), jnp.float32, low / len(split), top_value / len(split))
        return jnp.repeat(jnp.exp(draws), dims[dim] // parts).reshape((-1,) + (1,) * (len(dims) - dim - 1))

    gain = one(*split[0])
    for cut in split[1:]:
        gain = gain * one(*cut)
    return gain


def split_up(count, total, most, slope):
    weights = [(1 << 20) // math.isqrt(standing ** slope) + 1 for standing in range(2, count + 1)]
    rest, counts = total - most - (count - 1), [1] * (count - 1)
    while rest > 0:
        candidates = [i for i in range(count - 1) if counts[i] < most]
        whole, remaining = sum([weights[i] for i in candidates]), rest
        for i in candidates:
            more = min(most - counts[i], max(1, remaining * weights[i] // whole), rest)
            counts[i] = counts[i] + more
            rest = rest - more
    return np.array([most] + counts)


def uneven(rng, amount, total, bound, skew):
    if amount == 2:
        one = jax.random.randint(rng, (), max(1, total - bound), min(bound, total - 1) + 1)
        return jnp.stack([one, total - one])
    lengths = jnp.asarray(split_up(amount, total, bound, skew), jnp.int32)
    pairs = (amount - 1) // 2
    giver, receiver = lengths[1:1 + 2 * pairs:2], lengths[2:2 + 2 * pairs:2]
    margin = jnp.minimum(giver - 1, bound - receiver)
    moved = jax.random.randint(jax.random.fold_in(rng, 1), (pairs,), 0, 1 << 20) % (margin + 1)
    lengths = lengths.at[1:1 + 2 * pairs:2].set(giver - moved).at[2:2 + 2 * pairs:2].set(receiver + moved)
    return lengths[jax.random.permutation(jax.random.fold_in(rng, 2), amount)]


def normal_values(key, shape, spread, bound, pieces=(), kind=jnp.bfloat16):
    values = jax.random.normal(key, shape, jnp.float32) * spread
    if len(pieces) > 0:
        values = level_of(key, shape, pieces, -0.22, 0.18) * values
    return jnp.clip(values, min=-bound, max=bound).astype(kind)


def setup_inputs(seed: int = 0) -> dict:
    arg_keys = jax.random.split(jax.random.key(seed), 15)
    return {
        "tokens": normal_values(arg_keys[0], (GROUPS, MICRO, LEN, D), 1.0, 6.0, ((0, 4), (2, 8))),
        "cotangent": normal_values(arg_keys[1], (GROUPS, MICRO, LEN, D), 1.0, 6.0, ((0, 4), (2, 8))),
        "mixer_gain": jnp.clip(1.0 + 0.1 * jax.random.normal(arg_keys[2], (D,), jnp.float32), 0.5, 1.5).astype(jnp.bfloat16),
        "query_weight": normal_values(arg_keys[3], (D, D), D ** -0.5, 0.125, ((0, 8),)),
        "key_weight": normal_values(arg_keys[4], (D, KVD), D ** -0.5, 0.125, ((0, 8),)),
        "value_weight": normal_values(arg_keys[5], (D, KVD), D ** -0.5, 0.125, ((0, 8),)),
        "output_weight": normal_values(arg_keys[6], (D, D), (max(D // 128, 1)) ** -0.5, 1.5, ((0, 8),)),
        "feed_gain": jnp.clip(1.0 + 0.1 * jax.random.normal(arg_keys[7], (D,), jnp.float32), 0.5, 1.5).astype(jnp.bfloat16),
        "gate_weight": normal_values(arg_keys[8], (D, FF), D ** -0.5, 0.125, ((0, 8),)),
        "up_weight": normal_values(arg_keys[9], (D, FF), D ** -0.5, 0.125, ((0, 8),)),
        "down_weight": normal_values(arg_keys[10], (FF, D), FF ** -0.5, 0.078125, ((0, 8),)),
        "doc_ids": jax.vmap(lambda own: jnp.searchsorted(jnp.cumsum(uneven(own, SEGS, LEN, LEN // 2, 2)), jnp.arange(LEN), side="right"))(jax.random.split(arg_keys[11], GROUPS * MICRO)).reshape((GROUPS, MICRO, LEN)).astype(jnp.int32),
        "prefix_len": set_ends(jax.random.randint(arg_keys[12], (GROUPS, MICRO, SEGS), 1 + LEN // 40, LEN // 4 + 1), jax.random.fold_in(arg_keys[12], 1), 1 + LEN // 40, (LEN // 4 + 1) - 1).astype(jnp.int32),
        "block_order": jax.vmap(lambda own: jax.random.permutation(own, BLOCKS))(jax.random.split(arg_keys[13], GROUPS * MICRO)).reshape((GROUPS, MICRO, BLOCKS)).astype(jnp.int32),
    }


highest = lax.Precision.HIGHEST
epsilon = 1e-05

@jax.custom_vjp
def low(v):
    return lax.optimization_barrier(v.astype(jnp.bfloat16)).astype(jnp.float32)

@jax.custom_vjp
def low_back(v):
    return v

def low_keep(v):
    return (low(v), None)

def low_pass(kept, grad):
    return (grad,)

def back_keep(v):
    return (v, None)

def back_low(kept, grad):
    return (low(grad),)
low.defvjp(low_keep, low_pass)
low_back.defvjp(back_keep, back_low)

def positions(order_row, doc_row, prefix_row, length):
    count = order_row.shape[0]
    block_width = length // count
    index = jnp.arange(length, dtype=jnp.int32)
    slot = index // block_width
    block = lax.optimization_barrier(jnp.sum(jnp.where(slot[:, None] == jnp.arange(count, dtype=jnp.int32)[None, :], order_row[None, :], 0), axis=1, dtype=jnp.int32))
    place = (block * block_width + index % block_width).astype(jnp.int32)
    labels = jnp.arange(SEGS, dtype=jnp.int32)
    starts = lax.optimization_barrier(jnp.sum((doc_row[None, :] < labels[:, None]).astype(jnp.int32), axis=1, dtype=jnp.int32))
    member = lax.optimization_barrier(jnp.sum((place[:, None] >= starts[None, 1:]).astype(jnp.int32), axis=1, dtype=jnp.int32))
    picked = member[:, None] == labels[None, :]
    start_of = lax.optimization_barrier(jnp.sum(jnp.where(picked, starts[None, :], 0), axis=1, dtype=jnp.int32))
    limit = lax.optimization_barrier(jnp.sum(jnp.where(picked, starts[None, :] + prefix_row[None, :], 0), axis=1, dtype=jnp.int32))
    return (place, member, place - start_of, limit)

def angles_for(relative):
    halfway = HEAD_DIM // 2
    frequency = 10000.0 ** (-(2.0 * jnp.arange(halfway, dtype=jnp.float32)) / HEAD_DIM)
    return relative.astype(jnp.float32)[:, None] * frequency[None, :]

def rotary(field, angle, sign):
    halfway = field.shape[-1] // 2
    cosine = jnp.cos(angle)[:, None, :]
    sine = sign * jnp.sin(angle)[:, None, :]
    front = field[..., :halfway]
    behind = field[..., halfway:]
    return jnp.concatenate([front * cosine - behind * sine, behind * cosine + front * sine], axis=-1)

def matmul(left, right):
    return jnp.dot(left, right, precision=highest)

def layer(values, gain_mixer, weight_query, weight_key, weight_value, weight_output, gain_feed, weight_gate, weight_up, weight_down, angle, visible):
    length = values.shape[0]
    grouped = HEADS // KV_HEADS
    scale = HEAD_DIM ** (-0.5)
    normed = low(values * lax.rsqrt(lax.optimization_barrier(jnp.mean(values * values, axis=1, keepdims=True)) + epsilon) * gain_mixer)
    query = low(rotary(low_back(matmul(normed, weight_query)).reshape(length, HEADS, HEAD_DIM), angle, 1.0))
    keys = low(rotary(low_back(matmul(normed, weight_key)).reshape(length, KV_HEADS, HEAD_DIM), angle, 1.0))
    vals = low(low_back(matmul(normed, weight_value))).reshape(length, KV_HEADS, HEAD_DIM)
    query_groups = query.reshape(length, KV_HEADS, grouped, HEAD_DIM).transpose(1, 2, 0, 3)
    key_groups = keys.transpose(1, 0, 2)
    value_groups = vals.transpose(1, 0, 2)

    def attend_head(items):
        query_head, key_head, value_head = items
        scores = low_back(jnp.einsum('gtd,jd->gtj', query_head, key_head, precision=highest) * scale)
        scores = jnp.where(visible[None], scores, -1000000000.0)
        probs = low(jax.nn.softmax(scores, axis=-1))
        return jnp.einsum('gtj,jd->gtd', probs, value_head, precision=highest)
    mixed = lax.map(jax.checkpoint(attend_head), (query_groups, key_groups, value_groups))
    attended = low(low_back(mixed.transpose(2, 0, 1, 3).reshape(length, HEADS * HEAD_DIM)))
    hidden = values + low_back(matmul(attended, weight_output))
    normed_two = low(hidden * lax.rsqrt(lax.optimization_barrier(jnp.mean(hidden * hidden, axis=1, keepdims=True)) + epsilon) * gain_feed)
    gate = low_back(matmul(normed_two, weight_gate))
    upward = low_back(matmul(normed_two, weight_up))
    inner = low(jax.nn.silu(gate) * upward)
    return hidden + low_back(matmul(inner, weight_down))

def reference(tokens, cotangent, mixer_gain, query_weight, key_weight, value_weight, output_weight, feed_gain, gate_weight, up_weight, down_weight, doc_ids, prefix_len, block_order):
    weights = tuple((w_item.astype(jnp.float32) for w_item in (mixer_gain, query_weight, key_weight, value_weight, output_weight, feed_gain, gate_weight, up_weight, down_weight)))
    row_count = GROUPS * MICRO
    token_rows = tokens.reshape(row_count, LEN, D)
    grad_rows = cotangent.reshape(row_count, LEN, D)
    doc_rows = doc_ids.reshape(row_count, LEN)
    prefix_rows = prefix_len.reshape(row_count, SEGS)
    order_rows = block_order.reshape(row_count, BLOCKS)

    def one_row(running, items):
        token_row, grad_row, doc_row, prefix_row, order_row = items
        place, member, relative, limit = positions(order_row, doc_row, prefix_row, LEN)
        angle = angles_for(relative)
        visible = (member[:, None] == member[None, :]) & ((place[None, :] <= place[:, None]) | (place[None, :] < limit[None, :]))

        def forward(values, *params):
            return layer(values, *params, angle, visible)
        result, pull = jax.vjp(forward, token_row.astype(jnp.float32), *weights)
        grads = pull(grad_row.astype(jnp.float32))
        running = tuple((acc + part for acc, part in zip(running, grads[1:])))
        return (running, (result.astype(jnp.bfloat16), grads[0].astype(jnp.bfloat16)))
    initial = tuple((jnp.zeros(w_item.shape, jnp.float32) for w_item in weights))
    totals, (outputs, input_grads) = lax.scan(one_row, initial, (token_rows, grad_rows, doc_rows, prefix_rows, order_rows))
    return (outputs.reshape(tokens.shape), input_grads.reshape(tokens.shape), totals[0], totals[1], totals[2], totals[3], totals[4], totals[5], totals[6], totals[7], totals[8])
```

```python
import jax
import jax.numpy as jnp
from jax import lax
from jax.sharding import PartitionSpec as P

HEADS = 32
KV_HEADS = 4
HEAD_DIM = 64
MICRO = 2
SEGS = 3


epsilon = 1e-05


def positions(order_row, doc_row, prefix_row, length):
    count = order_row.shape[0]
    block_width = length // count
    index = jnp.arange(length, dtype=jnp.int32)
    slot = index // block_width
    block = jnp.sum(
        jnp.where(
            slot[:, None] == jnp.arange(count, dtype=jnp.int32)[None, :], order_row[None, :], 0
        ),
        axis=1,
        dtype=jnp.int32,
    )
    place = block * block_width + index % block_width
    labels = jnp.arange(SEGS, dtype=jnp.int32)
    starts = jnp.sum(
        (doc_row[None, :] < labels[:, None]).astype(jnp.int32), axis=1, dtype=jnp.int32
    )
    member = jnp.sum(
        (place[:, None] >= starts[None, 1:]).astype(jnp.int32), axis=1, dtype=jnp.int32
    )
    picked = member[:, None] == labels[None, :]
    start_of = jnp.sum(jnp.where(picked, starts[None, :], 0), axis=1, dtype=jnp.int32)
    limit = jnp.sum(
        jnp.where(picked, starts[None, :] + prefix_row[None, :], 0), axis=1, dtype=jnp.int32
    )
    return (place, member, place - start_of, limit)


def angles_for(relative):
    halfway = HEAD_DIM // 2
    frequency = 10000.0 ** (-(2.0 * jnp.arange(halfway, dtype=jnp.float32)) / HEAD_DIM)
    return relative.astype(jnp.float32)[:, None] * frequency[None, :]


def rotary(field, angle, sign):
    halfway = field.shape[-1] // 2
    cosine = jnp.cos(angle)[:, None, :]
    sine = sign * jnp.sin(angle)[:, None, :]
    front = field[..., :halfway]
    behind = field[..., halfway:]
    return jnp.concatenate(
        [front * cosine - behind * sine, behind * cosine + front * sine], axis=-1
    )


def rms_scale(values, gain):
    return values * lax.rsqrt(jnp.mean(values * values, axis=1, keepdims=True) + epsilon) * gain


def gated(gate_part, up_part):
    return jax.nn.silu(gate_part) * up_part


def contract_rows(left, right):
    return lax.dot_general(
        left, right, (((0,), (0,)), ((), ())), preferred_element_type=jnp.float32
    )


def times_transpose(left, right):
    return lax.dot_general(
        left, right, (((1,), (1,)), ((), ())), preferred_element_type=jnp.float32
    )


def local(
    tokens,
    cotangent,
    mixer_gain,
    query_weight,
    key_weight,
    value_weight,
    output_weight,
    feed_gain,
    gate_weight,
    up_weight,
    down_weight,
    doc_ids,
    prefix_len,
    block_order,
):
    micro, tok_count, width = tokens.shape[1:]
    devices = lax.axis_size("fsdp")
    length = tok_count * devices
    own_rows = micro * tok_count
    all_rows = own_rows * devices
    shard_rows = width // devices
    heads_here = HEADS // devices
    grouped = HEADS // KV_HEADS
    sharing = devices // KV_HEADS
    query_width = heads_here * HEAD_DIM
    hidden_width = down_weight.shape[0]
    scale = HEAD_DIM ** (-0.5)
    gain_mixer = mixer_gain.astype(jnp.float32)
    gain_feed = feed_gain.astype(jnp.float32)

    def gather_rows(rows):
        return lax.all_gather(rows, "fsdp", axis=0, tiled=True)

    def scatter_sum(partial):
        return lax.psum_scatter(
            partial.astype(jnp.bfloat16), "fsdp", scatter_dimension=0, tiled=True
        ).astype(jnp.float32)

    def exchange(blocks):
        return lax.all_to_all(blocks, "fsdp", 0, 0, tiled=True)

    def sum_copies(partial):
        return lax.psum(partial.astype(jnp.bfloat16), "rep").astype(jnp.float32)

    query_blocks = query_weight.reshape(shard_rows, devices, query_width).transpose(1, 0, 2)
    key_blocks = jnp.repeat(
        key_weight.reshape(shard_rows, KV_HEADS, HEAD_DIM).transpose(1, 0, 2), sharing, axis=0
    )
    value_blocks = jnp.repeat(
        value_weight.reshape(shard_rows, KV_HEADS, HEAD_DIM).transpose(1, 0, 2), sharing, axis=0
    )
    mixer_columns = exchange(
        jnp.concatenate([query_blocks, key_blocks, value_blocks], axis=2)
    ).reshape(width, query_width + 2 * HEAD_DIM)
    gate_blocks = gate_weight.reshape(shard_rows, devices, hidden_width).transpose(1, 0, 2)
    up_blocks = up_weight.reshape(shard_rows, devices, hidden_width).transpose(1, 0, 2)
    feed_columns = exchange(jnp.concatenate([gate_blocks, up_blocks], axis=2)).reshape(
        width, 2 * hidden_width
    )

    infos = [
        positions(block_order[0, row], doc_ids[0, row], prefix_len[0, row], length)
        for row in range(micro)
    ]
    visible = jnp.stack(
        [
            (member[:, None] == member[None, :])
            & ((place[None, :] <= place[:, None]) | (place[None, :] < limit[None, :]))
            for place, member, relative, limit in infos
        ]
    )
    angle = jnp.concatenate([angles_for(info[2]) for info in infos], axis=0)

    inputs = tokens[0].reshape(own_rows, width).astype(jnp.float32)
    grad_rows = cotangent[0].reshape(own_rows, width)
    normed = rms_scale(inputs, gain_mixer).astype(jnp.bfloat16)
    all_normed = gather_rows(normed)
    all_grad_rows = gather_rows(grad_rows)

    def by_row(field):
        return (
            field.reshape(devices, micro, tok_count, -1)
            .transpose(1, 0, 2, 3)
            .reshape(micro * length, -1)
        )

    def by_device(field):
        return (
            field.reshape(micro, devices, tok_count, -1)
            .transpose(1, 0, 2, 3)
            .reshape(all_rows, -1)
        )

    raw = by_row(jnp.dot(all_normed, mixer_columns, preferred_element_type=jnp.float32))
    query = rotary(
        raw[:, :query_width].reshape(-1, heads_here, HEAD_DIM), angle, 1.0
    ).astype(jnp.bfloat16)
    query = query.reshape(micro, length, heads_here, HEAD_DIM).transpose(0, 2, 1, 3)
    keys = rotary(
        raw[:, query_width : query_width + HEAD_DIM].reshape(-1, 1, HEAD_DIM), angle, 1.0
    ).astype(jnp.bfloat16)
    keys = keys.reshape(micro, length, HEAD_DIM)
    values = raw[:, query_width + HEAD_DIM :].astype(jnp.bfloat16).reshape(micro, length, HEAD_DIM)

    scores = jnp.einsum("bgtd,bjd->bgtj", query, keys, preferred_element_type=jnp.float32) * scale
    scores = jnp.where(visible[:, None], scores, -1000000000.0)
    peak = jnp.max(scores, axis=-1, keepdims=True)
    raised = jnp.exp(scores - peak)
    totals = jnp.sum(raised, axis=-1, keepdims=True)
    probs = (raised / totals).astype(jnp.bfloat16)
    mixed = jnp.einsum("bgtj,bjd->bgtd", probs, values, preferred_element_type=jnp.float32)
    log_sums = peak + jnp.log(totals)
    attended = by_device(
        mixed.astype(jnp.bfloat16).transpose(0, 2, 1, 3).reshape(micro * length, query_width)
    )
    branch = scatter_sum(jnp.dot(attended, output_weight, preferred_element_type=jnp.float32))
    hidden = inputs + branch
    normed_two = rms_scale(hidden, gain_feed).astype(jnp.bfloat16)
    all_normed_two = gather_rows(normed_two)
    both = jnp.dot(all_normed_two, feed_columns, preferred_element_type=jnp.float32)
    gate, upward = both[:, :hidden_width], both[:, hidden_width:]
    inner = gated(gate, upward).astype(jnp.bfloat16)
    down = scatter_sum(jnp.dot(inner, down_weight, preferred_element_type=jnp.float32))
    layer_out = (hidden + down).astype(jnp.bfloat16).reshape(1, micro, tok_count, width)

    grad_inner = times_transpose(all_grad_rows, down_weight)
    grad_gate_f, grad_up_f = jax.vjp(gated, gate, upward)[1](grad_inner)
    grad_both = jnp.concatenate([grad_gate_f, grad_up_f], axis=1).astype(jnp.bfloat16)
    down_grad = sum_copies(contract_rows(inner, all_grad_rows))
    grad_normed_two = scatter_sum(times_transpose(grad_both, feed_columns))
    feed_blocks = exchange(
        contract_rows(all_normed_two, grad_both)
        .astype(jnp.bfloat16)
        .reshape(devices, shard_rows, 2 * hidden_width)
    )
    feed_blocks = sum_copies(feed_blocks)
    gate_grad = feed_blocks[:, :, :hidden_width].transpose(1, 0, 2).reshape(shard_rows, -1)
    up_grad = feed_blocks[:, :, hidden_width:].transpose(1, 0, 2).reshape(shard_rows, -1)

    hidden_norm_grad, feed_part = jax.vjp(rms_scale, hidden, gain_feed)[1](grad_normed_two)
    grad_hidden = grad_rows.astype(jnp.float32) + hidden_norm_grad
    all_grad_branch = gather_rows(grad_hidden.astype(jnp.bfloat16))
    grad_attended = times_transpose(all_grad_branch, output_weight).astype(jnp.bfloat16)
    output_grad = sum_copies(contract_rows(attended, all_grad_branch))

    grad_heads = (
        by_row(grad_attended)
        .reshape(micro, length, heads_here, HEAD_DIM)
        .transpose(0, 2, 1, 3)
    )
    scores = jnp.einsum("bgtd,bjd->bgtj", query, keys, preferred_element_type=jnp.float32) * scale
    scores = jnp.where(visible[:, None], scores, -1000000000.0)
    probs_back = jnp.exp(scores - log_sums)
    grad_probs = jnp.einsum(
        "bgtd,bjd->bgtj", grad_heads, values, preferred_element_type=jnp.float32
    )
    inner_sum = jnp.sum(probs_back * grad_probs, axis=-1, keepdims=True)
    grad_scores = (probs_back * (grad_probs - inner_sum)).astype(jnp.bfloat16)
    grad_query_rot = (
        jnp.einsum("bgtj,bjd->bgtd", grad_scores, keys, preferred_element_type=jnp.float32) * scale
    )
    grad_key_rot = (
        jnp.einsum("bgtj,bgtd->bjd", grad_scores, query, preferred_element_type=jnp.float32)
        * scale
    )
    grad_value = jnp.einsum(
        "bgtj,bgtd->bjd",
        probs_back.astype(jnp.bfloat16),
        grad_heads,
        preferred_element_type=jnp.float32,
    )
    grad_query = rotary(
        grad_query_rot.transpose(0, 2, 1, 3).reshape(-1, heads_here, HEAD_DIM), angle, -1.0
    ).reshape(-1, query_width)
    grad_key = rotary(grad_key_rot.reshape(-1, 1, HEAD_DIM), angle, -1.0).reshape(-1, HEAD_DIM)
    grad_mixer = by_device(
        jnp.concatenate(
            [grad_query, grad_key, grad_value.reshape(-1, HEAD_DIM)], axis=1
        ).astype(jnp.bfloat16)
    )
    grad_normed = scatter_sum(times_transpose(grad_mixer, mixer_columns))
    mixer_blocks = exchange(
        contract_rows(all_normed, grad_mixer)
        .astype(jnp.bfloat16)
        .reshape(devices, shard_rows, query_width + 2 * HEAD_DIM)
    )
    mixer_blocks = sum_copies(mixer_blocks)
    query_grad = mixer_blocks[:, :, :query_width].transpose(1, 0, 2).reshape(shard_rows, -1)
    pairs = mixer_blocks[:, :, query_width:].reshape(
        KV_HEADS, sharing, shard_rows, 2, HEAD_DIM
    ).sum(axis=1)
    key_grad = pairs[:, :, 0].transpose(1, 0, 2).reshape(shard_rows, -1)
    value_grad = pairs[:, :, 1].transpose(1, 0, 2).reshape(shard_rows, -1)
    input_norm_grad, mixer_part = jax.vjp(rms_scale, inputs, gain_mixer)[1](grad_normed)
    input_grad = (
        (grad_hidden + input_norm_grad).astype(jnp.bfloat16).reshape(1, micro, tok_count, width)
    )
    mixer_total, feed_total = lax.psum((mixer_part, feed_part), ("rep", "fsdp"))
    return (
        layer_out,
        input_grad,
        mixer_total,
        query_grad,
        key_grad,
        value_grad,
        output_grad,
        feed_total,
        gate_grad,
        up_grad,
        down_grad,
    )


def solution(mesh):
    placed = (
        P("rep", None, "fsdp", None),
        P("rep", None, "fsdp", None),
        P(),
        P("fsdp", None),
        P("fsdp", None),
        P("fsdp", None),
        P("fsdp", None),
        P(),
        P("fsdp", None),
        P("fsdp", None),
        P("fsdp", None),
        P("rep", None, None),
        P("rep", None, None),
        P("rep", None, None),
    )
    return jax.shard_map(
        local,
        mesh=mesh,
        in_specs=placed,
        out_specs=(
            P("rep", None, "fsdp", None),
            P("rep", None, "fsdp", None),
            P(),
            P("fsdp", None),
            P("fsdp", None),
            P("fsdp", None),
            P("fsdp", None),
            P(),
            P("fsdp", None),
            P("fsdp", None),
            P("fsdp", None),
        ),
        check_vma=False,
    )
```

```python
import jax
import jax.numpy as jnp
from jax import lax
from jax.experimental import pallas as pl
from jax.experimental.pallas import tpu as pltpu
from jax.sharding import PartitionSpec as P

HEADS = 32
KV_HEADS = 4
HEAD_DIM = 64
MICRO = 2
SEGS = 3


epsilon = 1e-05


def positions(order_row, doc_row, prefix_row, length):
    count = order_row.shape[0]
    block_width = length // count
    index = jnp.arange(length, dtype=jnp.int32)
    slot = index // block_width
    block = jnp.sum(
        jnp.where(
            slot[:, None] == jnp.arange(count, dtype=jnp.int32)[None, :], order_row[None, :], 0
        ),
        axis=1,
        dtype=jnp.int32,
    )
    place = block * block_width + index % block_width
    labels = jnp.arange(SEGS, dtype=jnp.int32)
    starts = jnp.sum(
        (doc_row[None, :] < labels[:, None]).astype(jnp.int32), axis=1, dtype=jnp.int32
    )
    member = jnp.sum(
        (place[:, None] >= starts[None, 1:]).astype(jnp.int32), axis=1, dtype=jnp.int32
    )
    picked = member[:, None] == labels[None, :]
    start_of = jnp.sum(jnp.where(picked, starts[None, :], 0), axis=1, dtype=jnp.int32)
    limit = jnp.sum(
        jnp.where(picked, starts[None, :] + prefix_row[None, :], 0), axis=1, dtype=jnp.int32
    )
    return (place, member, place - start_of, limit)


def angles_for(relative):
    halfway = HEAD_DIM // 2
    frequency = 10000.0 ** (-(2.0 * jnp.arange(halfway, dtype=jnp.float32)) / HEAD_DIM)
    return relative.astype(jnp.float32)[:, None] * frequency[None, :]


def rms_scale(values, gain):
    return values * lax.rsqrt(jnp.mean(values * values, axis=1, keepdims=True) + epsilon) * gain


def gated(gate_part, up_part):
    return jax.nn.silu(gate_part) * up_part


def contract_rows(left, right):
    return lax.dot_general(
        left, right, (((0,), (0,)), ((), ())), preferred_element_type=jnp.float32
    )


def times_transpose(left, right):
    return lax.dot_general(
        left, right, (((1,), (1,)), ((), ())), preferred_element_type=jnp.float32
    )


def dot_rows(left, right):
    return jnp.dot(left, right, preferred_element_type=jnp.float32)


def turn(field, cosine, sine):
    lane = lax.broadcasted_iota(jnp.int32, field.shape, 1) % HEAD_DIM
    half = HEAD_DIM // 2
    swapped = jnp.where(
        lane < half, pltpu.roll(field, 2 * HEAD_DIM - half, 1), pltpu.roll(field, half, 1)
    )
    return field * cosine + swapped * sine


def seen(columns, rows):
    place_q, member_q = columns[:, 0:1], columns[:, 1:2]
    place_k, member_k, limit_k = rows[0:1, :], rows[1:2, :], rows[2:3, :]
    return (member_q == member_k) & ((place_k <= place_q) | (place_k < limit_k))


def attend_kernel(raw_ref, cos_ref, sin_ref, column_ref, row_ref, out_ref, query_ref, kv_ref, log_ref):
    scale = HEAD_DIM ** (-0.5)
    cosine, sine = cos_ref[...], sin_ref[...]
    visible = seen(column_ref[...], row_ref[...])
    wide = 2 * HEAD_DIM
    pair_count = raw_ref.shape[1] // wide - 1
    first = lax.broadcasted_iota(jnp.int32, cosine.shape, 1) < HEAD_DIM
    kv = raw_ref[:, pair_count * wide :]
    keys_values = jnp.where(first, turn(kv, cosine, sine), kv)
    swapped = pltpu.roll(keys_values, HEAD_DIM, 1)
    keys = jnp.where(first, keys_values, swapped).astype(jnp.bfloat16)
    values = jnp.where(first, swapped, keys_values).astype(jnp.bfloat16)
    kv_ref[...] = keys_values.astype(jnp.bfloat16)
    logs = jnp.zeros(cosine.shape, jnp.float32)
    lanes = lax.broadcasted_iota(jnp.int32, cosine.shape, 1)
    for pair in range(pair_count):
        at = slice(pair * wide, (pair + 1) * wide)
        query = turn(raw_ref[:, at], cosine, sine).astype(jnp.bfloat16)
        query_ref[:, at] = query
        results = []
        for member in range(2):
            chosen = first if member == 0 else jnp.logical_not(first)
            one = jnp.where(chosen, query, jnp.zeros_like(query))
            scores = (
                lax.dot_general(
                    one, keys, (((1,), (1,)), ((), ())), preferred_element_type=jnp.float32
                )
                * scale
            )
            scores = jnp.where(visible, scores, -1000000000.0)
            peak = jnp.max(scores, axis=1, keepdims=True)
            raised = jnp.exp(scores - peak)
            totals = jnp.sum(raised, axis=1, keepdims=True)
            probs = (raised * (1.0 / totals)).astype(jnp.bfloat16)
            results.append(dot_rows(probs, values))
            logs = jnp.where(lanes == 2 * pair + member, peak + jnp.log(totals), logs)
        out_ref[:, at] = jnp.where(first, results[0], results[1]).astype(jnp.bfloat16)
    log_ref[...] = logs


def attend_back_kernel(
    query_ref, kv_ref, grad_ref, log_ref, cos_ref, sin_ref, column_ref, row_ref, out_ref
):
    scale = HEAD_DIM ** (-0.5)
    cosine, sine = cos_ref[...], sin_ref[...]
    visible = seen(column_ref[...], row_ref[...])
    wide = 2 * HEAD_DIM
    pair_count = query_ref.shape[1] // wide
    first = lax.broadcasted_iota(jnp.int32, cosine.shape, 1) < HEAD_DIM
    lanes = lax.broadcasted_iota(jnp.int32, cosine.shape, 1)
    keys_values = kv_ref[...]
    swapped = pltpu.roll(keys_values.astype(jnp.float32), HEAD_DIM, 1).astype(jnp.bfloat16)
    keys = jnp.where(first, keys_values, swapped)
    values = jnp.where(first, swapped, keys_values)
    logs = log_ref[...]
    grad_keys = jnp.zeros(cosine.shape, jnp.float32)
    grad_values = jnp.zeros(cosine.shape, jnp.float32)
    for pair in range(pair_count):
        at = slice(pair * wide, (pair + 1) * wide)
        query, grad = query_ref[:, at], grad_ref[:, at]
        results = []
        for member in range(2):
            chosen = first if member == 0 else jnp.logical_not(first)
            one = jnp.where(chosen, query, jnp.zeros_like(query))
            grad_one = jnp.where(chosen, grad, jnp.zeros_like(grad))
            log_one = jnp.sum(
                jnp.where(lanes == 2 * pair + member, logs, 0.0), axis=1, keepdims=True
            )
            scores = (
                lax.dot_general(
                    one, keys, (((1,), (1,)), ((), ())), preferred_element_type=jnp.float32
                )
                * scale
            )
            probs = jnp.exp(jnp.where(visible, scores, -1000000000.0) - log_one)
            grad_probs = lax.dot_general(
                grad_one, values, (((1,), (1,)), ((), ())), preferred_element_type=jnp.float32
            )
            inner_sum = jnp.sum(probs * grad_probs, axis=1, keepdims=True)
            grad_scores = (probs * (grad_probs - inner_sum)).astype(jnp.bfloat16)
            results.append(dot_rows(grad_scores, keys) * scale)
            grad_keys = grad_keys + contract_rows(grad_scores, one)
            grad_values = grad_values + contract_rows(probs.astype(jnp.bfloat16), grad_one)
        joined = jnp.where(first, results[0], results[1])
        out_ref[:, at] = turn(joined, cosine, -sine).astype(jnp.bfloat16)
    grad_keys = (grad_keys + pltpu.roll(grad_keys, HEAD_DIM, 1)) * scale
    grad_values = grad_values + pltpu.roll(grad_values, HEAD_DIM, 1)
    last = jnp.where(first, turn(grad_keys, cosine, -sine), grad_values)
    out_ref[:, pair_count * wide :] = last.astype(jnp.bfloat16)


def whole(*_):
    return (0, 0)


def whole_specs(arrays):
    return [pl.BlockSpec(a.shape, whole) for a in arrays]


def attend(raw, cosine, sine, columns, rows):
    length, wide = raw.shape
    query_width = wide - 2 * HEAD_DIM
    heads = query_width // HEAD_DIM
    outs = [
        jax.ShapeDtypeStruct((length, query_width), jnp.bfloat16),
        jax.ShapeDtypeStruct((length, query_width), jnp.bfloat16),
        jax.ShapeDtypeStruct((length, 2 * HEAD_DIM), jnp.bfloat16),
        jax.ShapeDtypeStruct((length, 2 * HEAD_DIM), jnp.float32),
    ]
    args = (raw, cosine, sine, columns, rows)
    return pl.pallas_call(
        attend_kernel,
        grid=(1,),
        in_specs=whole_specs(args),
        out_specs=whole_specs(outs),
        out_shape=outs,
        compiler_params=pltpu.CompilerParams(vmem_limit_bytes=48 * 1024 * 1024),
        cost_estimate=pl.CostEstimate(
            flops=heads * length * length * 2 * HEAD_DIM * 8,
            transcendentals=heads * length * length,
            bytes_accessed=length * wide * 8,
        ),
        name="attend",
    )(*args)


def attend_back(query, kv, grad, logs, cosine, sine, columns, rows):
    length, query_width = query.shape
    heads = query_width // HEAD_DIM
    out = jax.ShapeDtypeStruct((length, query_width + 2 * HEAD_DIM), jnp.bfloat16)
    args = (query, kv, grad, logs, cosine, sine, columns, rows)
    return pl.pallas_call(
        attend_back_kernel,
        grid=(1,),
        in_specs=whole_specs(args),
        out_specs=pl.BlockSpec(out.shape, whole),
        out_shape=out,
        compiler_params=pltpu.CompilerParams(vmem_limit_bytes=48 * 1024 * 1024),
        cost_estimate=pl.CostEstimate(
            flops=heads * length * length * 2 * HEAD_DIM * 20,
            transcendentals=heads * length * length,
            bytes_accessed=length * query_width * 8,
        ),
        name="attend_back",
    )(*args)


def pick_kernel(place_ref, gate_ref, up_ref, out_ref):
    width = gate_ref.shape[1]
    out_ref[0, :, :width] = gate_ref[...]
    out_ref[0, :, width:] = up_ref[...]


def pick_blocks(me, side, gate, up, chips, picks, halved):
    rows, total = gate.shape
    width = total // chips
    if halved:
        rows = rows // 2
    if width % 128:
        both = jnp.concatenate(
            [a.reshape(a.shape[0], chips, width).transpose(1, 0, 2) for a in (gate, up)], axis=2
        )
        if halved:
            both = lax.dynamic_slice_in_dim(both, side * rows, rows, 1)
        return jnp.stack(
            [lax.dynamic_index_in_dim(both, me // 2 ^ j, 0, keepdims=False) for j in picks]
        )
    first = picks[0]
    column = pl.BlockSpec(
        (rows, width), lambda s, place: (place[1] if halved else 0, place[0] // 2 ^ (s + first))
    )
    return pl.pallas_call(
        pick_kernel,
        grid_spec=pltpu.PrefetchScalarGridSpec(
            num_scalar_prefetch=1,
            grid=(len(picks),),
            in_specs=[column, column],
            out_specs=pl.BlockSpec((1, rows, 2 * width), lambda s, place: (s, 0, 0)),
        ),
        out_shape=jax.ShapeDtypeStruct((len(picks), rows, 2 * width), gate.dtype),
        compiler_params=pltpu.CompilerParams(vmem_limit_bytes=16 * 1024 * 1024),
        cost_estimate=pl.CostEstimate(
            flops=0, transcendentals=0, bytes_accessed=8 * rows * width * len(picks)
        ),
        name="pick_blocks",
    )(jnp.stack([me, side]), gate, up)


def put_first(place_ref, piece_ref, out_ref):
    out_ref[...] = piece_ref[...].reshape(out_ref.shape)


def put_next(place_ref, piece_ref, held_ref, out_ref):
    put_first(place_ref, piece_ref, out_ref)


def put_block(me, side, piece, p, flip, held):
    devices = lax.axis_size("fsdp")
    rows, width = piece.shape
    half = rows if flip is not None else rows // 2
    parts = 1 if flip is not None else 2
    block = pl.BlockSpec(
        (1, parts, half, width),
        lambda s, place: (place[0] ^ p, 0 if flip is None else place[1] ^ flip, 0, 0),
    )
    extra = [] if held is None else [held]
    return pl.pallas_call(
        put_first if held is None else put_next,
        grid_spec=pltpu.PrefetchScalarGridSpec(
            num_scalar_prefetch=1,
            grid=(1,),
            in_specs=[pl.BlockSpec((rows, width), lambda s, place: (0, 0))]
            + [pl.BlockSpec(memory_space=pl.ANY)] * len(extra),
            out_specs=block,
        ),
        out_shape=jax.ShapeDtypeStruct((devices, 2, half, width), piece.dtype),
        input_output_aliases={2: 0} if extra else {},
        compiler_params=pltpu.CompilerParams(vmem_limit_bytes=16 * 1024 * 1024),
        cost_estimate=pl.CostEstimate(
            flops=0, transcendentals=0, bytes_accessed=4 * rows * width
        ),
        name="put_block",
    )(jnp.stack([me, side]), piece, *extra)


def place_kernel(place_ref, near_ref, far_ref, out_ref):
    @pl.when(pl.program_id(1) == 0)
    def _():
        out_ref[...] = near_ref[...]

    @pl.when(pl.program_id(1) == 1)
    def _():
        out_ref[...] = far_ref[...]


def place_blocks(me, near, far):
    chips, rows, width = near.shape
    block = pl.BlockSpec((1, rows, width), lambda j, b, place: (j, 0, 0))
    return pl.pallas_call(
        place_kernel,
        grid_spec=pltpu.PrefetchScalarGridSpec(
            num_scalar_prefetch=1,
            grid=(chips, 2),
            in_specs=[block, block],
            out_specs=pl.BlockSpec(
                (1, rows, width), lambda j, b, place: (place[0] ^ (2 * j + b), 0, 0)
            ),
        ),
        out_shape=jax.ShapeDtypeStruct((2 * chips, rows, width), near.dtype),
        compiler_params=pltpu.CompilerParams(vmem_limit_bytes=16 * 1024 * 1024),
        cost_estimate=pl.CostEstimate(
            flops=0, transcendentals=0, bytes_accessed=8 * chips * rows * width
        ),
        name="place_blocks",
    )(me.reshape(1), near, far).reshape(2 * chips * rows, width)


def spread_first(place_ref, piece_ref, gate_ref, up_ref):
    width = gate_ref.shape[1]
    gate_ref[...] = piece_ref[:, :width].astype(jnp.float32)
    up_ref[...] = piece_ref[:, width:].astype(jnp.float32)


def spread_next(place_ref, piece_ref, gate_in, up_in, gate_ref, up_ref):
    spread_first(place_ref, piece_ref, gate_ref, up_ref)


def spread(me, j, piece, chips, held):
    rows, both = piece.shape
    width = both // 2
    out = jax.ShapeDtypeStruct((rows, width * chips), jnp.float32)
    column = pl.BlockSpec((rows, width), lambda s, place: (0, place[0] // 2 ^ j))
    anywhere = pl.BlockSpec(memory_space=pl.ANY)
    return pl.pallas_call(
        spread_next if held else spread_first,
        grid_spec=pltpu.PrefetchScalarGridSpec(
            num_scalar_prefetch=1,
            grid=(1,),
            in_specs=[pl.BlockSpec((rows, both), lambda s, place: (0, 0))]
            + [anywhere] * len(held),
            out_specs=[column, column],
        ),
        out_shape=[out, out],
        input_output_aliases={2: 0, 3: 1} if held else {},
        compiler_params=pltpu.CompilerParams(vmem_limit_bytes=24 * 1024 * 1024),
        cost_estimate=pl.CostEstimate(
            flops=0, transcendentals=0, bytes_accessed=6 * rows * both
        ),
        name="spread",
    )(me.reshape(1), piece, *held)


class Flow:
    def __init__(self, token):
        self.token = token

    def after(self, *arrays):
        held = lax.optimization_barrier((self.token,) + arrays)[1:]
        return held if len(held) > 1 else held[0]

    def until(self, *arrays):
        held = lax.optimization_barrier((self.token,) + arrays)
        self.token = held[0]
        return held[1:] if len(held) > 2 else held[1]


class Chain:
    def __init__(self, flow, copies, index):
        self.flow, self.copies, self.index = flow, copies, index
        half = copies // 2
        ends = [(s, copies - 1 - s) for s in range(half - 1)]
        self.stages = [(True, [(a, a + 1), (b, b - 1)], None) for a, b in ends]
        self.stages.append((True, [(half - 1, half), (half, half - 1)], None))
        self.stages += [(False, [(a + 1, a), (b - 1, b)], (a, b)) for a, b in reversed(ends)]
        self.waiting, self.moving, self.results = [], [], {}

    def add(self, name, part):
        self.waiting.append((name, part))

    def start(self, part, stage):
        return lax.ppermute(part, "rep", self.stages[stage][1])

    def step(self):
        moving = list(reversed(self.moving))
        self.moving = []
        if self.waiting:
            name, part = self.waiting.pop(0)
            part = self.flow.after(part)
            self.moving.append((name, part, self.start(part, 0), 0))
        for name, part, came, stage in moving:
            came = self.flow.until(came)
            adds, _, outer = self.stages[stage]
            if adds:
                part = (part.astype(jnp.float32) + came.astype(jnp.float32)).astype(jnp.bfloat16)
            else:
                here = (self.index == outer[0]) | (self.index == outer[1])
                part = jnp.where(here, came, part)
            if stage + 1 == len(self.stages):
                self.results[name] = part
            else:
                part = self.flow.until(part)
                self.moving.insert(0, (name, part, self.start(part, stage + 1), stage + 1))
        self.moving.sort(key=lambda item: -item[3])

    def finish(self):
        while self.waiting or self.moving:
            self.step()


def local(
    tokens,
    cotangent,
    mixer_gain,
    query_weight,
    key_weight,
    value_weight,
    output_weight,
    feed_gain,
    gate_weight,
    up_weight,
    down_weight,
    doc_ids,
    prefix_len,
    block_order,
):
    tok_count, width = tokens.shape[2:]
    devices = lax.axis_size("fsdp")
    chips = devices // 2
    copies = lax.axis_size("rep")
    me = lax.axis_index("fsdp")
    core = me % 2
    copy_index = lax.axis_index("rep")
    side = copy_index % 2
    length = tok_count * devices
    shard_rows = width // devices
    half_shard = shard_rows // 2
    query_width = HEADS // chips * HEAD_DIM
    sharing = max(1, chips // KV_HEADS)
    down_rows = down_weight.shape[0]
    hidden_width = 2 * down_rows
    gain_mixer = mixer_gain.astype(jnp.float32)
    gain_feed = feed_gain.astype(jnp.float32)
    low = jnp.bfloat16
    full = jnp.float32
    flow = Flow(jnp.zeros((8, 128), full) + copy_index.astype(full))
    chain = Chain(flow, copies, copy_index)

    def swap(array, bits):
        return lax.ppermute(array, "fsdp", [(d, d ^ bits) for d in range(devices)])

    def swap_copies(array, bits):
        return lax.ppermute(array, "rep", [(d, d ^ bits) for d in range(copies)])

    def one_of(array, index, axis=0):
        return lax.dynamic_index_in_dim(array, index, axis, keepdims=False)

    def both_cores(mine, other):
        return jnp.where(
            core == 0,
            jnp.concatenate([mine, other], axis=0),
            jnp.concatenate([other, mine], axis=0),
        )

    def gather_start(own):
        return (own, swap(own, 2), swap(own, 4)) if chips == 4 else (own,)

    def gather_end(parts):
        if chips == 4:
            own, along_x, along_y = parts
            mid = own.shape[0] // 2
            return jnp.concatenate(
                [own, along_x, along_y, swap(along_y[:mid], 2), swap(along_x[mid:], 4)], axis=0
            )
        (own,) = parts
        bits = 2
        while bits < devices:
            own = jnp.concatenate([own, swap(own, bits)], axis=0)
            bits = 2 * bits
        return own

    def scatter_sum(partial):
        if chips == 4:
            mine, to_x, to_y, across = jnp.split(partial, 4, axis=0)
            mid = mine.shape[0] // 2
            across = across.astype(low)
            from_x, from_y = swap(across[:mid], 2), swap(across[mid:], 4)
            to_x = jnp.concatenate([to_x[:mid], to_x[mid:] + from_y.astype(full)], axis=0)
            to_y = jnp.concatenate([to_y[:mid] + from_x.astype(full), to_y[mid:]], axis=0)
            came_x, came_y = swap(to_x.astype(low), 2), swap(to_y.astype(low), 4)
            return mine + came_x.astype(full) + came_y.astype(full)
        bits = devices // 2
        while bits > 1:
            rows = partial.shape[0] // 2
            partial = partial[:rows] + swap(partial[rows:].astype(low), bits).astype(full)
            bits = bits // 2
        return partial

    def by_core(array):
        mine, other = one_of(array, core), one_of(array, 1 - core)
        return jnp.concatenate([mine, swap(other, 1)], axis=0)

    def by_token(rows):
        mine, other = rows[:tok_count], swap(rows[tok_count:], 1)
        return jnp.where(core == 0, jnp.stack([mine, other]), jnp.stack([other, mine]))[None]

    inputs = by_core(tokens[0]).astype(full)
    normed_parts = gather_start(rms_scale(inputs, gain_mixer).astype(low))

    query_blocks = query_weight.reshape(shard_rows, chips, query_width).transpose(1, 0, 2)
    key_value = [
        jnp.repeat(a.reshape(shard_rows, KV_HEADS, HEAD_DIM).transpose(1, 0, 2), sharing, axis=0)
        for a in (key_weight, value_weight)
    ]
    mixer_blocks = jnp.concatenate([query_blocks] + key_value, axis=2)
    mixer_near = [one_of(mixer_blocks, me // 2 ^ j) for j in range(chips)]
    mixer_near = [swap(piece, 2 * j) if j else piece for j, piece in enumerate(mixer_near)]
    normed = gather_end(normed_parts)
    mixer_near = jnp.stack(mixer_near)

    info = positions(
        one_of(block_order[0], core), one_of(doc_ids[0], core), one_of(prefix_len[0], core), length
    )
    facts = jnp.stack(info).reshape(4, devices, tok_count)
    facts = jnp.stack([one_of(facts, me ^ p, 1) for p in range(devices)], axis=1)
    place, member, relative, limit = facts.reshape(4, length)
    rows = jnp.concatenate([jnp.stack([place, member, limit]), jnp.zeros((5, length), jnp.int32)])
    columns = jnp.stack([place, member], axis=1)
    angle = angles_for(relative)
    cosine, sine = jnp.cos(angle), jnp.sin(angle)
    cosine = jnp.concatenate([cosine] * 4, axis=1)
    sine = jnp.concatenate([-sine, sine, -sine, sine], axis=1)

    feed_own = pick_blocks(me, side, gate_weight, up_weight, chips, range(1), False)[0]
    feed_away = pick_blocks(me, side, gate_weight, up_weight, chips, range(1, chips), True)
    output_rows = both_cores(output_weight, swap(output_weight, 1))
    down_all = both_cores(down_weight, swap(down_weight, 1))
    grad_rows = by_core(cotangent[0])
    feed_own_far = swap(feed_own, 1)
    feed_columns = put_block(me, side, feed_own, 0, None, None)
    feed_columns = put_block(me, side, feed_own_far, 1, None, feed_columns)

    normed, mixer_near = flow.until(normed, mixer_near)
    split = (chips + 1) // 2 + 1
    early = [swap(flow.after(feed_away[j - 1]), 2 * j) for j in range(1, split)]
    mixer_columns = place_blocks(me, mixer_near, swap(mixer_near, 1))
    raw = dot_rows(normed, mixer_columns)
    attended, query, kv, logs = attend(raw, cosine, sine, columns, rows)
    branch = flow.until(dot_rows(attended, output_rows))

    def take(j, piece):
        nonlocal feed_columns
        feed_columns = put_block(me, side, piece, 2 * j, 0, feed_columns)
        feed_columns = put_block(me, side, swap(piece, 1), 2 * j + 1, 0, feed_columns)

    def take_other(j, piece):
        nonlocal feed_columns
        feed_columns = put_block(me, side, piece, 2 * j, 1, feed_columns)
        feed_columns = put_block(me, side, swap(piece, 1), 2 * j + 1, 1, feed_columns)

    early = [flow.until(piece) for piece in early]
    late = [swap(flow.after(feed_away[j - 1]), 2 * j) for j in range(split, chips)]
    early_other = [swap_copies(piece, 1) for piece in early]
    for j, piece in enumerate(early, 1):
        take(j, piece)
    hidden = inputs + scatter_sum(branch)
    normed_two_own = flow.until(rms_scale(hidden, gain_feed).astype(low))
    normed_two_parts = gather_start(normed_two_own)
    late = [flow.until(piece) for piece in late]
    late_other = [swap_copies(piece, 1) for piece in late]
    for j, piece in enumerate(late, split):
        take(j, piece)
    normed_two_parts = flow.until(*normed_two_parts)
    if chips != 4:
        normed_two_parts = (normed_two_parts,)
    normed_two = gather_end(normed_two_parts)
    cotangent_parts = gather_start(flow.after(grad_rows))
    for j, piece in enumerate(early_other, 1):
        take_other(j, piece)
    for j, piece in enumerate(late_other, split):
        take_other(j, piece)
    feed_columns = feed_columns.reshape(width, 2 * hidden_width)
    normed_two = flow.until(normed_two)

    both = flow.until(dot_rows(normed_two, feed_columns))
    all_grad_rows = gather_end(cotangent_parts)
    gate, upward = both[:, :hidden_width], both[:, hidden_width:]
    inner, pull = jax.vjp(gated, gate, upward)
    inner = flow.until(inner.astype(low))

    def summed(mine, other, grads):
        came = swap(contract_rows(other, grads).astype(low), 1)
        return (contract_rows(mine, grads) + came.astype(full)).astype(low)

    left, right = inner[:, :down_rows], inner[:, down_rows:]
    down_part = flow.until(
        summed(
            jnp.where(core == 0, left, right), jnp.where(core == 0, right, left), all_grad_rows
        )
    )
    for piece, part in enumerate(jnp.split(down_part, 2, axis=0)):
        chain.add(("down", piece), part)
    chain.step()

    grad_inner = times_transpose(flow.after(all_grad_rows), down_all)
    grad_gate, grad_up = pull(grad_inner)
    grad_both = flow.until(jnp.concatenate([grad_gate, grad_up], axis=1).astype(low))
    partial_two = flow.until(times_transpose(grad_both, feed_columns))

    def columns_of(field):
        blocks = field.reshape(field.shape[0], devices, shard_rows)
        return [one_of(blocks, me ^ p, 1) for p in range(devices)]

    feed_fields = columns_of(normed_two)

    def feed_piece(j):
        return summed(feed_fields[2 * j], feed_fields[2 * j + 1], flow.after(grad_both))

    grad_normed_two = scatter_sum(partial_two)
    pieces = [feed_piece(0)]
    grad_normed_two, pieces[0] = flow.until(grad_normed_two, pieces[0])
    hidden_norm_grad, feed_part = jax.vjp(rms_scale, hidden, gain_feed)[1](grad_normed_two)
    grad_hidden = grad_rows.astype(full) + hidden_norm_grad
    grad_branch_parts = gather_start(flow.until(grad_hidden.astype(low)))
    chain.add(("feed", 0), pieces[0])
    chain.step()
    pieces += [feed_piece(j) for j in range(1, chips)]
    grad_branch = gather_end(grad_branch_parts)
    grad_branch = flow.until(grad_branch)
    pieces = list(flow.until(*pieces))
    moved = {j: swap(flow.after(pieces[j]), 2 * j) for j in range(1, split)}
    grad_attended = times_transpose(grad_branch, output_rows).astype(low)
    attended_halves = attended.reshape(length, 2, query_width // 2)
    output_part = flow.until(
        summed(one_of(attended_halves, core, 1), one_of(attended_halves, 1 - core, 1), grad_branch)
    )
    chain.add("output", output_part)
    chain.step()
    grad_mixer = flow.until(
        attend_back(query, kv, grad_attended, logs, cosine, sine, columns, rows)
    )
    partial = flow.until(times_transpose(grad_mixer, mixer_columns))
    grad_normed = scatter_sum(partial)
    mixer_fields = columns_of(normed)
    mixer_pieces = [
        summed(mixer_fields[2 * j], mixer_fields[2 * j + 1], grad_mixer) for j in range(chips)
    ]
    grad_normed = flow.until(grad_normed)
    mixer_pieces = [
        swap(piece, 2 * j) if j else piece for j, piece in enumerate(flow.until(*mixer_pieces))
    ]
    for j in range(1, split):
        moved[j] = flow.until(moved[j])
        chain.add(("feed", j), moved[j])
    for j in range(split, chips):
        moved[j] = swap(flow.after(pieces[j]), 2 * j)
    chain.step()
    input_norm_grad, mixer_part = jax.vjp(rms_scale, inputs, gain_mixer)[1](grad_normed)
    input_grad = by_token((grad_hidden + input_norm_grad).astype(low))
    gains = jnp.stack([mixer_part, feed_part]).reshape(2, 8, width // 8)
    if copies & (copies - 1) == 0:
        bits = 1
        while bits < devices:
            gains = gains + swap(gains, bits)
            bits = 2 * bits
        bits = 1
        while bits < copies:
            gains = gains + swap_copies(gains, bits)
            bits = 2 * bits
    else:
        gains = lax.psum(gains, ("rep", "fsdp"))
    mixer_total, feed_total = gains.reshape(2, width)
    down = flow.until(scatter_sum(dot_rows(flow.after(inner), down_all)))
    layer_out = by_token((hidden + down).astype(low))
    chain.step()
    chain.add("mixer", jnp.stack(flow.until(*mixer_pieces)))
    for j in range(split, chips):
        moved[j] = flow.until(moved[j])
        for piece, part in enumerate(jnp.split(moved[j], 4, axis=0)):
            chain.add(("feed", j, piece), part)
    chain.finish()
    results = chain.results
    down_grad = jnp.concatenate([results["down", 0], results["down", 1]], axis=0).astype(full)
    output_grad = results["output"].astype(full)
    done = [results["feed", j] for j in range(split)]
    done += [
        jnp.concatenate([results["feed", j, piece] for piece in range(4)], axis=0)
        for j in range(split, chips)
    ]
    if hidden_width % 128:
        stacked = jnp.stack(done)
        ordered = jnp.stack([one_of(stacked, me // 2 ^ j) for j in range(chips)])
        ordered = ordered.astype(full).reshape(chips, shard_rows, 2, hidden_width)
        gate_grad, up_grad = ordered.transpose(2, 1, 0, 3).reshape(2, shard_rows, -1)
    else:
        held = ()
        for j, piece in enumerate(done):
            held = spread(me, j, piece, chips, held)
        gate_grad, up_grad = held
    mixer_grads = jnp.stack([one_of(results["mixer"], me // 2 ^ j) for j in range(chips)])
    mixer_grads = mixer_grads.astype(full)
    query_grad = mixer_grads[:, :, :query_width].transpose(1, 0, 2).reshape(shard_rows, -1)
    shared = (
        mixer_grads[:, :, query_width:]
        .reshape(KV_HEADS, sharing, shard_rows, 2, HEAD_DIM)
        .sum(axis=1)
    )
    key_grad = shared[:, :, 0].transpose(1, 0, 2).reshape(shard_rows, -1)
    value_grad = shared[:, :, 1].transpose(1, 0, 2).reshape(shard_rows, -1)
    return (
        layer_out,
        input_grad,
        mixer_total,
        query_grad,
        key_grad,
        value_grad,
        output_grad,
        feed_total,
        gate_grad,
        up_grad,
        down_grad,
    )


def solution(mesh):
    placed = (
        P("rep", None, "fsdp", None),
        P("rep", None, "fsdp", None),
        P(),
        P("fsdp", None),
        P("fsdp", None),
        P("fsdp", None),
        P("fsdp", None),
        P(),
        P("fsdp", None),
        P("fsdp", None),
        P("fsdp", None),
        P("rep", None, None),
        P("rep", None, None),
        P("rep", None, None),
    )
    return jax.shard_map(
        local,
        mesh=mesh,
        in_specs=placed,
        out_specs=(
            P("rep", None, "fsdp", None),
            P("rep", None, "fsdp", None),
            P(),
            P("fsdp", None),
            P("fsdp", None),
            P("fsdp", None),
            P("fsdp", None),
            P(),
            P("fsdp", None),
            P("fsdp", None),
            P("fsdp", None),
        ),
        check_vma=False,
    )
```

```python
import functools

import jax
import jax.numpy as jnp
from jax import lax
from jax.experimental import pallas as pl
from jax.experimental.pallas import tpu as pltpu
from jax.sharding import PartitionSpec as P

HEADS = 32
KV_HEADS = 4
HEAD_DIM = 64
MICRO = 2
SEGS = 3


epsilon = 1e-05
FREE = pl.CostEstimate(flops=0, transcendentals=0, bytes_accessed=0)


def positions(order_row, doc_row, prefix_row, length):
    count = order_row.shape[0]
    block_width = length // count
    index = jnp.arange(length, dtype=jnp.int32)
    slot = index // block_width
    block = jnp.sum(
        jnp.where(
            slot[:, None] == jnp.arange(count, dtype=jnp.int32)[None, :], order_row[None, :], 0
        ),
        axis=1,
        dtype=jnp.int32,
    )
    place = block * block_width + index % block_width
    labels = jnp.arange(SEGS, dtype=jnp.int32)
    starts = jnp.sum(
        (doc_row[None, :] < labels[:, None]).astype(jnp.int32), axis=1, dtype=jnp.int32
    )
    member = jnp.sum(
        (place[:, None] >= starts[None, 1:]).astype(jnp.int32), axis=1, dtype=jnp.int32
    )
    picked = member[:, None] == labels[None, :]
    start_of = jnp.sum(jnp.where(picked, starts[None, :], 0), axis=1, dtype=jnp.int32)
    limit = jnp.sum(
        jnp.where(picked, starts[None, :] + prefix_row[None, :], 0), axis=1, dtype=jnp.int32
    )
    return (place, member, place - start_of, limit)


def angles_for(relative):
    halfway = HEAD_DIM // 2
    frequency = 10000.0 ** (-(2.0 * jnp.arange(halfway, dtype=jnp.float32)) / HEAD_DIM)
    return relative.astype(jnp.float32)[:, None] * frequency[None, :]


def rms_scale(values, gain):
    return values * lax.rsqrt(jnp.mean(values * values, axis=1, keepdims=True) + epsilon) * gain


def gated(gate_part, up_part):
    return jax.nn.silu(gate_part) * up_part


def contract_rows(left, right):
    return lax.dot_general(
        left, right, (((0,), (0,)), ((), ())), preferred_element_type=jnp.float32
    )


def times_transpose(left, right):
    return lax.dot_general(
        left, right, (((1,), (1,)), ((), ())), preferred_element_type=jnp.float32
    )


def dot_rows(left, right):
    return jnp.dot(left, right, preferred_element_type=jnp.float32)


def turn(field, cosine, sine):
    lane = lax.broadcasted_iota(jnp.int32, field.shape, 1) % HEAD_DIM
    half = HEAD_DIM // 2
    swapped = jnp.where(
        lane < half, pltpu.roll(field, 2 * HEAD_DIM - half, 1), pltpu.roll(field, half, 1)
    )
    return field * cosine + swapped * sine


def seen(columns, rows):
    place_q, member_q = columns[:, 0:1], columns[:, 1:2]
    place_k, member_k, limit_k = rows[0:1, :], rows[1:2, :], rows[2:3, :]
    return (member_q == member_k) & ((place_k <= place_q) | (place_k < limit_k))


def attend_kernel(raw_ref, cos_ref, sin_ref, column_ref, row_ref, out_ref, query_ref, kv_ref, log_ref):
    scale = HEAD_DIM ** (-0.5)
    cosine, sine = cos_ref[...], sin_ref[...]
    visible = seen(column_ref[...], row_ref[...])
    wide = 2 * HEAD_DIM
    pair_count = raw_ref.shape[1] // wide - 1
    first = lax.broadcasted_iota(jnp.int32, cosine.shape, 1) < HEAD_DIM
    kv = raw_ref[:, pair_count * wide :]
    keys_values = jnp.where(first, turn(kv, cosine, sine), kv)
    swapped = pltpu.roll(keys_values, HEAD_DIM, 1)
    keys = jnp.where(first, keys_values, swapped).astype(jnp.bfloat16)
    values = jnp.where(first, swapped, keys_values).astype(jnp.bfloat16)
    kv_ref[...] = keys_values.astype(jnp.bfloat16)
    logs = jnp.zeros(cosine.shape, jnp.float32)
    lanes = lax.broadcasted_iota(jnp.int32, cosine.shape, 1)
    for pair in range(pair_count):
        at = slice(pair * wide, (pair + 1) * wide)
        query = turn(raw_ref[:, at], cosine, sine).astype(jnp.bfloat16)
        query_ref[:, at] = query
        results = []
        for member in range(2):
            chosen = first if member == 0 else jnp.logical_not(first)
            one = jnp.where(chosen, query, jnp.zeros_like(query))
            scores = (
                lax.dot_general(
                    one, keys, (((1,), (1,)), ((), ())), preferred_element_type=jnp.float32
                )
                * scale
            )
            scores = jnp.where(visible, scores, -1000000000.0)
            peak = jnp.max(scores, axis=1, keepdims=True)
            raised = jnp.exp(scores - peak)
            totals = jnp.sum(raised, axis=1, keepdims=True)
            probs = (raised * (1.0 / totals)).astype(jnp.bfloat16)
            results.append(dot_rows(probs, values))
            logs = jnp.where(lanes == 2 * pair + member, peak + jnp.log(totals), logs)
        out_ref[:, at] = jnp.where(first, results[0], results[1]).astype(jnp.bfloat16)
    log_ref[...] = logs


def attend_back_kernel(
    query_ref, kv_ref, grad_ref, log_ref, cos_ref, sin_ref, column_ref, row_ref, out_ref
):
    scale = HEAD_DIM ** (-0.5)
    cosine, sine = cos_ref[...], sin_ref[...]
    visible = seen(column_ref[...], row_ref[...])
    wide = 2 * HEAD_DIM
    pair_count = query_ref.shape[1] // wide
    first = lax.broadcasted_iota(jnp.int32, cosine.shape, 1) < HEAD_DIM
    lanes = lax.broadcasted_iota(jnp.int32, cosine.shape, 1)
    keys_values = kv_ref[...]
    swapped = pltpu.roll(keys_values.astype(jnp.float32), HEAD_DIM, 1).astype(jnp.bfloat16)
    keys = jnp.where(first, keys_values, swapped)
    values = jnp.where(first, swapped, keys_values)
    logs = log_ref[...]
    grad_keys = jnp.zeros(cosine.shape, jnp.float32)
    grad_values = jnp.zeros(cosine.shape, jnp.float32)
    for pair in range(pair_count):
        at = slice(pair * wide, (pair + 1) * wide)
        query, grad = query_ref[:, at], grad_ref[:, at]
        results = []
        for member in range(2):
            chosen = first if member == 0 else jnp.logical_not(first)
            one = jnp.where(chosen, query, jnp.zeros_like(query))
            grad_one = jnp.where(chosen, grad, jnp.zeros_like(grad))
            log_one = jnp.sum(
                jnp.where(lanes == 2 * pair + member, logs, 0.0), axis=1, keepdims=True
            )
            scores = (
                lax.dot_general(
                    one, keys, (((1,), (1,)), ((), ())), preferred_element_type=jnp.float32
                )
                * scale
            )
            probs = jnp.exp(jnp.where(visible, scores, -1000000000.0) - log_one)
            grad_probs = lax.dot_general(
                grad_one, values, (((1,), (1,)), ((), ())), preferred_element_type=jnp.float32
            )
            inner_sum = jnp.sum(probs * grad_probs, axis=1, keepdims=True)
            grad_scores = (probs * (grad_probs - inner_sum)).astype(jnp.bfloat16)
            results.append(dot_rows(grad_scores, keys) * scale)
            grad_keys = grad_keys + contract_rows(grad_scores, one)
            grad_values = grad_values + contract_rows(probs.astype(jnp.bfloat16), grad_one)
        joined = jnp.where(first, results[0], results[1])
        out_ref[:, at] = turn(joined, cosine, -sine).astype(jnp.bfloat16)
    grad_keys = (grad_keys + pltpu.roll(grad_keys, HEAD_DIM, 1)) * scale
    grad_values = grad_values + pltpu.roll(grad_values, HEAD_DIM, 1)
    last = jnp.where(first, turn(grad_keys, cosine, -sine), grad_values)
    out_ref[:, pair_count * wide :] = last.astype(jnp.bfloat16)


def whole(*_):
    return (0, 0)


def whole_specs(arrays):
    return [pl.BlockSpec(a.shape, whole) for a in arrays]


def attend(raw, cosine, sine, columns, rows):
    length, wide = raw.shape
    query_width = wide - 2 * HEAD_DIM
    heads = query_width // HEAD_DIM
    outs = [
        jax.ShapeDtypeStruct((length, query_width), jnp.bfloat16),
        jax.ShapeDtypeStruct((length, query_width), jnp.bfloat16),
        jax.ShapeDtypeStruct((length, 2 * HEAD_DIM), jnp.bfloat16),
        jax.ShapeDtypeStruct((length, 2 * HEAD_DIM), jnp.float32),
    ]
    args = (raw, cosine, sine, columns, rows)
    return pl.pallas_call(
        attend_kernel,
        grid=(1,),
        in_specs=whole_specs(args),
        out_specs=whole_specs(outs),
        out_shape=outs,
        compiler_params=pltpu.CompilerParams(vmem_limit_bytes=48 * 1024 * 1024),
        cost_estimate=FREE,
        name="attend",
    )(*args)


def attend_back(query, kv, grad, logs, cosine, sine, columns, rows):
    length, query_width = query.shape
    heads = query_width // HEAD_DIM
    out = jax.ShapeDtypeStruct((length, query_width + 2 * HEAD_DIM), jnp.bfloat16)
    args = (query, kv, grad, logs, cosine, sine, columns, rows)
    return pl.pallas_call(
        attend_back_kernel,
        grid=(1,),
        in_specs=whole_specs(args),
        out_specs=pl.BlockSpec(out.shape, whole),
        out_shape=out,
        compiler_params=pltpu.CompilerParams(vmem_limit_bytes=48 * 1024 * 1024),
        cost_estimate=FREE,
        name="attend_back",
    )(*args)


def total_of(refs):
    total = refs[0][...].astype(jnp.float32)
    for ref in refs[1:]:
        total = total + ref[...].astype(jnp.float32)
    return total


def norm_kernel(gain_ref, *refs):
    low_ref, full_ref = refs[-2:]
    rows = total_of(refs[:-2])
    scale = lax.rsqrt(jnp.mean(rows * rows, axis=1, keepdims=True) + epsilon)
    full_ref[...] = rows
    low_ref[...] = (rows * scale * gain_ref[...].astype(jnp.float32)).astype(low_ref.dtype)


def norm_rows(gain, *parts):
    shape = parts[0].shape
    args = (gain.reshape(1, -1),) + parts
    outs = [jax.ShapeDtypeStruct(shape, jnp.bfloat16), jax.ShapeDtypeStruct(shape, jnp.float32)]
    return pl.pallas_call(
        norm_kernel,
        grid=(1,),
        in_specs=whole_specs(args),
        out_specs=whole_specs(outs),
        out_shape=outs,
        compiler_params=pltpu.CompilerParams(vmem_limit_bytes=32 * 1024 * 1024),
        cost_estimate=FREE,
        name="norm_rows",
    )(*args)


def norm_back_kernel(gain_ref, rows_ref, base_ref, *refs):
    low_ref, full_ref, gain_grad_ref = refs[-3:]
    rows, grad = rows_ref[...], total_of(refs[:-3])
    scale = lax.rsqrt(jnp.mean(rows * rows, axis=1, keepdims=True) + epsilon)
    gain_grad_ref[...] = jnp.sum(grad * rows * scale, axis=0, keepdims=True)
    inside = grad * gain_ref[...].astype(jnp.float32)
    slope = jnp.mean(inside * rows, axis=1, keepdims=True)
    result = base_ref[...].astype(jnp.float32) + scale * inside - rows * (scale**3 * slope)
    full_ref[...] = result
    low_ref[...] = result.astype(low_ref.dtype)


def norm_back(gain, rows, base, *parts):
    shape = rows.shape
    args = (gain.reshape(1, -1), rows, base) + parts
    outs = [
        jax.ShapeDtypeStruct(shape, jnp.bfloat16),
        jax.ShapeDtypeStruct(shape, jnp.float32),
        jax.ShapeDtypeStruct((1, shape[1]), jnp.float32),
    ]
    return pl.pallas_call(
        norm_back_kernel,
        grid=(1,),
        in_specs=whole_specs(args),
        out_specs=whole_specs(outs),
        out_shape=outs,
        compiler_params=pltpu.CompilerParams(vmem_limit_bytes=32 * 1024 * 1024),
        cost_estimate=FREE,
        name="norm_back",
    )(*args)


def pick_kernel(place_ref, gate_ref, up_ref, out_ref):
    for at in range(0, gate_ref.shape[1], 128):
        out_ref[0, :, 2 * at : 2 * at + 128] = gate_ref[:, at : at + 128]
        out_ref[0, :, 2 * at + 128 : 2 * at + 256] = up_ref[:, at : at + 128]


def pick_blocks(me, side, gate, up, chips, picks, halved):
    rows, total = gate.shape
    width = total // chips
    if halved:
        rows = rows // 2
    if width % 128:
        both = jnp.concatenate(
            [a.reshape(a.shape[0], chips, width).transpose(1, 0, 2) for a in (gate, up)], axis=2
        )
        if halved:
            both = lax.dynamic_slice_in_dim(both, side * rows, rows, 1)
        return jnp.stack(
            [lax.dynamic_index_in_dim(both, me // 2 ^ j, 0, keepdims=False) for j in picks]
        )
    first = picks[0]
    column = pl.BlockSpec(
        (rows, width), lambda s, place: (place[1] if halved else 0, place[0] // 2 ^ (s + first))
    )
    return pl.pallas_call(
        pick_kernel,
        grid_spec=pltpu.PrefetchScalarGridSpec(
            num_scalar_prefetch=1,
            grid=(len(picks),),
            in_specs=[column, column],
            out_specs=pl.BlockSpec((1, rows, 2 * width), lambda s, place: (s, 0, 0)),
        ),
        out_shape=jax.ShapeDtypeStruct((len(picks), rows, 2 * width), gate.dtype),
        compiler_params=pltpu.CompilerParams(vmem_limit_bytes=16 * 1024 * 1024),
        cost_estimate=FREE,
        name="pick_blocks",
    )(jnp.stack([me, side]), gate, up)


def tile_of(width):
    return 128 if width % 128 == 0 else width


def forward_kernel(place_ref, rows_ref, *refs, marks, shard):
    inner_ref, both_ref, weight_ref = refs[len(marks) :]
    for group, piece_ref in zip(marks, refs):
        count = piece_ref.shape[0] // len(group)
        for at, (p, flip) in enumerate(group):
            start = (place_ref[0] ^ p) * shard
            if flip is not None:
                start = start + (place_ref[1] ^ flip) * count
            weight_ref[pl.ds(pl.multiple_of(start, count), count), :] = piece_ref[
                at * count : (at + 1) * count, :
            ]
    both = dot_rows(rows_ref[...], weight_ref[...])
    half = both.shape[1] // 2
    gate, upward = both[:, :half], both[:, half:]
    both_ref[...] = both
    inner_ref[...] = (gate / (1.0 + jnp.exp(-gate)) * upward).astype(inner_ref.dtype)


def feed_forward(me, side, rows, pieces):
    count, width = rows.shape
    columns = pieces[0][1].shape[1]
    hidden = columns // 2
    tile = tile_of(hidden)
    marks = [mark for mark, _ in pieces]
    arrays = [piece for _, piece in pieces]
    outs = [
        jax.ShapeDtypeStruct((count, hidden), jnp.bfloat16),
        jax.ShapeDtypeStruct((count, columns), jnp.float32),
        jax.ShapeDtypeStruct((width, columns), jnp.bfloat16),
    ]
    return pl.pallas_call(
        functools.partial(
            forward_kernel, marks=marks, shard=width // lax.axis_size("fsdp")
        ),
        grid_spec=pltpu.PrefetchScalarGridSpec(
            num_scalar_prefetch=1,
            grid=(hidden // tile,),
            in_specs=[pl.BlockSpec((count, width), lambda s, place: (0, 0))]
            + [pl.BlockSpec((a.shape[0], 2 * tile), lambda s, place: (0, s)) for a in arrays],
            out_specs=[
                pl.BlockSpec((count, tile), lambda s, place: (0, s)),
                pl.BlockSpec((count, 2 * tile), lambda s, place: (0, s)),
                pl.BlockSpec((width, 2 * tile), lambda s, place: (0, s)),
            ],
        ),
        out_shape=outs,
        compiler_params=pltpu.CompilerParams(vmem_limit_bytes=48 * 1024 * 1024),
        cost_estimate=FREE,
        name="feed_forward",
    )(jnp.stack([me, side]), rows, *arrays)


def backward_kernel(grad_ref, weight_ref, both_ref, out_ref):
    grad = times_transpose(grad_ref[...], weight_ref[...])
    half = both_ref.shape[1] // 2
    gate, upward = both_ref[:, :half], both_ref[:, half:]
    sigmoid = 1.0 / (1.0 + jnp.exp(-gate))
    silu = gate * sigmoid
    out_ref[:, :half] = (
        grad * upward * (sigmoid + silu * (1.0 - sigmoid))
    ).astype(out_ref.dtype)
    out_ref[:, half:] = (grad * silu).astype(out_ref.dtype)


def feed_backward(grad_rows, weight, both):
    count, width = grad_rows.shape
    hidden = weight.shape[0]
    tile = tile_of(hidden)
    return pl.pallas_call(
        backward_kernel,
        grid=(hidden // tile,),
        in_specs=[
            pl.BlockSpec((count, width), lambda s: (0, 0)),
            pl.BlockSpec((tile, width), lambda s: (s, 0)),
            pl.BlockSpec((count, 2 * tile), lambda s: (0, s)),
        ],
        out_specs=pl.BlockSpec((count, 2 * tile), lambda s: (0, s)),
        out_shape=jax.ShapeDtypeStruct((count, 2 * hidden), jnp.bfloat16),
        compiler_params=pltpu.CompilerParams(vmem_limit_bytes=40 * 1024 * 1024),
        cost_estimate=FREE,
        name="feed_backward",
    )(grad_rows, weight, both)


def product_kernel(left_ref, right_ref, out_ref, *, kind):
    multiply = {"rows": dot_rows, "transpose": times_transpose, "outer": contract_rows}[kind]
    out_ref[...] = multiply(left_ref[...], right_ref[...]).astype(out_ref.dtype)


def product(kind, left, right, dtype):
    rows = left.shape[1 if kind == "outer" else 0]
    columns = right.shape[0 if kind == "transpose" else 1]
    tile = 256 if columns % 256 == 0 else 128
    right_spec = (
        pl.BlockSpec((tile, right.shape[1]), lambda s: (s, 0))
        if kind == "transpose"
        else pl.BlockSpec((right.shape[0], tile), lambda s: (0, s))
    )
    return pl.pallas_call(
        functools.partial(product_kernel, kind=kind),
        grid=(columns // tile,),
        in_specs=[pl.BlockSpec(left.shape, lambda s: (0, 0)), right_spec],
        out_specs=pl.BlockSpec((rows, tile), lambda s: (0, s)),
        out_shape=jax.ShapeDtypeStruct((rows, columns), dtype),
        compiler_params=pltpu.CompilerParams(vmem_limit_bytes=40 * 1024 * 1024),
        cost_estimate=FREE,
        name="product_" + kind,
    )(left, right)


def outer_kernel(place_ref, left_ref, right_ref, left_other_ref, right_other_ref, out_ref):
    total = contract_rows(left_ref[...], right_ref[...])
    total = total + contract_rows(left_other_ref[...], right_other_ref[...])
    out_ref[0] = total.astype(out_ref.dtype)


def outer_blocks(me, left, right, left_other, right_other, picks):
    tokens, width = right.shape
    rows = left.shape[1] // lax.axis_size("fsdp")
    first = picks[0]
    jump = picks[1] - first if len(picks) > 1 else 1
    column = pl.BlockSpec((tokens, rows), lambda s, place: (0, place[0] ^ (first + jump * s)))
    full = pl.BlockSpec((tokens, width), lambda s, place: (0, 0))
    return pl.pallas_call(
        outer_kernel,
        grid_spec=pltpu.PrefetchScalarGridSpec(
            num_scalar_prefetch=1,
            grid=(len(picks),),
            in_specs=[column, full, column, full],
            out_specs=pl.BlockSpec((1, rows, width), lambda s, place: (s, 0, 0)),
        ),
        out_shape=jax.ShapeDtypeStruct((len(picks), rows, width), jnp.bfloat16),
        compiler_params=pltpu.CompilerParams(vmem_limit_bytes=40 * 1024 * 1024),
        cost_estimate=FREE,
        name="outer_blocks",
    )(me.reshape(1), left, right, left_other, right_other)


def place_kernel(place_ref, near_ref, far_ref, out_ref):
    @pl.when(pl.program_id(1) == 0)
    def _():
        out_ref[...] = near_ref[...]

    @pl.when(pl.program_id(1) == 1)
    def _():
        out_ref[...] = far_ref[...]


def place_blocks(me, near, far):
    chips, rows, width = near.shape
    block = pl.BlockSpec((1, rows, width), lambda j, b, place: (j, 0, 0))
    return pl.pallas_call(
        place_kernel,
        grid_spec=pltpu.PrefetchScalarGridSpec(
            num_scalar_prefetch=1,
            grid=(chips, 2),
            in_specs=[block, block],
            out_specs=pl.BlockSpec(
                (1, rows, width), lambda j, b, place: (place[0] ^ (2 * j + b), 0, 0)
            ),
        ),
        out_shape=jax.ShapeDtypeStruct((2 * chips, rows, width), near.dtype),
        compiler_params=pltpu.CompilerParams(vmem_limit_bytes=16 * 1024 * 1024),
        cost_estimate=FREE,
        name="place_blocks",
    )(me.reshape(1), near, far).reshape(2 * chips * rows, width)


def spread_first(place_ref, piece_ref, gate_ref, up_ref):
    for at in range(0, gate_ref.shape[1], 128):
        gate_ref[:, at : at + 128] = piece_ref[:, 2 * at : 2 * at + 128].astype(jnp.float32)
        up_ref[:, at : at + 128] = piece_ref[:, 2 * at + 128 : 2 * at + 256].astype(jnp.float32)


def spread_next(place_ref, piece_ref, gate_in, up_in, gate_ref, up_ref):
    spread_first(place_ref, piece_ref, gate_ref, up_ref)


def spread(me, j, piece, chips, held):
    rows, both = piece.shape
    width = both // 2
    out = jax.ShapeDtypeStruct((rows, width * chips), jnp.float32)
    column = pl.BlockSpec((rows, width), lambda s, place: (0, place[0] // 2 ^ j))
    anywhere = pl.BlockSpec(memory_space=pl.ANY)
    return pl.pallas_call(
        spread_next if held else spread_first,
        grid_spec=pltpu.PrefetchScalarGridSpec(
            num_scalar_prefetch=1,
            grid=(1,),
            in_specs=[pl.BlockSpec((rows, both), lambda s, place: (0, 0))]
            + [anywhere] * len(held),
            out_specs=[column, column],
        ),
        out_shape=[out, out],
        input_output_aliases={2: 0, 3: 1} if held else {},
        compiler_params=pltpu.CompilerParams(vmem_limit_bytes=24 * 1024 * 1024),
        cost_estimate=FREE,
        name="spread",
    )(me.reshape(1), piece, *held)


class Flow:
    def __init__(self, token):
        self.token = token

    def after(self, *arrays):
        return lax.optimization_barrier((self.token,) + tuple(arrays))[1:]

    def until(self, *arrays):
        held = lax.optimization_barrier((self.token,) + tuple(arrays))
        self.token = held[0]
        return held[1:]


class Chain:
    def __init__(self, flow, copies, index):
        self.flow, self.copies, self.index = flow, copies, index
        half = copies // 2
        ends = [(s, copies - 1 - s) for s in range(half - 1)]
        self.stages = [([(a, a + 1), (b, b - 1)], None) for a, b in ends]
        self.stages.append(([(half - 1, half), (half, half - 1)], None))
        self.stages += [([(a + 1, a), (b - 1, b)], (a, b)) for a, b in reversed(ends)]
        self.waiting, self.moving, self.results = [], [], {}

    def add(self, name, *parts):
        self.waiting.append((name, parts))

    def start(self, parts, stage):
        return [lax.ppermute(part, "rep", self.stages[stage][0]) for part in parts]

    def step(self):
        moving, self.moving = self.moving, []
        if self.waiting:
            name, parts = self.waiting.pop(0)
            parts = self.flow.after(*parts)
            self.moving.append((name, parts, self.start(parts, 0), 0))
        if not moving:
            return
        arrived = iter(self.flow.until(*[array for item in moving for array in item[2]]))
        summed = []
        for name, parts, came, stage in moving:
            came = [next(arrived) for _ in came]
            outer = self.stages[stage][1]
            if outer is None:
                parts = [
                    (a.astype(jnp.float32) + b.astype(jnp.float32)).astype(a.dtype)
                    for a, b in zip(parts, came)
                ]
            else:
                here = (self.index == outer[0]) | (self.index == outer[1])
                parts = [jnp.where(here, b, a) for a, b in zip(parts, came)]
            if stage + 1 == len(self.stages):
                self.results[name] = parts
            else:
                summed.append((name, parts, stage + 1))
        ready = iter(self.flow.until(*[array for item in summed for array in item[1]]))
        for name, parts, stage in summed:
            parts = [next(ready) for _ in parts]
            self.moving.append((name, parts, self.start(parts, stage), stage))

    def finish(self):
        while self.waiting or self.moving:
            self.step()


def local(
    tokens,
    cotangent,
    mixer_gain,
    query_weight,
    key_weight,
    value_weight,
    output_weight,
    feed_gain,
    gate_weight,
    up_weight,
    down_weight,
    doc_ids,
    prefix_len,
    block_order,
):
    tok_count, width = tokens.shape[2:]
    devices = lax.axis_size("fsdp")
    chips = devices // 2
    copies = lax.axis_size("rep")
    me = lax.axis_index("fsdp")
    core = me % 2
    copy_index = lax.axis_index("rep")
    side = copy_index % 2
    length = tok_count * devices
    shard_rows = width // devices
    half_shard = shard_rows // 2
    query_width = HEADS // chips * HEAD_DIM
    sharing = max(1, chips // KV_HEADS)
    down_rows = down_weight.shape[0]
    hidden_width = 2 * down_rows
    low = jnp.bfloat16
    full = jnp.float32
    flow = Flow(jnp.zeros((8, 128), full) + copy_index.astype(full))
    chain = Chain(flow, copies, copy_index)

    def swap(array, bits):
        return lax.ppermute(array, "fsdp", [(d, d ^ bits) for d in range(devices)])

    def swap_copies(array, bits):
        return lax.ppermute(array, "rep", [(d, d ^ bits) for d in range(copies)])

    def one_of(array, index, axis=0):
        return lax.dynamic_index_in_dim(array, index, axis, keepdims=False)

    def both_cores(mine, other):
        return place_blocks(core, mine[None], other[None])

    def gather_start(own):
        return (own, swap(own, 2), swap(own, 4)) if chips == 4 else (own,)

    def gather_end(parts):
        if chips == 4:
            own, along_x, along_y = parts
            mid = own.shape[0] // 2
            return jnp.concatenate(
                [own, along_x, along_y, swap(along_y[:mid], 2), swap(along_x[mid:], 4)], axis=0
            )
        (own,) = parts
        bits = 2
        while bits < devices:
            own = jnp.concatenate([own, swap(own, bits)], axis=0)
            bits = 2 * bits
        return own

    def scatter_start(partial):
        if chips != 4:
            return (partial,)
        mine, to_x, to_y, across = jnp.split(partial, 4, axis=0)
        mid = mine.shape[0] // 2
        across = across.astype(low)
        return mine, to_x, to_y, swap(across[:mid], 2), swap(across[mid:], 4)

    def scatter_end(parts):
        if chips == 4:
            mine, to_x, to_y, from_x, from_y = parts
            mid = mine.shape[0] // 2
            to_x = jnp.concatenate([to_x[:mid], to_x[mid:] + from_y.astype(full)], axis=0)
            to_y = jnp.concatenate([to_y[:mid] + from_x.astype(full), to_y[mid:]], axis=0)
            came_x, came_y = swap(to_x.astype(low), 2), swap(to_y.astype(low), 4)
            return mine, came_x, came_y
        (partial,) = parts
        bits = devices // 2
        while bits > 1:
            rows = partial.shape[0] // 2
            partial = partial[:rows] + swap(partial[rows:].astype(low), bits).astype(full)
            bits = bits // 2
        return (partial,)

    def swap_cores(array, pieces):
        rows = array.shape[0] // pieces
        return [swap(array[at * rows : (at + 1) * rows], 1) for at in range(pieces)]

    def by_core(array):
        mine, other = one_of(array, core), one_of(array, 1 - core)
        return jnp.concatenate([mine, swap(other, 1)], axis=0)

    def by_token(rows):
        mine, other = rows[:tok_count], swap(rows[tok_count:], 1)
        return jnp.where(core == 0, jnp.stack([mine, other]), jnp.stack([other, mine]))[None]

    own_tokens = by_core(tokens[0])
    query_blocks = query_weight.reshape(shard_rows, chips, query_width).transpose(1, 0, 2)
    key_value = [
        jnp.repeat(a.reshape(shard_rows, KV_HEADS, HEAD_DIM).transpose(1, 0, 2), sharing, axis=0)
        for a in (key_weight, value_weight)
    ]
    mixer_blocks = jnp.concatenate([query_blocks] + key_value, axis=2)
    mixer_near = [one_of(mixer_blocks, me // 2 ^ j) for j in range(chips)]
    own_tokens, *mixer_near = flow.until(own_tokens, *mixer_near)
    normed_own, inputs = norm_rows(mixer_gain, own_tokens)
    normed_own, gate_weight, up_weight, block_order = flow.until(
        normed_own, gate_weight, up_weight, block_order
    )
    normed_parts = gather_start(normed_own)
    mixer_near = [swap(piece, 2 * j) if j else piece for j, piece in enumerate(mixer_near)]

    info = positions(
        one_of(block_order[0], core), one_of(doc_ids[0], core), one_of(prefix_len[0], core), length
    )
    facts = jnp.stack(info).reshape(4, devices, tok_count)
    facts = jnp.stack([one_of(facts, me ^ p, 1) for p in range(devices)], axis=1)
    place, member, relative, limit = facts.reshape(4, length)
    rows = jnp.concatenate([jnp.stack([place, member, limit]), jnp.zeros((5, length), jnp.int32)])
    columns = jnp.stack([place, member], axis=1)
    angle = angles_for(relative)
    cosine, sine = jnp.cos(angle), jnp.sin(angle)
    cosine = jnp.concatenate([cosine] * 4, axis=1)
    sine = jnp.concatenate([-sine, sine, -sine, sine], axis=1)

    feed_own = pick_blocks(me, side, gate_weight, up_weight, chips, range(1), False)[0]
    feed_away = pick_blocks(me, side, gate_weight, up_weight, chips, range(1, chips), True)
    output_rows = both_cores(output_weight, swap(output_weight, 1))
    down_all = both_cores(down_weight, swap(down_weight, 1))
    grad_rows = by_core(cotangent[0])
    feed_own_far = swap(feed_own, 1)
    cosine, sine, rows, columns, feed_own_far, feed_away, output_rows, down_all, *held = flow.until(
        cosine,
        sine,
        rows,
        columns,
        feed_own_far,
        feed_away,
        output_rows,
        down_all,
        *mixer_near,
        *normed_parts,
    )
    mixer_near, normed_parts = jnp.stack(held[:chips]), held[chips:]
    normed, mixer_near, grad_rows = flow.until(gather_end(normed_parts), mixer_near, grad_rows)
    split = (chips + 1) // 2 + 1
    away = [swap(flow.after(feed_away[j - 1])[0], 2 * j) for j in range(1, chips)]
    mixer_far = jnp.stack([swap(piece, 1) for piece in flow.after(*mixer_near)])
    mixer_columns = place_blocks(me, mixer_near, mixer_far)
    raw = product("rows", normed, mixer_columns, full)
    attended, query, kv, logs = attend(raw, cosine, sine, columns, rows)
    branch = product("rows", attended, output_rows, full)
    branch, *away = flow.until(branch, *away)
    early = swap_copies(jnp.concatenate(away[: split - 1], axis=0), 1)
    late = swap_copies(jnp.concatenate(away[split - 1 :], axis=0), 1)
    away_far = [swap(piece, 1) for piece in flow.after(*away)]
    parts = scatter_end(scatter_start(flow.after(branch)[0]))
    normed_two_own, hidden = norm_rows(feed_gain, inputs, *parts)
    normed_two_own, early, *away_far = flow.until(normed_two_own, early, *away_far)
    other = [early[j * half_shard : (j + 1) * half_shard] for j in range(split - 1)]
    other_far = [swap(piece, 1) for piece in other]
    normed_two_parts = flow.until(*gather_start(normed_two_own))
    cotangent_parts = gather_start(flow.after(grad_rows)[0])
    normed_two, late, *held = flow.until(
        gather_end(normed_two_parts), late, *other_far, *cotangent_parts
    )
    other_far, cotangent_parts = list(held[: split - 1]), held[split - 1 :]
    other += [late[j * half_shard : (j + 1) * half_shard] for j in range(chips - split)]
    other_far += list(flow.until(*[swap(piece, 1) for piece in other[split - 1 :]]))
    all_grad_rows = gather_end(cotangent_parts)
    normed_two_other = swap_cores(flow.after(normed_two)[0], 4)
    normed_other = swap_cores(flow.after(normed)[0], 4)
    feed_pieces = [([(0, None)], feed_own), ([(1, None)], feed_own_far)]
    for j in range(1, chips):
        feed_pieces.append(([(2 * j, 0)], away[j - 1]))
        feed_pieces.append(([(2 * j + 1, 0)], away_far[j - 1]))
        feed_pieces.append(([(2 * j, 1)], other[j - 1]))
        feed_pieces.append(([(2 * j + 1, 1)], other_far[j - 1]))
    inner, both, feed_columns = feed_forward(me, side, normed_two, feed_pieces)
    inner, both, feed_columns, all_grad_rows, *held = flow.until(
        inner, both, feed_columns, all_grad_rows, *normed_two_other, *normed_other
    )
    normed_two_other = jnp.concatenate(held[:4], axis=0)
    normed_other = jnp.concatenate(held[4:], axis=0)

    down_partial = product("outer", inner, all_grad_rows, low).reshape(2, down_rows, width)
    came = swap(one_of(down_partial, 1 - core), 1)
    down_part = (one_of(down_partial, core).astype(full) + came.astype(full)).astype(low)
    (down_part,) = flow.until(down_part)
    for piece, part in enumerate(jnp.split(down_part, 2, axis=0)):
        chain.add(("down", piece), part)
    chain.step()

    (grad_both,) = flow.until(feed_backward(flow.after(all_grad_rows)[0], down_all, both))
    grad_both_other = swap_cores(grad_both, 4)
    partial_two = product("transpose", grad_both, feed_columns, full)
    partial_two, *grad_both_other = flow.until(partial_two, *grad_both_other)
    chain.step()
    grad_both, *grad_both_other = flow.after(grad_both, *grad_both_other)
    grad_both_other = jnp.concatenate(grad_both_other, axis=0)
    parts = scatter_end(scatter_start(flow.after(partial_two)[0]))
    picks = range(0, devices, 2)
    pieces = outer_blocks(me, normed_two, grad_both, normed_two_other, grad_both_other, picks)
    pieces, *parts = flow.until(pieces, *parts)
    chain.add(("feed", 0), pieces[0])
    chain.step()
    (pieces,) = flow.after(pieces)
    pieces = [pieces[j] for j in range(chips)]
    grad_branch_own, grad_hidden, feed_part = norm_back(
        feed_gain, hidden, grad_rows, *flow.after(*parts)
    )
    grad_branch = gather_end(gather_start(grad_branch_own))
    output_partial = product("outer", attended, grad_branch, low)
    output_partial = output_partial.reshape(2, shard_rows, width)
    came = jnp.concatenate(swap_cores(one_of(output_partial, 1 - core), 2), axis=0)
    output_part = (one_of(output_partial, core).astype(full) + came.astype(full)).astype(low)
    grad_branch, output_part, *pieces = flow.until(grad_branch, output_part, *pieces)
    chain.add("output", output_part)
    chain.step()
    moved = {j: swap(flow.after(pieces[j])[0], 2 * j) for j in range(1, split)}
    grad_attended = product("transpose", *flow.after(grad_branch), output_rows, low)
    grad_mixer = attend_back(query, kv, grad_attended, logs, cosine, sine, columns, rows)
    grad_mixer_other = jnp.concatenate(swap_cores(grad_mixer, 2), axis=0)
    partial = product("transpose", grad_mixer, mixer_columns, full)
    mixer_pieces = outer_blocks(me, normed, grad_mixer, normed_other, grad_mixer_other, picks)
    partial, mixer_pieces, *early = flow.until(
        partial, mixer_pieces, *[moved[j] for j in range(1, split)]
    )
    for j, piece in enumerate(early, 1):
        chain.add(("feed", j), piece)
    chain.step()
    parts = scatter_end(scatter_start(flow.after(partial)[0]))
    down = product("rows", *flow.after(inner), down_all, full)
    down, *parts = flow.until(down, *parts)
    chain.step()
    for _ in range(split - 3):
        chain.step()
    (mixer_pieces,) = flow.after(mixer_pieces)
    mixer_pieces = [
        swap(mixer_pieces[j], 2 * j) if j else mixer_pieces[j] for j in range(chips)
    ]
    input_grad, _, mixer_part = norm_back(mixer_gain, inputs, grad_hidden, *flow.after(*parts))
    gains = jnp.concatenate([mixer_part, feed_part]).reshape(2, 8, width // 8)
    bits = 1
    while bits < devices:
        gains = gains + swap(gains, bits)
        bits = 2 * bits
    gains, input_grad, *mixer_pieces = flow.until(gains, input_grad, *mixer_pieces)
    chain.add("mixer", jnp.stack(mixer_pieces), gains)
    chain.step()
    late = flow.until(*[swap(flow.after(pieces[j])[0], 2 * j) for j in range(split, chips)])
    half = shard_rows // 2
    for piece in range(2):
        chain.add(("last", piece), *[a[piece * half : (piece + 1) * half] for a in late])
    chain.step()
    parts = flow.until(*scatter_end(scatter_start(flow.after(down)[0])))
    layer_out = by_token((hidden + sum(part.astype(full) for part in parts)).astype(low))
    input_grad = by_token(input_grad)
    chain.finish()
    results = chain.results
    down_grad = jnp.concatenate([results["down", piece][0] for piece in range(2)], axis=0)
    down_grad = down_grad.astype(full)
    output_grad = results["output"][0].astype(full)
    done = [results["feed", j][0] for j in range(split)]
    done += [jnp.concatenate(both, axis=0) for both in zip(results["last", 0], results["last", 1])]
    if hidden_width % 128:
        stacked = jnp.stack(done)
        ordered = jnp.stack([one_of(stacked, me // 2 ^ j) for j in range(chips)])
        ordered = ordered.astype(full).reshape(chips, shard_rows, 2, hidden_width)
        gate_grad, up_grad = ordered.transpose(2, 1, 0, 3).reshape(2, shard_rows, -1)
    else:
        held = ()
        for j, piece in enumerate(done):
            held = spread(me, j, piece, chips, held)
        gate_grad, up_grad = held
    mixer_grads = results["mixer"][0]
    mixer_grads = jnp.stack([one_of(mixer_grads, me // 2 ^ j) for j in range(chips)])
    mixer_grads = mixer_grads.astype(full)
    query_grad = mixer_grads[:, :, :query_width].transpose(1, 0, 2).reshape(shard_rows, -1)
    shared = (
        mixer_grads[:, :, query_width:]
        .reshape(KV_HEADS, sharing, shard_rows, 2, HEAD_DIM)
        .sum(axis=1)
    )
    key_grad = shared[:, :, 0].transpose(1, 0, 2).reshape(shard_rows, -1)
    value_grad = shared[:, :, 1].transpose(1, 0, 2).reshape(shard_rows, -1)
    mixer_total, feed_total = results["mixer"][1].reshape(2, width)
    return (
        layer_out,
        input_grad,
        mixer_total,
        query_grad,
        key_grad,
        value_grad,
        output_grad,
        feed_total,
        gate_grad,
        up_grad,
        down_grad,
    )


def solution(mesh):
    placed = (
        P("rep", None, "fsdp", None),
        P("rep", None, "fsdp", None),
        P(),
        P("fsdp", None),
        P("fsdp", None),
        P("fsdp", None),
        P("fsdp", None),
        P(),
        P("fsdp", None),
        P("fsdp", None),
        P("fsdp", None),
        P("rep", None, None),
        P("rep", None, None),
        P("rep", None, None),
    )
    return jax.shard_map(
        local,
        mesh=mesh,
        in_specs=placed,
        out_specs=(
            P("rep", None, "fsdp", None),
            P("rep", None, "fsdp", None),
            P(),
            P("fsdp", None),
            P("fsdp", None),
            P("fsdp", None),
            P("fsdp", None),
            P(),
            P("fsdp", None),
            P("fsdp", None),
            P("fsdp", None),
        ),
        check_vma=False,
    )
```

```python
import functools

import jax
import jax.numpy as jnp
from jax import lax
from jax.experimental import pallas as pl
from jax.experimental.pallas import tpu as pltpu
from jax.sharding import PartitionSpec as P

HEADS = 32
KV_HEADS = 4
HEAD_DIM = 64
MICRO = 2
SEGS = 3


epsilon = 1e-05
FREE = pl.CostEstimate(flops=0, transcendentals=0, bytes_accessed=0)


def positions(order_row, doc_row, prefix_row, length):
    count = order_row.shape[0]
    block_width = length // count
    index = jnp.arange(length, dtype=jnp.int32)
    slot = index // block_width
    block = jnp.sum(
        jnp.where(
            slot[:, None] == jnp.arange(count, dtype=jnp.int32)[None, :], order_row[None, :], 0
        ),
        axis=1,
        dtype=jnp.int32,
    )
    place = block * block_width + index % block_width
    labels = jnp.arange(SEGS, dtype=jnp.int32)
    starts = jnp.sum(
        (doc_row[None, :] < labels[:, None]).astype(jnp.int32), axis=1, dtype=jnp.int32
    )
    member = jnp.sum(
        (place[:, None] >= starts[None, 1:]).astype(jnp.int32), axis=1, dtype=jnp.int32
    )
    picked = member[:, None] == labels[None, :]
    start_of = jnp.sum(jnp.where(picked, starts[None, :], 0), axis=1, dtype=jnp.int32)
    limit = jnp.sum(
        jnp.where(picked, starts[None, :] + prefix_row[None, :], 0), axis=1, dtype=jnp.int32
    )
    return (place, member, place - start_of, limit)


def angles_for(relative):
    halfway = HEAD_DIM // 2
    frequency = 10000.0 ** (-(2.0 * jnp.arange(halfway, dtype=jnp.float32)) / HEAD_DIM)
    return relative.astype(jnp.float32)[:, None] * frequency[None, :]


def rms_scale(values, gain):
    return values * lax.rsqrt(jnp.mean(values * values, axis=1, keepdims=True) + epsilon) * gain


def gated(gate_part, up_part):
    return jax.nn.silu(gate_part) * up_part


def contract_rows(left, right):
    return lax.dot_general(
        left, right, (((0,), (0,)), ((), ())), preferred_element_type=jnp.float32
    )


def times_transpose(left, right):
    return lax.dot_general(
        left, right, (((1,), (1,)), ((), ())), preferred_element_type=jnp.float32
    )


def dot_rows(left, right):
    return jnp.dot(left, right, preferred_element_type=jnp.float32)


def turn(field, cosine, sine):
    lane = lax.broadcasted_iota(jnp.int32, field.shape, 1) % HEAD_DIM
    half = HEAD_DIM // 2
    swapped = jnp.where(
        lane < half, pltpu.roll(field, 2 * HEAD_DIM - half, 1), pltpu.roll(field, half, 1)
    )
    return field * cosine + swapped * sine


def seen(columns, rows):
    place_q, member_q = columns[:, 0:1], columns[:, 1:2]
    place_k, member_k, limit_k = rows[0:1, :], rows[1:2, :], rows[2:3, :]
    return (member_q == member_k) & ((place_k <= place_q) | (place_k < limit_k))


def attend_kernel(raw_ref, cos_ref, sin_ref, column_ref, row_ref, out_ref, query_ref, kv_ref, log_ref):
    scale = HEAD_DIM ** (-0.5)
    cosine, sine = cos_ref[...], sin_ref[...]
    visible = seen(column_ref[...], row_ref[...])
    wide = 2 * HEAD_DIM
    pair_count = raw_ref.shape[1] // wide - 1
    first = lax.broadcasted_iota(jnp.int32, cosine.shape, 1) < HEAD_DIM
    kv = raw_ref[:, pair_count * wide :]
    keys_values = jnp.where(first, turn(kv, cosine, sine), kv)
    swapped = pltpu.roll(keys_values, HEAD_DIM, 1)
    keys = jnp.where(first, keys_values, swapped).astype(jnp.bfloat16)
    values = jnp.where(first, swapped, keys_values).astype(jnp.bfloat16)
    kv_ref[...] = keys_values.astype(jnp.bfloat16)
    logs = jnp.zeros(cosine.shape, jnp.float32)
    lanes = lax.broadcasted_iota(jnp.int32, cosine.shape, 1)
    for pair in range(pair_count):
        at = slice(pair * wide, (pair + 1) * wide)
        query = turn(raw_ref[:, at], cosine, sine).astype(jnp.bfloat16)
        query_ref[:, at] = query
        results = []
        for member in range(2):
            chosen = first if member == 0 else jnp.logical_not(first)
            one = jnp.where(chosen, query, jnp.zeros_like(query))
            scores = (
                lax.dot_general(
                    one, keys, (((1,), (1,)), ((), ())), preferred_element_type=jnp.float32
                )
                * scale
            )
            scores = jnp.where(visible, scores, -1000000000.0)
            peak = jnp.max(scores, axis=1, keepdims=True)
            raised = jnp.exp(scores - peak)
            totals = jnp.sum(raised, axis=1, keepdims=True)
            probs = (raised * (1.0 / totals)).astype(jnp.bfloat16)
            results.append(dot_rows(probs, values))
            logs = jnp.where(lanes == 2 * pair + member, peak + jnp.log(totals), logs)
        out_ref[:, at] = jnp.where(first, results[0], results[1]).astype(jnp.bfloat16)
    log_ref[...] = logs


def attend_back_kernel(
    query_ref, kv_ref, grad_ref, log_ref, cos_ref, sin_ref, column_ref, row_ref, out_ref
):
    scale = HEAD_DIM ** (-0.5)
    cosine, sine = cos_ref[...], sin_ref[...]
    visible = seen(column_ref[...], row_ref[...])
    wide = 2 * HEAD_DIM
    pair_count = query_ref.shape[1] // wide
    first = lax.broadcasted_iota(jnp.int32, cosine.shape, 1) < HEAD_DIM
    lanes = lax.broadcasted_iota(jnp.int32, cosine.shape, 1)
    keys_values = kv_ref[...]
    swapped = pltpu.roll(keys_values.astype(jnp.float32), HEAD_DIM, 1).astype(jnp.bfloat16)
    keys = jnp.where(first, keys_values, swapped)
    values = jnp.where(first, swapped, keys_values)
    logs = log_ref[...]
    grad_keys = jnp.zeros(cosine.shape, jnp.float32)
    grad_values = jnp.zeros(cosine.shape, jnp.float32)
    for pair in range(pair_count):
        at = slice(pair * wide, (pair + 1) * wide)
        query, grad = query_ref[:, at], grad_ref[:, at]
        results = []
        for member in range(2):
            chosen = first if member == 0 else jnp.logical_not(first)
            one = jnp.where(chosen, query, jnp.zeros_like(query))
            grad_one = jnp.where(chosen, grad, jnp.zeros_like(grad))
            log_one = jnp.sum(
                jnp.where(lanes == 2 * pair + member, logs, 0.0), axis=1, keepdims=True
            )
            scores = (
                lax.dot_general(
                    one, keys, (((1,), (1,)), ((), ())), preferred_element_type=jnp.float32
                )
                * scale
            )
            probs = jnp.exp(jnp.where(visible, scores, -1000000000.0) - log_one)
            grad_probs = lax.dot_general(
                grad_one, values, (((1,), (1,)), ((), ())), preferred_element_type=jnp.float32
            )
            inner_sum = jnp.sum(probs * grad_probs, axis=1, keepdims=True)
            grad_scores = (probs * (grad_probs - inner_sum)).astype(jnp.bfloat16)
            results.append(dot_rows(grad_scores, keys) * scale)
            grad_keys = grad_keys + contract_rows(grad_scores, one)
            grad_values = grad_values + contract_rows(probs.astype(jnp.bfloat16), grad_one)
        joined = jnp.where(first, results[0], results[1])
        out_ref[:, at] = turn(joined, cosine, -sine).astype(jnp.bfloat16)
    grad_keys = (grad_keys + pltpu.roll(grad_keys, HEAD_DIM, 1)) * scale
    grad_values = grad_values + pltpu.roll(grad_values, HEAD_DIM, 1)
    last = jnp.where(first, turn(grad_keys, cosine, -sine), grad_values)
    out_ref[:, pair_count * wide :] = last.astype(jnp.bfloat16)


def whole(*_):
    return (0, 0)


def whole_specs(arrays):
    return [pl.BlockSpec(a.shape, whole) for a in arrays]


def attend(raw, cosine, sine, columns, rows):
    length, wide = raw.shape
    query_width = wide - 2 * HEAD_DIM
    heads = query_width // HEAD_DIM
    outs = [
        jax.ShapeDtypeStruct((length, query_width), jnp.bfloat16),
        jax.ShapeDtypeStruct((length, query_width), jnp.bfloat16),
        jax.ShapeDtypeStruct((length, 2 * HEAD_DIM), jnp.bfloat16),
        jax.ShapeDtypeStruct((length, 2 * HEAD_DIM), jnp.float32),
    ]
    args = (raw, cosine, sine, columns, rows)
    return pl.pallas_call(
        attend_kernel,
        grid=(1,),
        in_specs=whole_specs(args),
        out_specs=whole_specs(outs),
        out_shape=outs,
        compiler_params=pltpu.CompilerParams(vmem_limit_bytes=48 * 1024 * 1024),
        cost_estimate=FREE,
        name="attend",
    )(*args)


def attend_back(query, kv, grad, logs, cosine, sine, columns, rows):
    length, query_width = query.shape
    heads = query_width // HEAD_DIM
    out = jax.ShapeDtypeStruct((length, query_width + 2 * HEAD_DIM), jnp.bfloat16)
    args = (query, kv, grad, logs, cosine, sine, columns, rows)
    return pl.pallas_call(
        attend_back_kernel,
        grid=(1,),
        in_specs=whole_specs(args),
        out_specs=pl.BlockSpec(out.shape, whole),
        out_shape=out,
        compiler_params=pltpu.CompilerParams(vmem_limit_bytes=48 * 1024 * 1024),
        cost_estimate=FREE,
        name="attend_back",
    )(*args)


def total_of(refs):
    total = refs[0][...].astype(jnp.float32)
    for ref in refs[1:]:
        total = total + ref[...].astype(jnp.float32)
    return total


def norm_kernel(gain_ref, *refs):
    low_ref, full_ref = refs[-2:]
    rows = total_of(refs[:-2])
    scale = lax.rsqrt(jnp.mean(rows * rows, axis=1, keepdims=True) + epsilon)
    full_ref[...] = rows
    low_ref[...] = (rows * scale * gain_ref[...].astype(jnp.float32)).astype(low_ref.dtype)


def norm_rows(gain, *parts):
    shape = parts[0].shape
    args = (gain.reshape(1, -1),) + parts
    outs = [jax.ShapeDtypeStruct(shape, jnp.bfloat16), jax.ShapeDtypeStruct(shape, jnp.float32)]
    return pl.pallas_call(
        norm_kernel,
        grid=(1,),
        in_specs=whole_specs(args),
        out_specs=whole_specs(outs),
        out_shape=outs,
        compiler_params=pltpu.CompilerParams(vmem_limit_bytes=32 * 1024 * 1024),
        cost_estimate=FREE,
        name="norm_rows",
    )(*args)


def norm_back_kernel(gain_ref, rows_ref, base_ref, *refs):
    low_ref, full_ref, gain_grad_ref = refs[-3:]
    rows, grad = rows_ref[...], total_of(refs[:-3])
    scale = lax.rsqrt(jnp.mean(rows * rows, axis=1, keepdims=True) + epsilon)
    gain_grad_ref[...] = jnp.sum(grad * rows * scale, axis=0, keepdims=True)
    inside = grad * gain_ref[...].astype(jnp.float32)
    slope = jnp.mean(inside * rows, axis=1, keepdims=True)
    result = base_ref[...].astype(jnp.float32) + scale * inside - rows * (scale**3 * slope)
    full_ref[...] = result
    low_ref[...] = result.astype(low_ref.dtype)


def norm_back(gain, rows, base, *parts):
    shape = rows.shape
    args = (gain.reshape(1, -1), rows, base) + parts
    outs = [
        jax.ShapeDtypeStruct(shape, jnp.bfloat16),
        jax.ShapeDtypeStruct(shape, jnp.float32),
        jax.ShapeDtypeStruct((1, shape[1]), jnp.float32),
    ]
    return pl.pallas_call(
        norm_back_kernel,
        grid=(1,),
        in_specs=whole_specs(args),
        out_specs=whole_specs(outs),
        out_shape=outs,
        compiler_params=pltpu.CompilerParams(vmem_limit_bytes=32 * 1024 * 1024),
        cost_estimate=FREE,
        name="norm_back",
    )(*args)


def pick_kernel(place_ref, gate_ref, up_ref, out_ref):
    for at in range(0, gate_ref.shape[1], 128):
        out_ref[0, :, 2 * at : 2 * at + 128] = gate_ref[:, at : at + 128]
        out_ref[0, :, 2 * at + 128 : 2 * at + 256] = up_ref[:, at : at + 128]


def pick_blocks(me, side, gate, up, chips, picks, halved):
    rows, total = gate.shape
    width = total // chips
    if halved:
        rows = rows // 2
    if width % 128:
        both = jnp.concatenate(
            [a.reshape(a.shape[0], chips, width).transpose(1, 0, 2) for a in (gate, up)], axis=2
        )
        if halved:
            both = lax.dynamic_slice_in_dim(both, side * rows, rows, 1)
        return jnp.stack(
            [lax.dynamic_index_in_dim(both, me // 2 ^ j, 0, keepdims=False) for j in picks]
        )
    first = picks[0]
    column = pl.BlockSpec(
        (rows, width), lambda s, place: (place[1] if halved else 0, place[0] // 2 ^ (s + first))
    )
    return pl.pallas_call(
        pick_kernel,
        grid_spec=pltpu.PrefetchScalarGridSpec(
            num_scalar_prefetch=1,
            grid=(len(picks),),
            in_specs=[column, column],
            out_specs=pl.BlockSpec((1, rows, 2 * width), lambda s, place: (s, 0, 0)),
        ),
        out_shape=jax.ShapeDtypeStruct((len(picks), rows, 2 * width), gate.dtype),
        compiler_params=pltpu.CompilerParams(vmem_limit_bytes=16 * 1024 * 1024),
        cost_estimate=FREE,
        name="pick_blocks",
    )(jnp.stack([me, side]), gate, up)


def tile_of(width):
    return 128 if width % 128 == 0 else width


def forward_kernel(place_ref, rows_ref, *refs, marks, shard):
    inner_ref, both_ref, weight_ref = refs[len(marks) :]
    for group, piece_ref in zip(marks, refs):
        count = piece_ref.shape[0] // len(group)
        for at, (p, flip) in enumerate(group):
            start = (place_ref[0] ^ p) * shard
            if flip is not None:
                start = start + (place_ref[1] ^ flip) * count
            weight_ref[pl.ds(pl.multiple_of(start, count), count), :] = piece_ref[
                at * count : (at + 1) * count, :
            ]
    both = dot_rows(rows_ref[...], weight_ref[...])
    half = both.shape[1] // 2
    gate, upward = both[:, :half], both[:, half:]
    both_ref[...] = both
    inner_ref[...] = (gate / (1.0 + jnp.exp(-gate)) * upward).astype(inner_ref.dtype)


def feed_forward(me, side, rows, pieces):
    count, width = rows.shape
    columns = pieces[0][1].shape[1]
    hidden = columns // 2
    tile = tile_of(hidden)
    marks = [mark for mark, _ in pieces]
    arrays = [piece for _, piece in pieces]
    outs = [
        jax.ShapeDtypeStruct((count, hidden), jnp.bfloat16),
        jax.ShapeDtypeStruct((count, columns), jnp.float32),
        jax.ShapeDtypeStruct((width, columns), jnp.bfloat16),
    ]
    return pl.pallas_call(
        functools.partial(
            forward_kernel, marks=marks, shard=width // lax.axis_size("fsdp")
        ),
        grid_spec=pltpu.PrefetchScalarGridSpec(
            num_scalar_prefetch=1,
            grid=(hidden // tile,),
            in_specs=[pl.BlockSpec((count, width), lambda s, place: (0, 0))]
            + [pl.BlockSpec((a.shape[0], 2 * tile), lambda s, place: (0, s)) for a in arrays],
            out_specs=[
                pl.BlockSpec((count, tile), lambda s, place: (0, s)),
                pl.BlockSpec((count, 2 * tile), lambda s, place: (0, s)),
                pl.BlockSpec((width, 2 * tile), lambda s, place: (0, s)),
            ],
        ),
        out_shape=outs,
        compiler_params=pltpu.CompilerParams(vmem_limit_bytes=48 * 1024 * 1024),
        cost_estimate=FREE,
        name="feed_forward",
    )(jnp.stack([me, side]), rows, *arrays)


def backward_kernel(grad_ref, weight_ref, both_ref, out_ref):
    grad = times_transpose(grad_ref[...], weight_ref[...])
    half = both_ref.shape[1] // 2
    gate, upward = both_ref[:, :half], both_ref[:, half:]
    sigmoid = 1.0 / (1.0 + jnp.exp(-gate))
    silu = gate * sigmoid
    out_ref[:, :half] = (
        grad * upward * (sigmoid + silu * (1.0 - sigmoid))
    ).astype(out_ref.dtype)
    out_ref[:, half:] = (grad * silu).astype(out_ref.dtype)


def feed_backward(grad_rows, weight, both):
    count, width = grad_rows.shape
    hidden = weight.shape[0]
    tile = tile_of(hidden)
    return pl.pallas_call(
        backward_kernel,
        grid=(hidden // tile,),
        in_specs=[
            pl.BlockSpec((count, width), lambda s: (0, 0)),
            pl.BlockSpec((tile, width), lambda s: (s, 0)),
            pl.BlockSpec((count, 2 * tile), lambda s: (0, s)),
        ],
        out_specs=pl.BlockSpec((count, 2 * tile), lambda s: (0, s)),
        out_shape=jax.ShapeDtypeStruct((count, 2 * hidden), jnp.bfloat16),
        compiler_params=pltpu.CompilerParams(vmem_limit_bytes=40 * 1024 * 1024),
        cost_estimate=FREE,
        name="feed_backward",
    )(grad_rows, weight, both)


def product_kernel(left_ref, right_ref, out_ref, *, kind):
    multiply = {"rows": dot_rows, "transpose": times_transpose, "outer": contract_rows}[kind]
    out_ref[...] = multiply(left_ref[...], right_ref[...]).astype(out_ref.dtype)


def product(kind, left, right, dtype):
    rows = left.shape[1 if kind == "outer" else 0]
    columns = right.shape[0 if kind == "transpose" else 1]
    tile = 256 if columns % 256 == 0 else 128
    right_spec = (
        pl.BlockSpec((tile, right.shape[1]), lambda s: (s, 0))
        if kind == "transpose"
        else pl.BlockSpec((right.shape[0], tile), lambda s: (0, s))
    )
    return pl.pallas_call(
        functools.partial(product_kernel, kind=kind),
        grid=(columns // tile,),
        in_specs=[pl.BlockSpec(left.shape, lambda s: (0, 0)), right_spec],
        out_specs=pl.BlockSpec((rows, tile), lambda s: (0, s)),
        out_shape=jax.ShapeDtypeStruct((rows, columns), dtype),
        compiler_params=pltpu.CompilerParams(vmem_limit_bytes=40 * 1024 * 1024),
        cost_estimate=FREE,
        name="product_" + kind,
    )(left, right)


def outer_kernel(place_ref, left_ref, right_ref, left_other_ref, right_other_ref, out_ref):
    total = contract_rows(left_ref[...], right_ref[...])
    total = total + contract_rows(left_other_ref[...], right_other_ref[...])
    out_ref[0] = total.astype(out_ref.dtype)


def outer_blocks(me, left, right, left_other, right_other, picks):
    tokens, width = right.shape
    rows = left.shape[1] // lax.axis_size("fsdp")
    first = picks[0]
    jump = picks[1] - first if len(picks) > 1 else 1
    column = pl.BlockSpec((tokens, rows), lambda s, place: (0, place[0] ^ (first + jump * s)))
    full = pl.BlockSpec((tokens, width), lambda s, place: (0, 0))
    return pl.pallas_call(
        outer_kernel,
        grid_spec=pltpu.PrefetchScalarGridSpec(
            num_scalar_prefetch=1,
            grid=(len(picks),),
            in_specs=[column, full, column, full],
            out_specs=pl.BlockSpec((1, rows, width), lambda s, place: (s, 0, 0)),
        ),
        out_shape=jax.ShapeDtypeStruct((len(picks), rows, width), jnp.bfloat16),
        compiler_params=pltpu.CompilerParams(vmem_limit_bytes=40 * 1024 * 1024),
        cost_estimate=FREE,
        name="outer_blocks",
    )(me.reshape(1), left, right, left_other, right_other)


def place_kernel(place_ref, near_ref, far_ref, out_ref):
    @pl.when(pl.program_id(1) == 0)
    def _():
        out_ref[...] = near_ref[...]

    @pl.when(pl.program_id(1) == 1)
    def _():
        out_ref[...] = far_ref[...]


def place_blocks(me, near, far):
    chips, rows, width = near.shape
    block = pl.BlockSpec((1, rows, width), lambda j, b, place: (j, 0, 0))
    return pl.pallas_call(
        place_kernel,
        grid_spec=pltpu.PrefetchScalarGridSpec(
            num_scalar_prefetch=1,
            grid=(chips, 2),
            in_specs=[block, block],
            out_specs=pl.BlockSpec(
                (1, rows, width), lambda j, b, place: (place[0] ^ (2 * j + b), 0, 0)
            ),
        ),
        out_shape=jax.ShapeDtypeStruct((2 * chips, rows, width), near.dtype),
        compiler_params=pltpu.CompilerParams(vmem_limit_bytes=16 * 1024 * 1024),
        cost_estimate=FREE,
        name="place_blocks",
    )(me.reshape(1), near, far).reshape(2 * chips * rows, width)


def spread_first(place_ref, piece_ref, gate_ref, up_ref):
    for at in range(0, gate_ref.shape[1], 128):
        gate_ref[:, at : at + 128] = piece_ref[:, 2 * at : 2 * at + 128].astype(jnp.float32)
        up_ref[:, at : at + 128] = piece_ref[:, 2 * at + 128 : 2 * at + 256].astype(jnp.float32)


def spread_next(place_ref, piece_ref, gate_in, up_in, gate_ref, up_ref):
    spread_first(place_ref, piece_ref, gate_ref, up_ref)


def spread(me, j, piece, chips, held):
    rows, both = piece.shape
    width = both // 2
    out = jax.ShapeDtypeStruct((rows, width * chips), jnp.float32)
    column = pl.BlockSpec((rows, width), lambda s, place: (0, place[0] // 2 ^ j))
    anywhere = pl.BlockSpec(memory_space=pl.ANY)
    return pl.pallas_call(
        spread_next if held else spread_first,
        grid_spec=pltpu.PrefetchScalarGridSpec(
            num_scalar_prefetch=1,
            grid=(1,),
            in_specs=[pl.BlockSpec((rows, both), lambda s, place: (0, 0))]
            + [anywhere] * len(held),
            out_specs=[column, column],
        ),
        out_shape=[out, out],
        input_output_aliases={2: 0, 3: 1} if held else {},
        compiler_params=pltpu.CompilerParams(vmem_limit_bytes=24 * 1024 * 1024),
        cost_estimate=FREE,
        name="spread",
    )(me.reshape(1), piece, *held)


class Flow:
    def __init__(self, token):
        self.token = token

    def after(self, *arrays):
        return lax.optimization_barrier((self.token,) + tuple(arrays))[1:]

    def until(self, *arrays):
        held = lax.optimization_barrier((self.token,) + tuple(arrays))
        self.token = held[0]
        return held[1:]


class Chain:
    def __init__(self, flow, copies, index):
        self.flow, self.copies, self.index = flow, copies, index
        half = copies // 2
        ends = [(s, copies - 1 - s) for s in range(half - 1)]
        self.stages = [([(a, a + 1), (b, b - 1)], None) for a, b in ends]
        self.stages.append(([(half - 1, half), (half, half - 1)], None))
        self.stages += [([(a + 1, a), (b - 1, b)], (a, b)) for a, b in reversed(ends)]
        self.waiting, self.moving, self.results = [], [], {}

    def add(self, name, *parts):
        self.waiting.append((name, parts))

    def start(self, parts, stage):
        return [lax.ppermute(part, "rep", self.stages[stage][0]) for part in parts]

    def step(self):
        moving, self.moving = self.moving, []
        if self.waiting:
            name, parts = self.waiting.pop(0)
            parts = self.flow.after(*parts)
            self.moving.append((name, parts, self.start(parts, 0), 0))
        if not moving:
            return
        arrived = iter(self.flow.until(*[array for item in moving for array in item[2]]))
        summed = []
        for name, parts, came, stage in moving:
            came = [next(arrived) for _ in came]
            outer = self.stages[stage][1]
            if outer is None:
                parts = [
                    (a.astype(jnp.float32) + b.astype(jnp.float32)).astype(a.dtype)
                    for a, b in zip(parts, came)
                ]
            else:
                here = (self.index == outer[0]) | (self.index == outer[1])
                parts = [jnp.where(here, b, a) for a, b in zip(parts, came)]
            if stage + 1 == len(self.stages):
                self.results[name] = parts
            else:
                summed.append((name, parts, stage + 1))
        for name, parts, stage in summed:
            self.moving.append((name, parts, self.start(parts, stage), stage))

    def finish(self):
        while self.waiting or self.moving:
            self.step()


def local(
    tokens,
    cotangent,
    mixer_gain,
    query_weight,
    key_weight,
    value_weight,
    output_weight,
    feed_gain,
    gate_weight,
    up_weight,
    down_weight,
    doc_ids,
    prefix_len,
    block_order,
):
    tok_count, width = tokens.shape[2:]
    devices = lax.axis_size("fsdp")
    chips = devices // 2
    copies = lax.axis_size("rep")
    me = lax.axis_index("fsdp")
    core = me % 2
    copy_index = lax.axis_index("rep")
    side = copy_index % 2
    length = tok_count * devices
    shard_rows = width // devices
    half_shard = shard_rows // 2
    query_width = HEADS // chips * HEAD_DIM
    sharing = max(1, chips // KV_HEADS)
    down_rows = down_weight.shape[0]
    hidden_width = 2 * down_rows
    low = jnp.bfloat16
    full = jnp.float32
    flow = Flow(jnp.zeros((8, 128), full) + copy_index.astype(full))
    chain = Chain(flow, copies, copy_index)

    def swap(array, bits):
        return lax.ppermute(array, "fsdp", [(d, d ^ bits) for d in range(devices)])

    def swap_copies(array, bits):
        return lax.ppermute(array, "rep", [(d, d ^ bits) for d in range(copies)])

    def one_of(array, index, axis=0):
        return lax.dynamic_index_in_dim(array, index, axis, keepdims=False)

    def both_cores(mine, other):
        return place_blocks(core, mine[None], other[None])

    def gather_start(own):
        return (own, swap(own, 2), swap(own, 4)) if chips == 4 else (own,)

    def gather_end(parts):
        if chips == 4:
            own, along_x, along_y = parts
            mid = own.shape[0] // 2
            return [own, along_x, along_y, swap(along_y[:mid], 2), swap(along_x[mid:], 4)]
        (own,) = parts
        bits = 2
        while bits < devices:
            own = jnp.concatenate([own, swap(own, bits)], axis=0)
            bits = 2 * bits
        return [own]

    def joined(parts):
        return jnp.concatenate(parts, axis=0) if len(parts) > 1 else parts[0]

    def scatter_start(partial):
        if chips != 4:
            return (partial,)
        mine, to_x, to_y, across = jnp.split(partial, 4, axis=0)
        mid = mine.shape[0] // 2
        across = across.astype(low)
        return mine, to_x, to_y, swap(across[:mid], 2), swap(across[mid:], 4)

    def scatter_end(parts):
        if chips == 4:
            mine, to_x, to_y, from_x, from_y = parts
            mid = mine.shape[0] // 2
            to_x = jnp.concatenate([to_x[:mid], to_x[mid:] + from_y.astype(full)], axis=0)
            to_y = jnp.concatenate([to_y[:mid] + from_x.astype(full), to_y[mid:]], axis=0)
            came_x, came_y = swap(to_x.astype(low), 2), swap(to_y.astype(low), 4)
            return mine, came_x, came_y
        (partial,) = parts
        bits = devices // 2
        while bits > 1:
            rows = partial.shape[0] // 2
            partial = partial[:rows] + swap(partial[rows:].astype(low), bits).astype(full)
            bits = bits // 2
        return (partial,)

    def swap_cores(array, pieces):
        rows = array.shape[0] // pieces
        return [swap(array[at * rows : (at + 1) * rows], 1) for at in range(pieces)]

    def by_core(array):
        mine, other = one_of(array, core), one_of(array, 1 - core)
        return jnp.concatenate([mine, swap(other, 1)], axis=0)

    def by_token(rows):
        mine, other = rows[:tok_count], swap(rows[tok_count:], 1)
        return jnp.where(core == 0, jnp.stack([mine, other]), jnp.stack([other, mine]))[None]

    own_tokens = by_core(tokens[0])
    query_blocks = query_weight.reshape(shard_rows, chips, query_width).transpose(1, 0, 2)
    key_value = [
        jnp.repeat(a.reshape(shard_rows, KV_HEADS, HEAD_DIM).transpose(1, 0, 2), sharing, axis=0)
        for a in (key_weight, value_weight)
    ]
    mixer_blocks = jnp.concatenate([query_blocks] + key_value, axis=2)
    mixer_near = [one_of(mixer_blocks, me // 2 ^ j) for j in range(chips)]
    output_far = swap(output_weight, 1)
    own_tokens, output_far, *mixer_near = flow.until(own_tokens, output_far, *mixer_near)
    normed_own, inputs = norm_rows(mixer_gain, own_tokens)
    normed_own, gate_weight, up_weight = flow.until(normed_own, gate_weight, up_weight)
    normed_parts = gather_start(normed_own)
    mixer_near = [swap(piece, 2 * j) if j else piece for j, piece in enumerate(mixer_near)]

    feed_own = pick_blocks(me, side, gate_weight, up_weight, chips, range(1), False)[0]
    feed_away = pick_blocks(me, side, gate_weight, up_weight, chips, range(1, chips), True)
    feed_own, feed_away, *held = flow.until(feed_own, feed_away, *mixer_near, *normed_parts)
    mixer_near, normed_parts = jnp.stack(held[:chips]), held[chips:]
    held = flow.until(*swap_cores(mixer_near, 2), *gather_end(normed_parts))
    mixer_far, normed = joined(held[:2]), joined(held[2:])
    split = (chips + 1) // 2 + 1
    away = [swap(flow.after(feed_away[j - 1])[0], 2 * j) for j in range(1, chips)]
    (block_order,) = flow.after(block_order)
    info = positions(
        one_of(block_order[0], core), one_of(doc_ids[0], core), one_of(prefix_len[0], core), length
    )
    facts = jnp.stack(info).reshape(4, devices, tok_count)
    facts = jnp.stack([one_of(facts, me ^ p, 1) for p in range(devices)], axis=1)
    place, member, relative, limit = facts.reshape(4, length)
    rows = jnp.concatenate([jnp.stack([place, member, limit]), jnp.zeros((5, length), jnp.int32)])
    columns = jnp.stack([place, member], axis=1)
    angle = angles_for(relative)
    cosine, sine = jnp.cos(angle), jnp.sin(angle)
    cosine = jnp.concatenate([cosine] * 4, axis=1)
    sine = jnp.concatenate([-sine, sine, -sine, sine], axis=1)

    output_rows = both_cores(output_weight, output_far)
    mixer_columns = place_blocks(me, mixer_near, mixer_far)
    (normed,) = flow.after(normed)
    raw = product("rows", normed, mixer_columns, full)
    attended, query, kv, logs = attend(raw, cosine, sine, columns, rows)
    branch = product("rows", attended, output_rows, full)
    normed_other = swap_cores(normed, 2)
    held = flow.until(branch, *away, *normed_other)
    branch, away, normed_other = held[0], held[1:chips], joined(held[chips:])
    away = joined(away)
    other, away_far = swap_copies(away, 1), swap(away, 1)
    feed_own_far = swap(*flow.after(feed_own), 1)
    parts = flow.until(*scatter_end(scatter_start(flow.after(branch)[0])))
    normed_two_own, hidden = norm_rows(feed_gain, inputs, *parts)
    (normed_two_own,) = flow.until(normed_two_own)
    normed_two_parts = flow.until(*gather_start(normed_two_own))
    held = flow.until(other, away_far, feed_own_far, *gather_end(normed_two_parts))
    other, away_far, feed_own_far, normed_two = held[0], held[1], held[2], joined(held[3:])
    grad_rows = by_core(*flow.after(cotangent[0]))
    other_far, grad_rows = flow.until(swap(other, 1), grad_rows)
    (own, down_weight) = flow.after(grad_rows, down_weight)
    down_far = swap(down_weight, 1)
    cotangent_rows = (
        [own] + [swap(own, 2 * j) for j in range(1, chips)]
        if chips == 4
        else gather_end(gather_start(own))
    )
    normed_two_other = swap(flow.after(normed_two)[0], 1)
    feed_pieces = [([(0, None)], feed_own), ([(1, None)], feed_own_far)]
    for kind, array in enumerate((away, away_far, other, other_far)):
        feed_pieces.append(([(2 * j + kind % 2, kind // 2) for j in range(1, chips)], array))
    inner, both, feed_columns, normed_two_other, down_far, *held = flow.until(
        *feed_forward(me, side, normed_two, feed_pieces),
        normed_two_other,
        down_far,
        *cotangent_rows,
    )
    all_grad_rows = joined(held)
    down_all = both_cores(down_weight, down_far)

    down_partial = product("outer", inner, all_grad_rows, low).reshape(2, down_rows, width)
    came = swap_cores(one_of(down_partial, 1 - core), 2)
    grad_both, *came = flow.until(feed_backward(all_grad_rows, down_all, both), *came)
    mine = [
        lax.dynamic_slice_in_dim(
            down_partial.reshape(2 * down_rows, width),
            core * down_rows + piece * (down_rows // 2),
            down_rows // 2,
            0,
        )
        for piece in range(2)
    ]
    down_parts = flow.until(
        *[(x.astype(full) + y.astype(full)).astype(low) for x, y in zip(mine, came)]
    )
    for piece in range(2):
        chain.add(("down", piece), down_parts[piece])
    chain.step()

    (grad_both,) = flow.after(grad_both)
    grad_both_other = swap_cores(grad_both, 4)
    partial_two = product("transpose", grad_both, feed_columns, full)
    partial_two, *held = flow.until(partial_two, *grad_both_other)
    grad_both_other = joined(held)
    chain.step()
    parts = scatter_end(scatter_start(*flow.after(partial_two)))
    picks = range(0, devices, 2)
    pieces = outer_blocks(
        me, normed_two, *flow.after(grad_both), normed_two_other, grad_both_other, picks
    )
    grad_branch_own, grad_hidden, feed_part = norm_back(
        feed_gain, hidden, grad_rows, *flow.until(*parts)
    )
    pieces, *parts = flow.until(pieces, *gather_start(grad_branch_own))
    chain.add(("feed", 0), pieces[0])
    chain.step()
    (pieces,) = flow.after(pieces)
    pieces = [pieces[j] for j in range(chips)]
    grad_branch = joined(gather_end(flow.after(*parts)))
    output_partial = product("outer", attended, grad_branch, low)
    output_partial = output_partial.reshape(2, shard_rows, width)
    came = swap_cores(one_of(output_partial, 1 - core), 2)
    grad_attended = product("transpose", grad_branch, output_rows, low)
    grad_mixer = attend_back(query, kv, grad_attended, logs, cosine, sine, columns, rows)
    partial = product("transpose", grad_mixer, mixer_columns, full)
    grad_mixer_other = swap_cores(grad_mixer, 2)
    partial, grad_mixer, held, *came = flow.until(
        partial, grad_mixer, output_partial, *came, *grad_mixer_other
    )
    grad_mixer_other, came = joined(came[2:]), came[:2]
    output_part = (one_of(held, core).astype(full) + joined(came).astype(full)).astype(low)
    pieces = list(flow.until(*pieces))
    chain.add("output", output_part)
    chain.step()
    moved = {j: swap(flow.after(pieces[j])[0], 2 * j) for j in range(1, split)}
    mixer_pieces = outer_blocks(me, normed, *flow.after(grad_mixer), normed_other, grad_mixer_other, picks)
    mixer_pieces, *early = flow.until(mixer_pieces, *[moved[j] for j in range(1, split)])
    for j, piece in enumerate(early, 1):
        chain.add(("feed", j), piece)
    chain.step()
    parts = scatter_end(scatter_start(flow.after(partial)[0]))
    input_grad, _, mixer_part = norm_back(
        mixer_gain, inputs, flow.after(grad_hidden)[0], *flow.until(*parts)
    )
    (input_grad,) = flow.until(input_grad)
    chain.step()
    for _ in range(split - 3):
        chain.step()
    (mixer_pieces,) = flow.after(mixer_pieces)
    mixer_pieces = flow.until(
        *[swap(mixer_pieces[j], 2 * j) if j else mixer_pieces[j] for j in range(chips)]
    )
    chain.add("mixer", jnp.stack(mixer_pieces))
    chain.step()
    late = [swap(flow.after(pieces[j])[0], 2 * j) for j in range(split, chips)]
    down = product("rows", *flow.after(inner), down_all, full)
    down, *late = flow.until(down, *late)
    half = shard_rows // 2
    chain.add(("last", 0), *[piece[:half] for piece in late])
    chain.step()
    gains = jnp.concatenate([mixer_part, feed_part]).reshape(2, 8, width // 8)
    (gains,) = flow.after(gains)
    bits = 1
    while bits < devices:
        gains = gains + swap(gains, bits)
        bits = 2 * bits
    gains, *parts = flow.until(gains, *scatter_start(flow.after(down)[0]))
    chain.add(("last", 1), *[piece[half:] for piece in late], gains)
    chain.step()
    parts = flow.until(*scatter_end(flow.after(*parts)))
    layer_out = by_token((hidden + sum(part.astype(full) for part in parts)).astype(low))
    input_grad = by_token(input_grad)
    chain.finish()
    results = chain.results
    down_grad = jnp.concatenate([results["down", piece][0] for piece in range(2)], axis=0)
    down_grad = down_grad.astype(full)
    output_grad = results["output"][0].astype(full)
    done = [results["feed", j][0] for j in range(split)]
    done += [jnp.concatenate(both, axis=0) for both in zip(results["last", 0], results["last", 1])]
    if hidden_width % 128:
        stacked = jnp.stack(done)
        ordered = jnp.stack([one_of(stacked, me // 2 ^ j) for j in range(chips)])
        ordered = ordered.astype(full).reshape(chips, shard_rows, 2, hidden_width)
        gate_grad, up_grad = ordered.transpose(2, 1, 0, 3).reshape(2, shard_rows, -1)
    else:
        held = ()
        for j, piece in enumerate(done):
            held = spread(me, j, piece, chips, held)
        gate_grad, up_grad = held
    mixer_grads = results["mixer"][0]
    mixer_grads = jnp.stack([one_of(mixer_grads, me // 2 ^ j) for j in range(chips)])
    mixer_grads = mixer_grads.astype(full)
    query_grad = mixer_grads[:, :, :query_width].transpose(1, 0, 2).reshape(shard_rows, -1)
    shared = (
        mixer_grads[:, :, query_width:]
        .reshape(KV_HEADS, sharing, shard_rows, 2, HEAD_DIM)
        .sum(axis=1)
    )
    key_grad = shared[:, :, 0].transpose(1, 0, 2).reshape(shard_rows, -1)
    value_grad = shared[:, :, 1].transpose(1, 0, 2).reshape(shard_rows, -1)
    mixer_total, feed_total = results["last", 1][-1].reshape(2, width)
    return (
        layer_out,
        input_grad,
        mixer_total,
        query_grad,
        key_grad,
        value_grad,
        output_grad,
        feed_total,
        gate_grad,
        up_grad,
        down_grad,
    )


def solution(mesh):
    placed = (
        P("rep", None, "fsdp", None),
        P("rep", None, "fsdp", None),
        P(),
        P("fsdp", None),
        P("fsdp", None),
        P("fsdp", None),
        P("fsdp", None),
        P(),
        P("fsdp", None),
        P("fsdp", None),
        P("fsdp", None),
        P("rep", None, None),
        P("rep", None, None),
        P("rep", None, None),
    )
    return jax.shard_map(
        local,
        mesh=mesh,
        in_specs=placed,
        out_specs=(
            P("rep", None, "fsdp", None),
            P("rep", None, "fsdp", None),
            P(),
            P("fsdp", None),
            P("fsdp", None),
            P("fsdp", None),
            P("fsdp", None),
            P(),
            P("fsdp", None),
            P("fsdp", None),
            P("fsdp", None),
        ),
        check_vma=False,
    )
```

```python
import functools

import jax
import jax.numpy as jnp
from jax import lax
from jax.experimental import pallas as pl
from jax.experimental.pallas import tpu as pltpu
from jax.sharding import PartitionSpec as P

HEADS = 32
KV_HEADS = 4
HEAD_DIM = 64
MICRO = 2
SEGS = 3


epsilon = 1e-05
FREE = pl.CostEstimate(flops=0, transcendentals=0, bytes_accessed=0)


def positions(order_row, doc_row, prefix_row, length):
    count = order_row.shape[0]
    block_width = length // count
    index = jnp.arange(length, dtype=jnp.int32)
    slot = index // block_width
    block = jnp.sum(
        jnp.where(
            slot[:, None] == jnp.arange(count, dtype=jnp.int32)[None, :], order_row[None, :], 0
        ),
        axis=1,
        dtype=jnp.int32,
    )
    place = block * block_width + index % block_width
    labels = jnp.arange(SEGS, dtype=jnp.int32)
    starts = jnp.sum(
        (doc_row[None, :] < labels[:, None]).astype(jnp.int32), axis=1, dtype=jnp.int32
    )
    member = jnp.sum(
        (place[:, None] >= starts[None, 1:]).astype(jnp.int32), axis=1, dtype=jnp.int32
    )
    picked = member[:, None] == labels[None, :]
    start_of = jnp.sum(jnp.where(picked, starts[None, :], 0), axis=1, dtype=jnp.int32)
    limit = jnp.sum(
        jnp.where(picked, starts[None, :] + prefix_row[None, :], 0), axis=1, dtype=jnp.int32
    )
    return (place, member, place - start_of, limit)


def angles_for(relative):
    halfway = HEAD_DIM // 2
    frequency = 10000.0 ** (-(2.0 * jnp.arange(halfway, dtype=jnp.float32)) / HEAD_DIM)
    return relative.astype(jnp.float32)[:, None] * frequency[None, :]


def rms_scale(values, gain):
    return values * lax.rsqrt(jnp.mean(values * values, axis=1, keepdims=True) + epsilon) * gain


def gated(gate_part, up_part):
    return jax.nn.silu(gate_part) * up_part


def contract_rows(left, right):
    return lax.dot_general(
        left, right, (((0,), (0,)), ((), ())), preferred_element_type=jnp.float32
    )


def times_transpose(left, right):
    return lax.dot_general(
        left, right, (((1,), (1,)), ((), ())), preferred_element_type=jnp.float32
    )


def dot_rows(left, right):
    return jnp.dot(left, right, preferred_element_type=jnp.float32)


def turn(field, cosine, sine):
    lane = lax.broadcasted_iota(jnp.int32, field.shape, 1) % HEAD_DIM
    half = HEAD_DIM // 2
    swapped = jnp.where(
        lane < half, pltpu.roll(field, 2 * HEAD_DIM - half, 1), pltpu.roll(field, half, 1)
    )
    return field * cosine + swapped * sine


def seen(columns, rows):
    place_q, member_q = columns[:, 0:1], columns[:, 1:2]
    place_k, member_k, limit_k = rows[0:1, :], rows[1:2, :], rows[2:3, :]
    return (member_q == member_k) & ((place_k <= place_q) | (place_k < limit_k))


def attend_kernel(raw_ref, cos_ref, sin_ref, column_ref, row_ref, out_ref, query_ref, kv_ref, log_ref):
    scale = HEAD_DIM ** (-0.5)
    cosine, sine = cos_ref[...], sin_ref[...]
    visible = seen(column_ref[...], row_ref[...])
    wide = 2 * HEAD_DIM
    pair_count = raw_ref.shape[1] // wide - 1
    first = lax.broadcasted_iota(jnp.int32, cosine.shape, 1) < HEAD_DIM
    kv = raw_ref[:, pair_count * wide :]
    keys_values = jnp.where(first, turn(kv, cosine, sine), kv)
    swapped = pltpu.roll(keys_values, HEAD_DIM, 1)
    keys = jnp.where(first, keys_values, swapped).astype(jnp.bfloat16)
    values = jnp.where(first, swapped, keys_values).astype(jnp.bfloat16)
    kv_ref[...] = keys_values.astype(jnp.bfloat16)
    logs = jnp.zeros(cosine.shape, jnp.float32)
    lanes = lax.broadcasted_iota(jnp.int32, cosine.shape, 1)
    for pair in range(pair_count):
        at = slice(pair * wide, (pair + 1) * wide)
        query = turn(raw_ref[:, at], cosine, sine).astype(jnp.bfloat16)
        query_ref[:, at] = query
        results = []
        for member in range(2):
            chosen = first if member == 0 else jnp.logical_not(first)
            one = jnp.where(chosen, query, jnp.zeros_like(query))
            scores = (
                lax.dot_general(
                    one, keys, (((1,), (1,)), ((), ())), preferred_element_type=jnp.float32
                )
                * scale
            )
            scores = jnp.where(visible, scores, -1000000000.0)
            peak = jnp.max(scores, axis=1, keepdims=True)
            raised = jnp.exp(scores - peak)
            totals = jnp.sum(raised, axis=1, keepdims=True)
            probs = (raised * (1.0 / totals)).astype(jnp.bfloat16)
            results.append(dot_rows(probs, values))
            logs = jnp.where(lanes == 2 * pair + member, peak + jnp.log(totals), logs)
        out_ref[:, at] = jnp.where(first, results[0], results[1]).astype(jnp.bfloat16)
    log_ref[...] = logs


def attend_back_kernel(
    query_ref, kv_ref, grad_ref, log_ref, cos_ref, sin_ref, column_ref, row_ref, out_ref
):
    scale = HEAD_DIM ** (-0.5)
    cosine, sine = cos_ref[...], sin_ref[...]
    visible = seen(column_ref[...], row_ref[...])
    wide = 2 * HEAD_DIM
    pair_count = query_ref.shape[1] // wide
    first = lax.broadcasted_iota(jnp.int32, cosine.shape, 1) < HEAD_DIM
    lanes = lax.broadcasted_iota(jnp.int32, cosine.shape, 1)
    keys_values = kv_ref[...]
    swapped = pltpu.roll(keys_values.astype(jnp.float32), HEAD_DIM, 1).astype(jnp.bfloat16)
    keys = jnp.where(first, keys_values, swapped)
    values = jnp.where(first, swapped, keys_values)
    logs = log_ref[...]
    grad_keys = jnp.zeros(cosine.shape, jnp.float32)
    grad_values = jnp.zeros(cosine.shape, jnp.float32)
    for pair in range(pair_count):
        at = slice(pair * wide, (pair + 1) * wide)
        query, grad = query_ref[:, at], grad_ref[:, at]
        results = []
        for member in range(2):
            chosen = first if member == 0 else jnp.logical_not(first)
            one = jnp.where(chosen, query, jnp.zeros_like(query))
            grad_one = jnp.where(chosen, grad, jnp.zeros_like(grad))
            log_one = jnp.sum(
                jnp.where(lanes == 2 * pair + member, logs, 0.0), axis=1, keepdims=True
            )
            scores = (
                lax.dot_general(
                    one, keys, (((1,), (1,)), ((), ())), preferred_element_type=jnp.float32
                )
                * scale
            )
            probs = jnp.exp(jnp.where(visible, scores, -1000000000.0) - log_one)
            grad_probs = lax.dot_general(
                grad_one, values, (((1,), (1,)), ((), ())), preferred_element_type=jnp.float32
            )
            inner_sum = jnp.sum(probs * grad_probs, axis=1, keepdims=True)
            grad_scores = (probs * (grad_probs - inner_sum)).astype(jnp.bfloat16)
            results.append(dot_rows(grad_scores, keys) * scale)
            grad_keys = grad_keys + contract_rows(grad_scores, one)
            grad_values = grad_values + contract_rows(probs.astype(jnp.bfloat16), grad_one)
        joined = jnp.where(first, results[0], results[1])
        out_ref[:, at] = turn(joined, cosine, -sine).astype(jnp.bfloat16)
    grad_keys = (grad_keys + pltpu.roll(grad_keys, HEAD_DIM, 1)) * scale
    grad_values = grad_values + pltpu.roll(grad_values, HEAD_DIM, 1)
    last = jnp.where(first, turn(grad_keys, cosine, -sine), grad_values)
    out_ref[:, pair_count * wide :] = last.astype(jnp.bfloat16)


def whole(*_):
    return (0, 0)


def whole_specs(arrays):
    return [pl.BlockSpec(a.shape, whole) for a in arrays]


def attend(raw, cosine, sine, columns, rows):
    length, wide = raw.shape
    query_width = wide - 2 * HEAD_DIM
    heads = query_width // HEAD_DIM
    outs = [
        jax.ShapeDtypeStruct((length, query_width), jnp.bfloat16),
        jax.ShapeDtypeStruct((length, query_width), jnp.bfloat16),
        jax.ShapeDtypeStruct((length, 2 * HEAD_DIM), jnp.bfloat16),
        jax.ShapeDtypeStruct((length, 2 * HEAD_DIM), jnp.float32),
    ]
    args = (raw, cosine, sine, columns, rows)
    return pl.pallas_call(
        attend_kernel,
        grid=(1,),
        in_specs=whole_specs(args),
        out_specs=whole_specs(outs),
        out_shape=outs,
        compiler_params=pltpu.CompilerParams(vmem_limit_bytes=48 * 1024 * 1024),
        cost_estimate=FREE,
        name="attend",
    )(*args)


def attend_back(query, kv, grad, logs, cosine, sine, columns, rows):
    length, query_width = query.shape
    heads = query_width // HEAD_DIM
    out = jax.ShapeDtypeStruct((length, query_width + 2 * HEAD_DIM), jnp.bfloat16)
    args = (query, kv, grad, logs, cosine, sine, columns, rows)
    return pl.pallas_call(
        attend_back_kernel,
        grid=(1,),
        in_specs=whole_specs(args),
        out_specs=pl.BlockSpec(out.shape, whole),
        out_shape=out,
        compiler_params=pltpu.CompilerParams(vmem_limit_bytes=48 * 1024 * 1024),
        cost_estimate=FREE,
        name="attend_back",
    )(*args)


def total_of(refs):
    total = refs[0][...].astype(jnp.float32)
    for ref in refs[1:]:
        total = total + ref[...].astype(jnp.float32)
    return total


def norm_kernel(gain_ref, *refs):
    low_ref, full_ref = refs[-2:]
    rows = total_of(refs[:-2])
    scale = lax.rsqrt(jnp.mean(rows * rows, axis=1, keepdims=True) + epsilon)
    full_ref[...] = rows
    low_ref[...] = (rows * scale * gain_ref[...].astype(jnp.float32)).astype(low_ref.dtype)


def norm_rows(gain, *parts):
    shape = parts[0].shape
    args = (gain.reshape(1, -1),) + parts
    outs = [jax.ShapeDtypeStruct(shape, jnp.bfloat16), jax.ShapeDtypeStruct(shape, jnp.float32)]
    return pl.pallas_call(
        norm_kernel,
        grid=(1,),
        in_specs=whole_specs(args),
        out_specs=whole_specs(outs),
        out_shape=outs,
        compiler_params=pltpu.CompilerParams(vmem_limit_bytes=32 * 1024 * 1024),
        cost_estimate=FREE,
        name="norm_rows",
    )(*args)


def norm_back_kernel(gain_ref, rows_ref, base_ref, *refs):
    low_ref, full_ref, gain_grad_ref = refs[-3:]
    rows, grad = rows_ref[...], total_of(refs[:-3])
    scale = lax.rsqrt(jnp.mean(rows * rows, axis=1, keepdims=True) + epsilon)
    gain_grad_ref[...] = jnp.sum(grad * rows * scale, axis=0, keepdims=True)
    inside = grad * gain_ref[...].astype(jnp.float32)
    slope = jnp.mean(inside * rows, axis=1, keepdims=True)
    result = base_ref[...].astype(jnp.float32) + scale * inside - rows * (scale**3 * slope)
    full_ref[...] = result
    low_ref[...] = result.astype(low_ref.dtype)


def norm_back(gain, rows, base, *parts):
    shape = rows.shape
    args = (gain.reshape(1, -1), rows, base) + parts
    outs = [
        jax.ShapeDtypeStruct(shape, jnp.bfloat16),
        jax.ShapeDtypeStruct(shape, jnp.float32),
        jax.ShapeDtypeStruct((1, shape[1]), jnp.float32),
    ]
    return pl.pallas_call(
        norm_back_kernel,
        grid=(1,),
        in_specs=whole_specs(args),
        out_specs=whole_specs(outs),
        out_shape=outs,
        compiler_params=pltpu.CompilerParams(vmem_limit_bytes=32 * 1024 * 1024),
        cost_estimate=FREE,
        name="norm_back",
    )(*args)


def pick_kernel(place_ref, gate_ref, up_ref, out_ref):
    for at in range(0, gate_ref.shape[1], 128):
        out_ref[0, :, 2 * at : 2 * at + 128] = gate_ref[:, at : at + 128]
        out_ref[0, :, 2 * at + 128 : 2 * at + 256] = up_ref[:, at : at + 128]


def pick_blocks(me, side, gate, up, chips, picks, halved):
    rows, total = gate.shape
    width = total // chips
    if halved:
        rows = rows // 2
    if width % 128:
        both = jnp.concatenate(
            [a.reshape(a.shape[0], chips, width).transpose(1, 0, 2) for a in (gate, up)], axis=2
        )
        if halved:
            both = lax.dynamic_slice_in_dim(both, side * rows, rows, 1)
        return jnp.stack(
            [lax.dynamic_index_in_dim(both, me // 2 ^ j, 0, keepdims=False) for j in picks]
        )
    first = picks[0]
    column = pl.BlockSpec(
        (rows, width), lambda s, place: (place[1] if halved else 0, place[0] // 2 ^ (s + first))
    )
    return pl.pallas_call(
        pick_kernel,
        grid_spec=pltpu.PrefetchScalarGridSpec(
            num_scalar_prefetch=1,
            grid=(len(picks),),
            in_specs=[column, column],
            out_specs=pl.BlockSpec((1, rows, 2 * width), lambda s, place: (s, 0, 0)),
        ),
        out_shape=jax.ShapeDtypeStruct((len(picks), rows, 2 * width), gate.dtype),
        compiler_params=pltpu.CompilerParams(vmem_limit_bytes=16 * 1024 * 1024),
        cost_estimate=FREE,
        name="pick_blocks",
    )(jnp.stack([me, side]), gate, up)


def tile_of(width):
    return 128 if width % 128 == 0 else width


def forward_kernel(place_ref, rows_ref, *refs, marks, shard):
    inner_ref, both_ref, weight_ref = refs[len(marks) :]
    for group, piece_ref in zip(marks, refs):
        count = piece_ref.shape[0] // len(group)
        for at, (p, flip) in enumerate(group):
            start = (place_ref[0] ^ p) * shard
            if flip is not None:
                start = start + (place_ref[1] ^ flip) * count
            weight_ref[pl.ds(pl.multiple_of(start, count), count), :] = piece_ref[
                at * count : (at + 1) * count, :
            ]
    both = dot_rows(rows_ref[...], weight_ref[...])
    half = both.shape[1] // 2
    gate, upward = both[:, :half], both[:, half:]
    both_ref[...] = both
    inner_ref[...] = (gate / (1.0 + jnp.exp(-gate)) * upward).astype(inner_ref.dtype)


def feed_forward(me, side, rows, pieces):
    count, width = rows.shape
    columns = pieces[0][1].shape[1]
    hidden = columns // 2
    tile = tile_of(hidden)
    marks = [mark for mark, _ in pieces]
    arrays = [piece for _, piece in pieces]
    outs = [
        jax.ShapeDtypeStruct((count, hidden), jnp.bfloat16),
        jax.ShapeDtypeStruct((count, columns), jnp.float32),
        jax.ShapeDtypeStruct((width, columns), jnp.bfloat16),
    ]
    return pl.pallas_call(
        functools.partial(
            forward_kernel, marks=marks, shard=width // lax.axis_size("fsdp")
        ),
        grid_spec=pltpu.PrefetchScalarGridSpec(
            num_scalar_prefetch=1,
            grid=(hidden // tile,),
            in_specs=[pl.BlockSpec((count, width), lambda s, place: (0, 0))]
            + [pl.BlockSpec((a.shape[0], 2 * tile), lambda s, place: (0, s)) for a in arrays],
            out_specs=[
                pl.BlockSpec((count, tile), lambda s, place: (0, s)),
                pl.BlockSpec((count, 2 * tile), lambda s, place: (0, s)),
                pl.BlockSpec((width, 2 * tile), lambda s, place: (0, s)),
            ],
        ),
        out_shape=outs,
        compiler_params=pltpu.CompilerParams(vmem_limit_bytes=48 * 1024 * 1024),
        cost_estimate=FREE,
        name="feed_forward",
    )(jnp.stack([me, side]), rows, *arrays)


def backward_kernel(grad_ref, weight_ref, both_ref, out_ref):
    grad = times_transpose(grad_ref[...], weight_ref[...])
    half = both_ref.shape[1] // 2
    gate, upward = both_ref[:, :half], both_ref[:, half:]
    sigmoid = 1.0 / (1.0 + jnp.exp(-gate))
    silu = gate * sigmoid
    out_ref[:, :half] = (
        grad * upward * (sigmoid + silu * (1.0 - sigmoid))
    ).astype(out_ref.dtype)
    out_ref[:, half:] = (grad * silu).astype(out_ref.dtype)


def feed_backward(grad_rows, weight, both):
    count, width = grad_rows.shape
    hidden = weight.shape[0]
    tile = tile_of(hidden)
    return pl.pallas_call(
        backward_kernel,
        grid=(hidden // tile,),
        in_specs=[
            pl.BlockSpec((count, width), lambda s: (0, 0)),
            pl.BlockSpec((tile, width), lambda s: (s, 0)),
            pl.BlockSpec((count, 2 * tile), lambda s: (0, s)),
        ],
        out_specs=pl.BlockSpec((count, 2 * tile), lambda s: (0, s)),
        out_shape=jax.ShapeDtypeStruct((count, 2 * hidden), jnp.bfloat16),
        compiler_params=pltpu.CompilerParams(vmem_limit_bytes=40 * 1024 * 1024),
        cost_estimate=FREE,
        name="feed_backward",
    )(grad_rows, weight, both)


def product_kernel(left_ref, right_ref, out_ref, *, kind):
    multiply = {"rows": dot_rows, "transpose": times_transpose, "outer": contract_rows}[kind]
    out_ref[...] = multiply(left_ref[...], right_ref[...]).astype(out_ref.dtype)


def product(kind, left, right, dtype):
    rows = left.shape[1 if kind == "outer" else 0]
    columns = right.shape[0 if kind == "transpose" else 1]
    tile = 256 if columns % 256 == 0 else 128
    right_spec = (
        pl.BlockSpec((tile, right.shape[1]), lambda s: (s, 0))
        if kind == "transpose"
        else pl.BlockSpec((right.shape[0], tile), lambda s: (0, s))
    )
    return pl.pallas_call(
        functools.partial(product_kernel, kind=kind),
        grid=(columns // tile,),
        in_specs=[pl.BlockSpec(left.shape, lambda s: (0, 0)), right_spec],
        out_specs=pl.BlockSpec((rows, tile), lambda s: (0, s)),
        out_shape=jax.ShapeDtypeStruct((rows, columns), dtype),
        compiler_params=pltpu.CompilerParams(vmem_limit_bytes=40 * 1024 * 1024),
        cost_estimate=FREE,
        name="product_" + kind,
    )(left, right)


def outer_kernel(place_ref, left_ref, right_ref, left_other_ref, right_other_ref, *out_refs):
    total = contract_rows(left_ref[...], right_ref[...])
    total = total + contract_rows(left_other_ref[...], right_other_ref[...])
    for at, out_ref in enumerate(out_refs):

        @pl.when(pl.program_id(0) == at)
        def _():
            out_ref[...] = total.astype(out_ref.dtype)


def outer_blocks(me, left, right, left_other, right_other, picks):
    tokens, width = right.shape
    rows = left.shape[1] // lax.axis_size("fsdp")
    first = picks[0]
    jump = picks[1] - first if len(picks) > 1 else 1
    column = pl.BlockSpec((tokens, rows), lambda s, place: (0, place[0] ^ (first + jump * s)))
    full = pl.BlockSpec((tokens, width), lambda s, place: (0, 0))
    block = pl.BlockSpec((rows, width), lambda s, place: (0, 0))
    return pl.pallas_call(
        outer_kernel,
        grid_spec=pltpu.PrefetchScalarGridSpec(
            num_scalar_prefetch=1,
            grid=(len(picks),),
            in_specs=[column, full, column, full],
            out_specs=[block] * len(picks),
        ),
        out_shape=[jax.ShapeDtypeStruct((rows, width), jnp.bfloat16)] * len(picks),
        compiler_params=pltpu.CompilerParams(vmem_limit_bytes=48 * 1024 * 1024),
        cost_estimate=FREE,
        name="outer_blocks",
    )(me.reshape(1), left, right, left_other, right_other)


def place_kernel(place_ref, near_ref, far_ref, out_ref):
    @pl.when(pl.program_id(1) == 0)
    def _():
        out_ref[...] = near_ref[...]

    @pl.when(pl.program_id(1) == 1)
    def _():
        out_ref[...] = far_ref[...]


def place_blocks(me, near, far):
    chips, rows, width = near.shape
    block = pl.BlockSpec((1, rows, width), lambda j, b, place: (j, 0, 0))
    return pl.pallas_call(
        place_kernel,
        grid_spec=pltpu.PrefetchScalarGridSpec(
            num_scalar_prefetch=1,
            grid=(chips, 2),
            in_specs=[block, block],
            out_specs=pl.BlockSpec(
                (1, rows, width), lambda j, b, place: (place[0] ^ (2 * j + b), 0, 0)
            ),
        ),
        out_shape=jax.ShapeDtypeStruct((2 * chips, rows, width), near.dtype),
        compiler_params=pltpu.CompilerParams(vmem_limit_bytes=16 * 1024 * 1024),
        cost_estimate=FREE,
        name="place_blocks",
    )(me.reshape(1), near, far).reshape(2 * chips * rows, width)


def spread_first(place_ref, piece_ref, gate_ref, up_ref):
    for at in range(0, gate_ref.shape[1], 128):
        gate_ref[:, at : at + 128] = piece_ref[:, 2 * at : 2 * at + 128].astype(jnp.float32)
        up_ref[:, at : at + 128] = piece_ref[:, 2 * at + 128 : 2 * at + 256].astype(jnp.float32)


def spread_next(place_ref, piece_ref, gate_in, up_in, gate_ref, up_ref):
    spread_first(place_ref, piece_ref, gate_ref, up_ref)


def spread(me, j, piece, chips, held):
    rows, both = piece.shape
    width = both // 2
    out = jax.ShapeDtypeStruct((rows, width * chips), jnp.float32)
    column = pl.BlockSpec((rows, width), lambda s, place: (0, place[0] // 2 ^ j))
    anywhere = pl.BlockSpec(memory_space=pl.ANY)
    return pl.pallas_call(
        spread_next if held else spread_first,
        grid_spec=pltpu.PrefetchScalarGridSpec(
            num_scalar_prefetch=1,
            grid=(1,),
            in_specs=[pl.BlockSpec((rows, both), lambda s, place: (0, 0))]
            + [anywhere] * len(held),
            out_specs=[column, column],
        ),
        out_shape=[out, out],
        input_output_aliases={2: 0, 3: 1} if held else {},
        compiler_params=pltpu.CompilerParams(vmem_limit_bytes=24 * 1024 * 1024),
        cost_estimate=FREE,
        name="spread",
    )(me.reshape(1), piece, *held)


class Flow:
    def __init__(self, token):
        self.token = token

    def after(self, *arrays):
        return lax.optimization_barrier((self.token,) + tuple(arrays))[1:]

    def until(self, *arrays):
        held = lax.optimization_barrier((self.token,) + tuple(arrays))
        self.token = held[0]
        return held[1:]


class Chain:
    def __init__(self, flow, copies, index):
        self.flow, self.copies, self.index = flow, copies, index
        half = copies // 2
        ends = [(s, copies - 1 - s) for s in range(half - 1)]
        self.stages = [([(a, a + 1), (b, b - 1)], None) for a, b in ends]
        self.stages.append(([(half - 1, half), (half, half - 1)], None))
        self.stages += [([(a + 1, a), (b - 1, b)], (a, b)) for a, b in reversed(ends)]
        self.waiting, self.moving, self.results = [], [], {}

    def add(self, name, *parts):
        self.waiting.append((name, parts))

    def start(self, parts, stage):
        return [lax.ppermute(part, "rep", self.stages[stage][0]) for part in parts]

    def step(self):
        moving, self.moving = self.moving, []
        if self.waiting:
            name, parts = self.waiting.pop(0)
            parts = self.flow.after(*parts)
            self.moving.append((name, parts, self.start(parts, 0), 0))
        if not moving:
            return
        arrived = iter(self.flow.until(*[array for item in moving for array in item[2]]))
        summed = []
        for name, parts, came, stage in moving:
            came = [next(arrived) for _ in came]
            outer = self.stages[stage][1]
            if outer is None:
                parts = [
                    (a.astype(jnp.float32) + b.astype(jnp.float32)).astype(a.dtype)
                    for a, b in zip(parts, came)
                ]
            else:
                here = (self.index == outer[0]) | (self.index == outer[1])
                parts = [jnp.where(here, b, a) for a, b in zip(parts, came)]
            if stage + 1 == len(self.stages):
                self.results[name] = parts
            else:
                summed.append((name, parts, stage + 1))
        for name, parts, stage in summed:
            self.moving.append((name, parts, self.start(parts, stage), stage))

    def finish(self):
        while self.waiting or self.moving:
            self.step()


def local(
    tokens,
    cotangent,
    mixer_gain,
    query_weight,
    key_weight,
    value_weight,
    output_weight,
    feed_gain,
    gate_weight,
    up_weight,
    down_weight,
    doc_ids,
    prefix_len,
    block_order,
):
    tok_count, width = tokens.shape[2:]
    devices = lax.axis_size("fsdp")
    chips = devices // 2
    copies = lax.axis_size("rep")
    me = lax.axis_index("fsdp")
    core = me % 2
    copy_index = lax.axis_index("rep")
    side = copy_index % 2
    length = tok_count * devices
    shard_rows = width // devices
    half_shard = shard_rows // 2
    query_width = HEADS // chips * HEAD_DIM
    sharing = max(1, chips // KV_HEADS)
    down_rows = down_weight.shape[0]
    hidden_width = 2 * down_rows
    low = jnp.bfloat16
    full = jnp.float32
    flow = Flow(jnp.zeros((8, 128), full) + copy_index.astype(full))
    chain = Chain(flow, copies, copy_index)

    def swap(array, bits):
        return lax.ppermute(array, "fsdp", [(d, d ^ bits) for d in range(devices)])

    def swap_copies(array, bits):
        return lax.ppermute(array, "rep", [(d, d ^ bits) for d in range(copies)])

    def one_of(array, index, axis=0):
        return lax.dynamic_index_in_dim(array, index, axis, keepdims=False)

    def both_cores(mine, other):
        return place_blocks(core, mine[None], other[None])

    def gather_start(own):
        return (own, swap(own, 2), swap(own, 4)) if chips == 4 else (own,)

    def gather_end(parts):
        if chips == 4:
            own, along_x, along_y = parts
            mid = own.shape[0] // 2
            return [own, along_x, along_y, swap(along_y[:mid], 2), swap(along_x[mid:], 4)]
        (own,) = parts
        bits = 2
        while bits < devices:
            own = jnp.concatenate([own, swap(own, bits)], axis=0)
            bits = 2 * bits
        return [own]

    def joined(parts):
        return jnp.concatenate(parts, axis=0) if len(parts) > 1 else parts[0]

    def scatter_start(partial):
        if chips != 4:
            return (partial,)
        mine, to_x, to_y, across = jnp.split(partial, 4, axis=0)
        mid = mine.shape[0] // 2
        across = across.astype(low)
        return mine, to_x, to_y, swap(across[:mid], 2), swap(across[mid:], 4)

    def scatter_end(parts):
        if chips == 4:
            mine, to_x, to_y, from_x, from_y = parts
            mid = mine.shape[0] // 2
            to_x = jnp.concatenate([to_x[:mid], to_x[mid:] + from_y.astype(full)], axis=0)
            to_y = jnp.concatenate([to_y[:mid] + from_x.astype(full), to_y[mid:]], axis=0)
            came_x, came_y = swap(to_x.astype(low), 2), swap(to_y.astype(low), 4)
            return mine, came_x, came_y
        (partial,) = parts
        bits = devices // 2
        while bits > 1:
            rows = partial.shape[0] // 2
            partial = partial[:rows] + swap(partial[rows:].astype(low), bits).astype(full)
            bits = bits // 2
        return (partial,)

    def swap_cores(array, pieces):
        rows = array.shape[0] // pieces
        return [swap(array[at * rows : (at + 1) * rows], 1) for at in range(pieces)]

    def by_core(array):
        mine, other = one_of(array, core), one_of(array, 1 - core)
        return jnp.concatenate([mine, swap(other, 1)], axis=0)

    def by_token(rows):
        mine, other = rows[:tok_count], swap(rows[tok_count:], 1)
        return jnp.where(core == 0, jnp.stack([mine, other]), jnp.stack([other, mine]))[None]

    own_tokens = by_core(tokens[0])
    query_blocks = query_weight.reshape(shard_rows, chips, query_width).transpose(1, 0, 2)
    key_value = [
        jnp.repeat(a.reshape(shard_rows, KV_HEADS, HEAD_DIM).transpose(1, 0, 2), sharing, axis=0)
        for a in (key_weight, value_weight)
    ]
    mixer_blocks = jnp.concatenate([query_blocks] + key_value, axis=2)
    mixer_near = [one_of(mixer_blocks, me // 2 ^ j) for j in range(chips)]
    output_far = swap(output_weight, 1)
    own_tokens, output_far, *mixer_near = flow.until(own_tokens, output_far, *mixer_near)
    normed_own, inputs = norm_rows(mixer_gain, own_tokens)
    normed_own, gate_weight, up_weight = flow.until(normed_own, gate_weight, up_weight)
    normed_parts = gather_start(normed_own)
    mixer_near = [swap(piece, 2 * j) if j else piece for j, piece in enumerate(mixer_near)]

    feed_own = pick_blocks(me, side, gate_weight, up_weight, chips, range(1), False)[0]
    feed_away = pick_blocks(me, side, gate_weight, up_weight, chips, range(1, chips), True)
    feed_own, feed_away, *held = flow.until(feed_own, feed_away, *mixer_near, *normed_parts)
    mixer_near, normed_parts = jnp.stack(held[:chips]), held[chips:]
    held = flow.until(*swap_cores(mixer_near, 2), *gather_end(normed_parts))
    mixer_far, normed = joined(held[:2]), joined(held[2:])
    split = (chips + 1) // 2 + 1
    away = [swap(flow.after(feed_away[j - 1])[0], 2 * j) for j in range(1, chips)]
    (block_order,) = flow.after(block_order)
    info = positions(
        one_of(block_order[0], core), one_of(doc_ids[0], core), one_of(prefix_len[0], core), length
    )
    facts = jnp.stack(info).reshape(4, devices, tok_count)
    facts = jnp.stack([one_of(facts, me ^ p, 1) for p in range(devices)], axis=1)
    place, member, relative, limit = facts.reshape(4, length)
    rows = jnp.concatenate([jnp.stack([place, member, limit]), jnp.zeros((5, length), jnp.int32)])
    columns = jnp.stack([place, member], axis=1)
    angle = angles_for(relative)
    cosine, sine = jnp.cos(angle), jnp.sin(angle)
    cosine = jnp.concatenate([cosine] * 4, axis=1)
    sine = jnp.concatenate([-sine, sine, -sine, sine], axis=1)

    output_rows = both_cores(output_weight, output_far)
    mixer_columns = place_blocks(me, mixer_near, mixer_far)
    (normed,) = flow.after(normed)
    raw = product("rows", normed, mixer_columns, full)
    attended, query, kv, logs = attend(raw, cosine, sine, columns, rows)
    branch = product("rows", attended, output_rows, full)
    normed_other = swap_cores(normed, 2)
    held = flow.until(branch, *away, *normed_other)
    branch, away, normed_other = held[0], held[1:chips], joined(held[chips:])
    away = joined(away)
    other, away_far = swap_copies(away, 1), swap(away, 1)
    feed_own_far = swap(*flow.after(feed_own), 1)
    parts = flow.until(*scatter_end(scatter_start(flow.after(branch)[0])))
    normed_two_own, hidden = norm_rows(feed_gain, inputs, *parts)
    (normed_two_own,) = flow.until(normed_two_own)
    normed_two_parts = flow.until(*gather_start(normed_two_own))
    held = flow.until(other, away_far, feed_own_far, *gather_end(normed_two_parts))
    other, away_far, feed_own_far, normed_two = held[0], held[1], held[2], joined(held[3:])
    grad_rows = by_core(*flow.after(cotangent[0]))
    other_far, grad_rows = flow.until(swap(other, 1), grad_rows)
    (own, down_weight) = flow.after(grad_rows, down_weight)
    down_far = swap(down_weight, 1)
    cotangent_rows = (
        [own] + [swap(own, 2 * j) for j in range(1, chips)]
        if chips == 4
        else gather_end(gather_start(own))
    )
    normed_two_other = swap(flow.after(normed_two)[0], 1)
    feed_pieces = [([(0, None)], feed_own), ([(1, None)], feed_own_far)]
    for kind, array in enumerate((away, away_far, other, other_far)):
        feed_pieces.append(([(2 * j + kind % 2, kind // 2) for j in range(1, chips)], array))
    inner, both, feed_columns, normed_two_other, down_far, *held = flow.until(
        *feed_forward(me, side, normed_two, feed_pieces),
        normed_two_other,
        down_far,
        *cotangent_rows,
    )
    all_grad_rows = joined(held)
    down_all = both_cores(down_weight, down_far)

    down_partial = product("outer", inner, all_grad_rows, low).reshape(2, down_rows, width)
    came = swap_cores(one_of(down_partial, 1 - core), 2)
    grad_both, *came = flow.until(feed_backward(all_grad_rows, down_all, both), *came)
    mine = [
        lax.dynamic_slice_in_dim(
            down_partial.reshape(2 * down_rows, width),
            core * down_rows + piece * (down_rows // 2),
            down_rows // 2,
            0,
        )
        for piece in range(2)
    ]
    down_parts = flow.until(
        *[(x.astype(full) + y.astype(full)).astype(low) for x, y in zip(mine, came)]
    )
    for piece in range(2):
        chain.add(("down", piece), down_parts[piece])
    chain.step()

    (grad_both,) = flow.after(grad_both)
    grad_both_other = swap_cores(grad_both, 4)
    partial_two = product("transpose", grad_both, feed_columns, full)
    partial_two, *held = flow.until(partial_two, *grad_both_other)
    grad_both_other = joined(held)
    chain.step()
    parts = scatter_end(scatter_start(*flow.after(partial_two)))
    picks = range(0, devices, 2)
    pieces = outer_blocks(
        me, normed_two, *flow.after(grad_both), normed_two_other, grad_both_other, picks
    )
    grad_branch_own, grad_hidden, feed_part = norm_back(
        feed_gain, hidden, grad_rows, *flow.until(*parts)
    )
    held = flow.until(*pieces, *gather_start(grad_branch_own))
    pieces, parts = held[:chips], held[chips:]
    chain.add(("feed", 0), pieces[0])
    chain.step()
    grad_branch = joined(gather_end(flow.after(*parts)))
    output_partial = product("outer", attended, grad_branch, low)
    output_partial = output_partial.reshape(2, shard_rows, width)
    came = swap_cores(one_of(output_partial, 1 - core), 2)
    grad_attended = product("transpose", grad_branch, output_rows, low)
    grad_mixer = attend_back(query, kv, grad_attended, logs, cosine, sine, columns, rows)
    partial = product("transpose", grad_mixer, mixer_columns, full)
    grad_mixer_other = swap_cores(grad_mixer, 2)
    partial, grad_mixer, held, *came = flow.until(
        partial, grad_mixer, output_partial, *came, *grad_mixer_other
    )
    grad_mixer_other, came = joined(came[2:]), came[:2]
    output_part = (one_of(held, core).astype(full) + joined(came).astype(full)).astype(low)
    chain.add("output", output_part)
    chain.step()
    moved = {j: swap(flow.after(pieces[j])[0], 2 * j) for j in range(1, split)}
    mixer_pieces = outer_blocks(
        me, normed, *flow.after(grad_mixer), normed_other, grad_mixer_other, picks
    )
    held = flow.until(*mixer_pieces, *[moved[j] for j in range(1, split)])
    mixer_pieces, early = held[:chips], held[chips:]
    for j, piece in enumerate(early, 1):
        chain.add(("feed", j), piece)
    chain.step()
    parts = scatter_end(scatter_start(flow.after(partial)[0]))
    input_grad, _, mixer_part = norm_back(
        mixer_gain, inputs, flow.after(grad_hidden)[0], *flow.until(*parts)
    )
    (input_grad,) = flow.until(input_grad)
    chain.step()
    for _ in range(split - 3):
        chain.step()
    gains = jnp.concatenate([mixer_part, feed_part]).reshape(2, 8, width // 8)
    gains, *mixer_pieces = flow.after(gains, *mixer_pieces)
    bits = 1
    while bits < devices:
        gains = gains + swap(gains, bits)
        bits = 2 * bits
    gains, *mixer_pieces = flow.until(
        gains, *[swap(mixer_pieces[j], 2 * j) if j else mixer_pieces[j] for j in range(chips)]
    )
    chain.add("mixer", jnp.stack(mixer_pieces))
    chain.step()
    late = [swap(flow.after(pieces[j])[0], 2 * j) for j in range(split, chips)]
    down = product("rows", *flow.after(inner), down_all, full)
    down, *late = flow.until(down, *late)
    for j, piece in enumerate(late, split):
        chain.add(("feed", j), piece, *([gains] if j == chips - 1 else []))
    chain.step()
    for _ in range(chips - split - 1):
        chain.step()
    parts = flow.until(*scatter_start(flow.after(down)[0]))
    chain.step()
    parts = flow.until(*scatter_end(flow.after(*parts)))
    layer_out = by_token((hidden + sum(part.astype(full) for part in parts)).astype(low))
    input_grad = by_token(input_grad)
    chain.finish()
    results = chain.results
    down_grad = jnp.concatenate([results["down", piece][0] for piece in range(2)], axis=0)
    down_grad = down_grad.astype(full)
    output_grad = results["output"][0].astype(full)
    done = [results["feed", j][0] for j in range(chips)]
    if hidden_width % 128:
        stacked = jnp.stack(done)
        ordered = jnp.stack([one_of(stacked, me // 2 ^ j) for j in range(chips)])
        ordered = ordered.astype(full).reshape(chips, shard_rows, 2, hidden_width)
        gate_grad, up_grad = ordered.transpose(2, 1, 0, 3).reshape(2, shard_rows, -1)
    else:
        held = ()
        for j, piece in enumerate(done):
            held = spread(me, j, piece, chips, held)
        gate_grad, up_grad = held
    mixer_grads = results["mixer"][0]
    mixer_grads = jnp.stack([one_of(mixer_grads, me // 2 ^ j) for j in range(chips)])
    mixer_grads = mixer_grads.astype(full)
    query_grad = mixer_grads[:, :, :query_width].transpose(1, 0, 2).reshape(shard_rows, -1)
    shared = (
        mixer_grads[:, :, query_width:]
        .reshape(KV_HEADS, sharing, shard_rows, 2, HEAD_DIM)
        .sum(axis=1)
    )
    key_grad = shared[:, :, 0].transpose(1, 0, 2).reshape(shard_rows, -1)
    value_grad = shared[:, :, 1].transpose(1, 0, 2).reshape(shard_rows, -1)
    mixer_total, feed_total = results["feed", chips - 1][1].reshape(2, width)
    return (
        layer_out,
        input_grad,
        mixer_total,
        query_grad,
        key_grad,
        value_grad,
        output_grad,
        feed_total,
        gate_grad,
        up_grad,
        down_grad,
    )


def solution(mesh):
    placed = (
        P("rep", None, "fsdp", None),
        P("rep", None, "fsdp", None),
        P(),
        P("fsdp", None),
        P("fsdp", None),
        P("fsdp", None),
        P("fsdp", None),
        P(),
        P("fsdp", None),
        P("fsdp", None),
        P("fsdp", None),
        P("rep", None, None),
        P("rep", None, None),
        P("rep", None, None),
    )
    return jax.shard_map(
        local,
        mesh=mesh,
        in_specs=placed,
        out_specs=(
            P("rep", None, "fsdp", None),
            P("rep", None, "fsdp", None),
            P(),
            P("fsdp", None),
            P("fsdp", None),
            P("fsdp", None),
            P("fsdp", None),
            P(),
            P("fsdp", None),
            P("fsdp", None),
            P("fsdp", None),
        ),
        check_vma=False,
    )
```

```python
import functools

import jax
import jax.numpy as jnp
from jax import lax
from jax.experimental import pallas as pl
from jax.experimental.pallas import tpu as pltpu
from jax.sharding import PartitionSpec as P

HEADS = 32
KV_HEADS = 4
HEAD_DIM = 64
MICRO = 2
SEGS = 3


epsilon = 1e-05
FREE = pl.CostEstimate(flops=0, transcendentals=0, bytes_accessed=0)


def positions(order_row, doc_row, prefix_row, length):
    count = order_row.shape[0]
    block_width = length // count
    index = jnp.arange(length, dtype=jnp.int32)
    slot = index // block_width
    block = jnp.sum(
        jnp.where(
            slot[:, None] == jnp.arange(count, dtype=jnp.int32)[None, :], order_row[None, :], 0
        ),
        axis=1,
        dtype=jnp.int32,
    )
    place = block * block_width + index % block_width
    labels = jnp.arange(SEGS, dtype=jnp.int32)
    starts = jnp.sum(
        (doc_row[None, :] < labels[:, None]).astype(jnp.int32), axis=1, dtype=jnp.int32
    )
    member = jnp.sum(
        (place[:, None] >= starts[None, 1:]).astype(jnp.int32), axis=1, dtype=jnp.int32
    )
    picked = member[:, None] == labels[None, :]
    start_of = jnp.sum(jnp.where(picked, starts[None, :], 0), axis=1, dtype=jnp.int32)
    limit = jnp.sum(
        jnp.where(picked, starts[None, :] + prefix_row[None, :], 0), axis=1, dtype=jnp.int32
    )
    return (place, member, place - start_of, limit)


def angles_for(relative):
    halfway = HEAD_DIM // 2
    frequency = 10000.0 ** (-(2.0 * jnp.arange(halfway, dtype=jnp.float32)) / HEAD_DIM)
    return relative.astype(jnp.float32)[:, None] * frequency[None, :]


def rms_scale(values, gain):
    return values * lax.rsqrt(jnp.mean(values * values, axis=1, keepdims=True) + epsilon) * gain


def gated(gate_part, up_part):
    return jax.nn.silu(gate_part) * up_part


def contract_rows(left, right):
    return lax.dot_general(
        left, right, (((0,), (0,)), ((), ())), preferred_element_type=jnp.float32
    )


def times_transpose(left, right):
    return lax.dot_general(
        left, right, (((1,), (1,)), ((), ())), preferred_element_type=jnp.float32
    )


def dot_rows(left, right):
    return jnp.dot(left, right, preferred_element_type=jnp.float32)


def turn(field, cosine, sine):
    lane = lax.broadcasted_iota(jnp.int32, field.shape, 1) % HEAD_DIM
    half = HEAD_DIM // 2
    swapped = jnp.where(
        lane < half, pltpu.roll(field, 2 * HEAD_DIM - half, 1), pltpu.roll(field, half, 1)
    )
    return field * cosine + swapped * sine


def seen(columns, rows):
    place_q, member_q = columns[:, 0:1], columns[:, 1:2]
    place_k, member_k, limit_k = rows[0:1, :], rows[1:2, :], rows[2:3, :]
    return (member_q == member_k) & ((place_k <= place_q) | (place_k < limit_k))


def attend_kernel(raw_ref, cos_ref, sin_ref, column_ref, row_ref, out_ref, query_ref, kv_ref, log_ref):
    scale = HEAD_DIM ** (-0.5)
    cosine, sine = cos_ref[...], sin_ref[...]
    visible = seen(column_ref[...], row_ref[...])
    wide = 2 * HEAD_DIM
    pair_count = raw_ref.shape[1] // wide - 1
    first = lax.broadcasted_iota(jnp.int32, cosine.shape, 1) < HEAD_DIM
    kv = raw_ref[:, pair_count * wide :]
    keys_values = jnp.where(first, turn(kv, cosine, sine), kv)
    swapped = pltpu.roll(keys_values, HEAD_DIM, 1)
    keys = jnp.where(first, keys_values, swapped).astype(jnp.bfloat16)
    values = jnp.where(first, swapped, keys_values).astype(jnp.bfloat16)
    kv_ref[...] = keys_values.astype(jnp.bfloat16)
    logs = jnp.zeros(cosine.shape, jnp.float32)
    lanes = lax.broadcasted_iota(jnp.int32, cosine.shape, 1)
    for pair in range(pair_count):
        at = slice(pair * wide, (pair + 1) * wide)
        query = turn(raw_ref[:, at], cosine, sine).astype(jnp.bfloat16)
        query_ref[:, at] = query
        results = []
        for member in range(2):
            chosen = first if member == 0 else jnp.logical_not(first)
            one = jnp.where(chosen, query, jnp.zeros_like(query))
            scores = (
                lax.dot_general(
                    one, keys, (((1,), (1,)), ((), ())), preferred_element_type=jnp.float32
                )
                * scale
            )
            scores = jnp.where(visible, scores, -1000000000.0)
            peak = jnp.max(scores, axis=1, keepdims=True)
            raised = jnp.exp(scores - peak)
            totals = jnp.sum(raised, axis=1, keepdims=True)
            probs = (raised * (1.0 / totals)).astype(jnp.bfloat16)
            results.append(dot_rows(probs, values))
            logs = jnp.where(lanes == 2 * pair + member, peak + jnp.log(totals), logs)
        out_ref[:, at] = jnp.where(first, results[0], results[1]).astype(jnp.bfloat16)
    log_ref[...] = logs


def attend_back_kernel(
    query_ref, kv_ref, grad_ref, log_ref, cos_ref, sin_ref, column_ref, row_ref, out_ref
):
    scale = HEAD_DIM ** (-0.5)
    cosine, sine = cos_ref[...], sin_ref[...]
    visible = seen(column_ref[...], row_ref[...])
    wide = 2 * HEAD_DIM
    pair_count = query_ref.shape[1] // wide
    first = lax.broadcasted_iota(jnp.int32, cosine.shape, 1) < HEAD_DIM
    lanes = lax.broadcasted_iota(jnp.int32, cosine.shape, 1)
    keys_values = kv_ref[...]
    swapped = pltpu.roll(keys_values.astype(jnp.float32), HEAD_DIM, 1).astype(jnp.bfloat16)
    keys = jnp.where(first, keys_values, swapped)
    values = jnp.where(first, swapped, keys_values)
    logs = log_ref[...]
    grad_keys = jnp.zeros(cosine.shape, jnp.float32)
    grad_values = jnp.zeros(cosine.shape, jnp.float32)
    for pair in range(pair_count):
        at = slice(pair * wide, (pair + 1) * wide)
        query, grad = query_ref[:, at], grad_ref[:, at]
        results = []
        for member in range(2):
            chosen = first if member == 0 else jnp.logical_not(first)
            one = jnp.where(chosen, query, jnp.zeros_like(query))
            grad_one = jnp.where(chosen, grad, jnp.zeros_like(grad))
            log_one = jnp.sum(
                jnp.where(lanes == 2 * pair + member, logs, 0.0), axis=1, keepdims=True
            )
            scores = (
                lax.dot_general(
                    one, keys, (((1,), (1,)), ((), ())), preferred_element_type=jnp.float32
                )
                * scale
            )
            probs = jnp.exp(jnp.where(visible, scores, -1000000000.0) - log_one)
            grad_probs = lax.dot_general(
                grad_one, values, (((1,), (1,)), ((), ())), preferred_element_type=jnp.float32
            )
            inner_sum = jnp.sum(probs * grad_probs, axis=1, keepdims=True)
            grad_scores = (probs * (grad_probs - inner_sum)).astype(jnp.bfloat16)
            results.append(dot_rows(grad_scores, keys) * scale)
            grad_keys = grad_keys + contract_rows(grad_scores, one)
            grad_values = grad_values + contract_rows(probs.astype(jnp.bfloat16), grad_one)
        joined = jnp.where(first, results[0], results[1])
        out_ref[:, at] = turn(joined, cosine, -sine).astype(jnp.bfloat16)
    grad_keys = (grad_keys + pltpu.roll(grad_keys, HEAD_DIM, 1)) * scale
    grad_values = grad_values + pltpu.roll(grad_values, HEAD_DIM, 1)
    last = jnp.where(first, turn(grad_keys, cosine, -sine), grad_values)
    out_ref[:, pair_count * wide :] = last.astype(jnp.bfloat16)


def whole(*_):
    return (0, 0)


def whole_specs(arrays):
    return [pl.BlockSpec(a.shape, whole) for a in arrays]


def attend(raw, cosine, sine, columns, rows):
    length, wide = raw.shape
    query_width = wide - 2 * HEAD_DIM
    heads = query_width // HEAD_DIM
    outs = [
        jax.ShapeDtypeStruct((length, query_width), jnp.bfloat16),
        jax.ShapeDtypeStruct((length, query_width), jnp.bfloat16),
        jax.ShapeDtypeStruct((length, 2 * HEAD_DIM), jnp.bfloat16),
        jax.ShapeDtypeStruct((length, 2 * HEAD_DIM), jnp.float32),
    ]
    args = (raw, cosine, sine, columns, rows)
    return pl.pallas_call(
        attend_kernel,
        grid=(1,),
        in_specs=whole_specs(args),
        out_specs=whole_specs(outs),
        out_shape=outs,
        compiler_params=pltpu.CompilerParams(vmem_limit_bytes=48 * 1024 * 1024),
        cost_estimate=FREE,
        name="attend",
    )(*args)


def attend_back(query, kv, grad, logs, cosine, sine, columns, rows):
    length, query_width = query.shape
    heads = query_width // HEAD_DIM
    out = jax.ShapeDtypeStruct((length, query_width + 2 * HEAD_DIM), jnp.bfloat16)
    args = (query, kv, grad, logs, cosine, sine, columns, rows)
    return pl.pallas_call(
        attend_back_kernel,
        grid=(1,),
        in_specs=whole_specs(args),
        out_specs=pl.BlockSpec(out.shape, whole),
        out_shape=out,
        compiler_params=pltpu.CompilerParams(vmem_limit_bytes=48 * 1024 * 1024),
        cost_estimate=FREE,
        name="attend_back",
    )(*args)


def total_of(refs):
    total = refs[0][...].astype(jnp.float32)
    for ref in refs[1:]:
        total = total + ref[...].astype(jnp.float32)
    return total


def norm_kernel(gain_ref, *refs):
    low_ref, full_ref = refs[-2:]
    rows = total_of(refs[:-2])
    scale = lax.rsqrt(jnp.mean(rows * rows, axis=1, keepdims=True) + epsilon)
    full_ref[...] = rows
    low_ref[...] = (rows * scale * gain_ref[...].astype(jnp.float32)).astype(low_ref.dtype)


def norm_rows(gain, *parts):
    shape = parts[0].shape
    args = (gain.reshape(1, -1),) + parts
    outs = [jax.ShapeDtypeStruct(shape, jnp.bfloat16), jax.ShapeDtypeStruct(shape, jnp.float32)]
    return pl.pallas_call(
        norm_kernel,
        grid=(1,),
        in_specs=whole_specs(args),
        out_specs=whole_specs(outs),
        out_shape=outs,
        compiler_params=pltpu.CompilerParams(vmem_limit_bytes=32 * 1024 * 1024),
        cost_estimate=FREE,
        name="norm_rows",
    )(*args)


def norm_back_kernel(gain_ref, rows_ref, base_ref, *refs):
    low_ref, full_ref, gain_grad_ref = refs[-3:]
    rows, grad = rows_ref[...], total_of(refs[:-3])
    scale = lax.rsqrt(jnp.mean(rows * rows, axis=1, keepdims=True) + epsilon)
    gain_grad_ref[...] = jnp.sum(grad * rows * scale, axis=0, keepdims=True)
    inside = grad * gain_ref[...].astype(jnp.float32)
    slope = jnp.mean(inside * rows, axis=1, keepdims=True)
    result = base_ref[...].astype(jnp.float32) + scale * inside - rows * (scale**3 * slope)
    full_ref[...] = result
    low_ref[...] = result.astype(low_ref.dtype)


def norm_back(gain, rows, base, *parts):
    shape = rows.shape
    args = (gain.reshape(1, -1), rows, base) + parts
    outs = [
        jax.ShapeDtypeStruct(shape, jnp.bfloat16),
        jax.ShapeDtypeStruct(shape, jnp.float32),
        jax.ShapeDtypeStruct((1, shape[1]), jnp.float32),
    ]
    return pl.pallas_call(
        norm_back_kernel,
        grid=(1,),
        in_specs=whole_specs(args),
        out_specs=whole_specs(outs),
        out_shape=outs,
        compiler_params=pltpu.CompilerParams(vmem_limit_bytes=32 * 1024 * 1024),
        cost_estimate=FREE,
        name="norm_back",
    )(*args)


def pick_kernel(place_ref, gate_ref, up_ref, out_ref):
    for at in range(0, gate_ref.shape[1], 128):
        out_ref[0, :, 2 * at : 2 * at + 128] = gate_ref[:, at : at + 128]
        out_ref[0, :, 2 * at + 128 : 2 * at + 256] = up_ref[:, at : at + 128]


def pick_blocks(me, side, gate, up, chips, picks, halved):
    rows, total = gate.shape
    width = total // chips
    if halved:
        rows = rows // 2
    if width % 128:
        both = jnp.concatenate(
            [a.reshape(a.shape[0], chips, width).transpose(1, 0, 2) for a in (gate, up)], axis=2
        )
        if halved:
            both = lax.dynamic_slice_in_dim(both, side * rows, rows, 1)
        return jnp.stack(
            [lax.dynamic_index_in_dim(both, me // 2 ^ j, 0, keepdims=False) for j in picks]
        )
    first = picks[0]
    column = pl.BlockSpec(
        (rows, width), lambda s, place: (place[1] if halved else 0, place[0] // 2 ^ (s + first))
    )
    return pl.pallas_call(
        pick_kernel,
        grid_spec=pltpu.PrefetchScalarGridSpec(
            num_scalar_prefetch=1,
            grid=(len(picks),),
            in_specs=[column, column],
            out_specs=pl.BlockSpec((1, rows, 2 * width), lambda s, place: (s, 0, 0)),
        ),
        out_shape=jax.ShapeDtypeStruct((len(picks), rows, 2 * width), gate.dtype),
        compiler_params=pltpu.CompilerParams(vmem_limit_bytes=16 * 1024 * 1024),
        cost_estimate=FREE,
        name="pick_blocks",
    )(jnp.stack([me, side]), gate, up)


def tile_of(width):
    return 128 if width % 128 == 0 else width


def forward_kernel(place_ref, rows_ref, *refs, marks, shard):
    inner_ref, both_ref, weight_ref = refs[len(marks) :]
    for group, piece_ref in zip(marks, refs):
        count = piece_ref.shape[0] // len(group)
        for at, (p, flip) in enumerate(group):
            start = (place_ref[0] ^ p) * shard
            if flip is not None:
                start = start + (place_ref[1] ^ flip) * count
            weight_ref[pl.ds(pl.multiple_of(start, count), count), :] = piece_ref[
                at * count : (at + 1) * count, :
            ]
    both = dot_rows(rows_ref[...], weight_ref[...])
    half = both.shape[1] // 2
    gate, upward = both[:, :half], both[:, half:]
    both_ref[...] = both
    inner_ref[...] = (gate / (1.0 + jnp.exp(-gate)) * upward).astype(inner_ref.dtype)


def feed_forward(me, side, rows, pieces):
    count, width = rows.shape
    columns = pieces[0][1].shape[1]
    hidden = columns // 2
    tile = tile_of(hidden)
    marks = [mark for mark, _ in pieces]
    arrays = [piece for _, piece in pieces]
    outs = [
        jax.ShapeDtypeStruct((count, hidden), jnp.bfloat16),
        jax.ShapeDtypeStruct((count, columns), jnp.float32),
        jax.ShapeDtypeStruct((width, columns), jnp.bfloat16),
    ]
    return pl.pallas_call(
        functools.partial(
            forward_kernel, marks=marks, shard=width // lax.axis_size("fsdp")
        ),
        grid_spec=pltpu.PrefetchScalarGridSpec(
            num_scalar_prefetch=1,
            grid=(hidden // tile,),
            in_specs=[pl.BlockSpec((count, width), lambda s, place: (0, 0))]
            + [pl.BlockSpec((a.shape[0], 2 * tile), lambda s, place: (0, s)) for a in arrays],
            out_specs=[
                pl.BlockSpec((count, tile), lambda s, place: (0, s)),
                pl.BlockSpec((count, 2 * tile), lambda s, place: (0, s)),
                pl.BlockSpec((width, 2 * tile), lambda s, place: (0, s)),
            ],
        ),
        out_shape=outs,
        compiler_params=pltpu.CompilerParams(vmem_limit_bytes=48 * 1024 * 1024),
        cost_estimate=FREE,
        name="feed_forward",
    )(jnp.stack([me, side]), rows, *arrays)


def backward_kernel(grad_ref, weight_ref, both_ref, out_ref):
    grad = times_transpose(grad_ref[...], weight_ref[...])
    half = both_ref.shape[1] // 2
    gate, upward = both_ref[:, :half], both_ref[:, half:]
    sigmoid = 1.0 / (1.0 + jnp.exp(-gate))
    silu = gate * sigmoid
    out_ref[:, :half] = (
        grad * upward * (sigmoid + silu * (1.0 - sigmoid))
    ).astype(out_ref.dtype)
    out_ref[:, half:] = (grad * silu).astype(out_ref.dtype)


def feed_backward(grad_rows, weight, both):
    count, width = grad_rows.shape
    hidden = weight.shape[0]
    tile = tile_of(hidden)
    return pl.pallas_call(
        backward_kernel,
        grid=(hidden // tile,),
        in_specs=[
            pl.BlockSpec((count, width), lambda s: (0, 0)),
            pl.BlockSpec((tile, width), lambda s: (s, 0)),
            pl.BlockSpec((count, 2 * tile), lambda s: (0, s)),
        ],
        out_specs=pl.BlockSpec((count, 2 * tile), lambda s: (0, s)),
        out_shape=jax.ShapeDtypeStruct((count, 2 * hidden), jnp.bfloat16),
        compiler_params=pltpu.CompilerParams(vmem_limit_bytes=40 * 1024 * 1024),
        cost_estimate=FREE,
        name="feed_backward",
    )(grad_rows, weight, both)


def product_kernel(left_ref, right_ref, out_ref, *, kind):
    multiply = {"rows": dot_rows, "transpose": times_transpose, "outer": contract_rows}[kind]
    out_ref[...] = multiply(left_ref[...], right_ref[...]).astype(out_ref.dtype)


def product(kind, left, right, dtype):
    rows = left.shape[1 if kind == "outer" else 0]
    columns = right.shape[0 if kind == "transpose" else 1]
    tile = 256 if columns % 256 == 0 else 128
    right_spec = (
        pl.BlockSpec((tile, right.shape[1]), lambda s: (s, 0))
        if kind == "transpose"
        else pl.BlockSpec((right.shape[0], tile), lambda s: (0, s))
    )
    return pl.pallas_call(
        functools.partial(product_kernel, kind=kind),
        grid=(columns // tile,),
        in_specs=[pl.BlockSpec(left.shape, lambda s: (0, 0)), right_spec],
        out_specs=pl.BlockSpec((rows, tile), lambda s: (0, s)),
        out_shape=jax.ShapeDtypeStruct((rows, columns), dtype),
        compiler_params=pltpu.CompilerParams(vmem_limit_bytes=40 * 1024 * 1024),
        cost_estimate=FREE,
        name="product_" + kind,
    )(left, right)


def outer_kernel(place_ref, left_ref, right_ref, left_other_ref, right_other_ref, *out_refs):
    total = contract_rows(left_ref[...], right_ref[...])
    total = total + contract_rows(left_other_ref[...], right_other_ref[...])
    for at, out_ref in enumerate(out_refs):

        @pl.when(pl.program_id(0) == at)
        def _():
            out_ref[...] = total.astype(out_ref.dtype)


def outer_blocks(me, left, right, left_other, right_other, picks):
    tokens, width = right.shape
    rows = left.shape[1] // lax.axis_size("fsdp")
    first = picks[0]
    jump = picks[1] - first if len(picks) > 1 else 1
    column = pl.BlockSpec((tokens, rows), lambda s, place: (0, place[0] ^ (first + jump * s)))
    full = pl.BlockSpec((tokens, width), lambda s, place: (0, 0))
    block = pl.BlockSpec((rows, width), lambda s, place: (0, 0))
    return pl.pallas_call(
        outer_kernel,
        grid_spec=pltpu.PrefetchScalarGridSpec(
            num_scalar_prefetch=1,
            grid=(len(picks),),
            in_specs=[column, full, column, full],
            out_specs=[block] * len(picks),
        ),
        out_shape=[jax.ShapeDtypeStruct((rows, width), jnp.bfloat16)] * len(picks),
        compiler_params=pltpu.CompilerParams(vmem_limit_bytes=48 * 1024 * 1024),
        cost_estimate=FREE,
        name="outer_blocks",
    )(me.reshape(1), left, right, left_other, right_other)


def place_kernel(place_ref, near_ref, far_ref, out_ref):
    @pl.when(pl.program_id(1) == 0)
    def _():
        out_ref[...] = near_ref[...]

    @pl.when(pl.program_id(1) == 1)
    def _():
        out_ref[...] = far_ref[...]


def place_blocks(me, near, far):
    chips, rows, width = near.shape
    block = pl.BlockSpec((1, rows, width), lambda j, b, place: (j, 0, 0))
    return pl.pallas_call(
        place_kernel,
        grid_spec=pltpu.PrefetchScalarGridSpec(
            num_scalar_prefetch=1,
            grid=(chips, 2),
            in_specs=[block, block],
            out_specs=pl.BlockSpec(
                (1, rows, width), lambda j, b, place: (place[0] ^ (2 * j + b), 0, 0)
            ),
        ),
        out_shape=jax.ShapeDtypeStruct((2 * chips, rows, width), near.dtype),
        compiler_params=pltpu.CompilerParams(vmem_limit_bytes=16 * 1024 * 1024),
        cost_estimate=FREE,
        name="place_blocks",
    )(me.reshape(1), near, far).reshape(2 * chips * rows, width)


def spread_first(place_ref, piece_ref, gate_ref, up_ref):
    for at in range(0, gate_ref.shape[1], 128):
        gate_ref[:, at : at + 128] = piece_ref[:, 2 * at : 2 * at + 128].astype(jnp.float32)
        up_ref[:, at : at + 128] = piece_ref[:, 2 * at + 128 : 2 * at + 256].astype(jnp.float32)


def spread_next(place_ref, piece_ref, gate_in, up_in, gate_ref, up_ref):
    spread_first(place_ref, piece_ref, gate_ref, up_ref)


def spread(me, j, piece, chips, held):
    rows, both = piece.shape
    width = both // 2
    out = jax.ShapeDtypeStruct((rows, width * chips), jnp.float32)
    column = pl.BlockSpec((rows, width), lambda s, place: (0, place[0] // 2 ^ j))
    anywhere = pl.BlockSpec(memory_space=pl.ANY)
    return pl.pallas_call(
        spread_next if held else spread_first,
        grid_spec=pltpu.PrefetchScalarGridSpec(
            num_scalar_prefetch=1,
            grid=(1,),
            in_specs=[pl.BlockSpec((rows, both), lambda s, place: (0, 0))]
            + [anywhere] * len(held),
            out_specs=[column, column],
        ),
        out_shape=[out, out],
        input_output_aliases={2: 0, 3: 1} if held else {},
        compiler_params=pltpu.CompilerParams(vmem_limit_bytes=24 * 1024 * 1024),
        cost_estimate=FREE,
        name="spread",
    )(me.reshape(1), piece, *held)


class Flow:
    def __init__(self, token):
        self.token = token

    def after(self, *arrays):
        return lax.optimization_barrier((self.token,) + tuple(arrays))[1:]

    def until(self, *arrays):
        held = lax.optimization_barrier((self.token,) + tuple(arrays))
        self.token = held[0]
        return held[1:]


class Chain:
    def __init__(self, flow, copies, index):
        self.flow, self.copies, self.index = flow, copies, index
        half = copies // 2
        ends = [(s, copies - 1 - s) for s in range(half - 1)]
        self.stages = [([(a, a + 1), (b, b - 1)], None) for a, b in ends]
        self.stages.append(([(half - 1, half), (half, half - 1)], None))
        self.stages += [([(a + 1, a), (b - 1, b)], (a, b)) for a, b in reversed(ends)]
        self.waiting, self.moving, self.results = [], [], {}

    def add(self, name, *parts):
        self.waiting.append((name, parts))

    def start(self, parts, stage):
        return [lax.ppermute(part, "rep", self.stages[stage][0]) for part in parts]

    def step(self):
        moving, self.moving = self.moving, []
        if self.waiting:
            name, parts = self.waiting.pop(0)
            parts = self.flow.after(*parts)
            self.moving.append((name, parts, self.start(parts, 0), 0))
        if not moving:
            return
        arrived = iter(self.flow.until(*[array for item in moving for array in item[2]]))
        summed = []
        for name, parts, came, stage in moving:
            came = [next(arrived) for _ in came]
            outer = self.stages[stage][1]
            if outer is None:
                parts = [
                    (a.astype(jnp.float32) + b.astype(jnp.float32)).astype(a.dtype)
                    for a, b in zip(parts, came)
                ]
            else:
                here = (self.index == outer[0]) | (self.index == outer[1])
                parts = [jnp.where(here, b, a) for a, b in zip(parts, came)]
            if stage + 1 == len(self.stages):
                self.results[name] = parts
            else:
                summed.append((name, parts, stage + 1))
        for name, parts, stage in summed:
            self.moving.append((name, parts, self.start(parts, stage), stage))

    def finish(self):
        while self.waiting or self.moving:
            self.step()


def local(
    tokens,
    cotangent,
    mixer_gain,
    query_weight,
    key_weight,
    value_weight,
    output_weight,
    feed_gain,
    gate_weight,
    up_weight,
    down_weight,
    doc_ids,
    prefix_len,
    block_order,
):
    tok_count, width = tokens.shape[2:]
    devices = lax.axis_size("fsdp")
    chips = devices // 2
    copies = lax.axis_size("rep")
    me = lax.axis_index("fsdp")
    core = me % 2
    copy_index = lax.axis_index("rep")
    side = copy_index % 2
    length = tok_count * devices
    shard_rows = width // devices
    half_shard = shard_rows // 2
    query_width = HEADS // chips * HEAD_DIM
    sharing = max(1, chips // KV_HEADS)
    down_rows = down_weight.shape[0]
    hidden_width = 2 * down_rows
    low = jnp.bfloat16
    full = jnp.float32
    flow = Flow(jnp.zeros((8, 128), full) + copy_index.astype(full))
    chain = Chain(flow, copies, copy_index)

    def swap(array, bits):
        return lax.ppermute(array, "fsdp", [(d, d ^ bits) for d in range(devices)])

    def swap_copies(array, bits):
        return lax.ppermute(array, "rep", [(d, d ^ bits) for d in range(copies)])

    def one_of(array, index, axis=0):
        return lax.dynamic_index_in_dim(array, index, axis, keepdims=False)

    def both_cores(mine, other):
        return place_blocks(core, mine[None], other[None])

    def gather_start(own):
        return (own, swap(own, 2), swap(own, 4)) if chips == 4 else (own,)

    def gather_end(parts):
        if chips == 4:
            own, along_x, along_y = parts
            mid = own.shape[0] // 2
            return [own, along_x, along_y, swap(along_y[:mid], 2), swap(along_x[mid:], 4)]
        (own,) = parts
        bits = 2
        while bits < devices:
            own = jnp.concatenate([own, swap(own, bits)], axis=0)
            bits = 2 * bits
        return [own]

    def joined(parts):
        return jnp.concatenate(parts, axis=0) if len(parts) > 1 else parts[0]

    def scatter_start(partial):
        if chips != 4:
            return (partial,)
        mine, to_x, to_y, across = jnp.split(partial, 4, axis=0)
        mid = mine.shape[0] // 2
        across = across.astype(low)
        return mine, to_x, to_y, swap(across[:mid], 2), swap(across[mid:], 4)

    def scatter_end(parts):
        if chips == 4:
            mine, to_x, to_y, from_x, from_y = parts
            mid = mine.shape[0] // 2
            to_x = jnp.concatenate([to_x[:mid], to_x[mid:] + from_y.astype(full)], axis=0)
            to_y = jnp.concatenate([to_y[:mid] + from_x.astype(full), to_y[mid:]], axis=0)
            came_x, came_y = swap(to_x.astype(low), 2), swap(to_y.astype(low), 4)
            return mine, came_x, came_y
        (partial,) = parts
        bits = devices // 2
        while bits > 1:
            rows = partial.shape[0] // 2
            partial = partial[:rows] + swap(partial[rows:].astype(low), bits).astype(full)
            bits = bits // 2
        return (partial,)

    def swap_cores(array, pieces):
        rows = array.shape[0] // pieces
        return [swap(array[at * rows : (at + 1) * rows], 1) for at in range(pieces)]

    def by_core(array):
        mine, other = one_of(array, core), one_of(array, 1 - core)
        return jnp.concatenate([mine, swap(other, 1)], axis=0)

    def by_token(rows):
        mine, other = rows[:tok_count], swap(rows[tok_count:], 1)
        return jnp.where(core == 0, jnp.stack([mine, other]), jnp.stack([other, mine]))[None]

    own_tokens = by_core(tokens[0])
    query_blocks = query_weight.reshape(shard_rows, chips, query_width).transpose(1, 0, 2)
    key_value = [
        jnp.repeat(a.reshape(shard_rows, KV_HEADS, HEAD_DIM).transpose(1, 0, 2), sharing, axis=0)
        for a in (key_weight, value_weight)
    ]
    mixer_blocks = jnp.concatenate([query_blocks] + key_value, axis=2)
    mixer_near = [one_of(mixer_blocks, me // 2 ^ j) for j in range(chips)]
    output_far = swap(output_weight, 1)
    own_tokens, output_far, *mixer_near = flow.until(own_tokens, output_far, *mixer_near)
    normed_own, inputs = norm_rows(mixer_gain, own_tokens)
    normed_own, gate_weight, up_weight = flow.until(normed_own, gate_weight, up_weight)
    normed_parts = gather_start(normed_own)
    mixer_near = [swap(piece, 2 * j) if j else piece for j, piece in enumerate(mixer_near)]

    feed_own = pick_blocks(me, side, gate_weight, up_weight, chips, range(1), False)[0]
    feed_away = pick_blocks(me, side, gate_weight, up_weight, chips, range(1, chips), True)
    feed_own, feed_away, *held = flow.until(feed_own, feed_away, *mixer_near, *normed_parts)
    mixer_near, normed_parts = jnp.stack(held[:chips]), held[chips:]
    held = flow.until(*swap_cores(mixer_near, 2), *gather_end(normed_parts))
    mixer_far, normed = joined(held[:2]), joined(held[2:])
    split = (chips + 1) // 2 + 1
    away = [swap(flow.after(feed_away[j - 1])[0], 2 * j) for j in range(1, chips)]
    (block_order,) = flow.after(block_order)
    info = positions(
        one_of(block_order[0], core), one_of(doc_ids[0], core), one_of(prefix_len[0], core), length
    )
    facts = jnp.stack(info).reshape(4, devices, tok_count)
    facts = jnp.stack([one_of(facts, me ^ p, 1) for p in range(devices)], axis=1)
    place, member, relative, limit = facts.reshape(4, length)
    rows = jnp.concatenate([jnp.stack([place, member, limit]), jnp.zeros((5, length), jnp.int32)])
    columns = jnp.stack([place, member], axis=1)
    angle = angles_for(relative)
    cosine, sine = jnp.cos(angle), jnp.sin(angle)
    cosine = jnp.concatenate([cosine] * 4, axis=1)
    sine = jnp.concatenate([-sine, sine, -sine, sine], axis=1)

    output_rows = both_cores(output_weight, output_far)
    mixer_columns = place_blocks(me, mixer_near, mixer_far)
    (normed,) = flow.after(normed)
    raw = product("rows", normed, mixer_columns, full)
    attended, query, kv, logs = attend(raw, cosine, sine, columns, rows)
    branch = product("rows", attended, output_rows, full)
    normed_other = swap_cores(normed, 2)
    held = flow.until(branch, *away, *normed_other)
    branch, away, normed_other = held[0], held[1:chips], joined(held[chips:])
    away = joined(away)
    other, away_far = swap_copies(away, 1), swap(away, 1)
    feed_own_far = swap(*flow.after(feed_own), 1)
    parts = flow.until(*scatter_end(scatter_start(flow.after(branch)[0])))
    normed_two_own, hidden = norm_rows(feed_gain, inputs, *parts)
    (normed_two_own,) = flow.until(normed_two_own)
    normed_two_parts = flow.until(*gather_start(normed_two_own))
    held = flow.until(other, away_far, feed_own_far, *gather_end(normed_two_parts))
    other, away_far, feed_own_far, normed_two = held[0], held[1], held[2], joined(held[3:])
    grad_rows = by_core(*flow.after(cotangent[0]))
    other_far, grad_rows = flow.until(swap(other, 1), grad_rows)
    (own, down_weight) = flow.after(grad_rows, down_weight)
    down_far = swap(down_weight, 1)
    cotangent_rows = (
        [own] + [swap(own, 2 * j) for j in range(1, chips)]
        if chips == 4
        else gather_end(gather_start(own))
    )
    normed_two_other = swap(flow.after(normed_two)[0], 1)
    feed_pieces = [([(0, None)], feed_own), ([(1, None)], feed_own_far)]
    for kind, array in enumerate((away, away_far, other, other_far)):
        feed_pieces.append(([(2 * j + kind % 2, kind // 2) for j in range(1, chips)], array))
    inner, both, feed_columns, normed_two_other, down_far, *held = flow.until(
        *feed_forward(me, side, normed_two, feed_pieces),
        normed_two_other,
        down_far,
        *cotangent_rows,
    )
    all_grad_rows = joined(held)
    down_all = both_cores(down_weight, down_far)

    down_partial = product("outer", inner, all_grad_rows, low).reshape(2, down_rows, width)
    came = swap_cores(one_of(down_partial, 1 - core), 2)
    down_all, *came = flow.until(down_all, *came)
    mine = [
        lax.dynamic_slice_in_dim(
            down_partial.reshape(2 * down_rows, width),
            core * down_rows + piece * (down_rows // 2),
            down_rows // 2,
            0,
        )
        for piece in range(2)
    ]
    down_parts = flow.until(
        *[(x.astype(full) + y.astype(full)).astype(low) for x, y in zip(mine, came)]
    )
    for piece in range(2):
        chain.add(("down", piece), down_parts[piece])
    chain.step()

    (grad_both,) = flow.until(feed_backward(*flow.after(all_grad_rows), down_all, both))
    grad_both_other = swap(grad_both, 1)
    partial_two = product("transpose", grad_both, feed_columns, full)
    (partial_two,) = flow.until(partial_two)
    chain.step()
    grad_both_other, *parts = flow.until(
        grad_both_other, *scatter_end(scatter_start(*flow.after(partial_two)))
    )
    picks = range(0, devices, 2)
    pieces = outer_blocks(
        me, normed_two, *flow.after(grad_both), normed_two_other, grad_both_other, picks
    )
    grad_branch_own, grad_hidden, feed_part = norm_back(
        feed_gain, hidden, grad_rows, *parts
    )
    held = flow.until(*pieces, *gather_start(grad_branch_own))
    pieces, parts = held[:chips], held[chips:]
    chain.add(("feed", 0), pieces[0])
    chain.step()
    grad_branch = joined(gather_end(flow.after(*parts)))
    output_partial = product("outer", attended, grad_branch, low)
    output_partial = output_partial.reshape(2, shard_rows, width)
    came = swap_cores(one_of(output_partial, 1 - core), 2)
    grad_attended = product("transpose", grad_branch, output_rows, low)
    grad_mixer = attend_back(query, kv, grad_attended, logs, cosine, sine, columns, rows)
    partial = product("transpose", grad_mixer, mixer_columns, full)
    grad_mixer_other = swap_cores(grad_mixer, 2)
    partial, grad_mixer, held, *came = flow.until(
        partial, grad_mixer, output_partial, *came, *grad_mixer_other
    )
    grad_mixer_other, came = joined(came[2:]), came[:2]
    output_part = (one_of(held, core).astype(full) + joined(came).astype(full)).astype(low)
    chain.add("output", output_part)
    chain.step()
    moved = {j: swap(flow.after(pieces[j])[0], 2 * j) for j in range(1, split)}
    mixer_pieces = outer_blocks(
        me, normed, *flow.after(grad_mixer), normed_other, grad_mixer_other, picks
    )
    held = flow.until(*mixer_pieces, *[moved[j] for j in range(1, split)])
    mixer_pieces, early = held[:chips], held[chips:]
    for j, piece in enumerate(early, 1):
        chain.add(("feed", j), piece)
    chain.step()
    parts = scatter_end(scatter_start(flow.after(partial)[0]))
    input_grad, _, mixer_part = norm_back(
        mixer_gain, inputs, flow.after(grad_hidden)[0], *flow.until(*parts)
    )
    (input_grad,) = flow.until(input_grad)
    chain.step()
    for _ in range(split - 3):
        chain.step()
    gains = jnp.concatenate([mixer_part, feed_part]).reshape(2, 8, width // 8)
    gains, *mixer_pieces = flow.after(gains, *mixer_pieces)
    bits = 1
    while bits < devices:
        gains = gains + swap(gains, bits)
        bits = 2 * bits
    gains, *mixer_pieces = flow.until(
        gains, *[swap(mixer_pieces[j], 2 * j) if j else mixer_pieces[j] for j in range(chips)]
    )
    chain.add("mixer", jnp.stack(mixer_pieces))
    chain.step()
    late = [swap(flow.after(pieces[j])[0], 2 * j) for j in range(split, chips)]
    down = product("rows", *flow.after(inner), down_all, full)
    down, *late = flow.until(down, *late)
    for j, piece in enumerate(late, split):
        chain.add(("feed", j), piece, *([gains] if j == chips - 1 else []))
    chain.step()
    for _ in range(chips - split - 1):
        chain.step()
    parts = flow.until(*scatter_start(flow.after(down)[0]))
    chain.step()
    parts = flow.until(*scatter_end(flow.after(*parts)))
    layer_out = by_token((hidden + sum(part.astype(full) for part in parts)).astype(low))
    input_grad = by_token(input_grad)
    chain.finish()
    results = chain.results
    down_grad = jnp.concatenate([results["down", piece][0] for piece in range(2)], axis=0)
    down_grad = down_grad.astype(full)
    output_grad = results["output"][0].astype(full)
    done = [results["feed", j][0] for j in range(chips)]
    if hidden_width % 128:
        stacked = jnp.stack(done)
        ordered = jnp.stack([one_of(stacked, me // 2 ^ j) for j in range(chips)])
        ordered = ordered.astype(full).reshape(chips, shard_rows, 2, hidden_width)
        gate_grad, up_grad = ordered.transpose(2, 1, 0, 3).reshape(2, shard_rows, -1)
    else:
        held = ()
        for j, piece in enumerate(done):
            held = spread(me, j, piece, chips, held)
        gate_grad, up_grad = held
    mixer_grads = results["mixer"][0]
    mixer_grads = jnp.stack([one_of(mixer_grads, me // 2 ^ j) for j in range(chips)])
    mixer_grads = mixer_grads.astype(full)
    query_grad = mixer_grads[:, :, :query_width].transpose(1, 0, 2).reshape(shard_rows, -1)
    shared = (
        mixer_grads[:, :, query_width:]
        .reshape(KV_HEADS, sharing, shard_rows, 2, HEAD_DIM)
        .sum(axis=1)
    )
    key_grad = shared[:, :, 0].transpose(1, 0, 2).reshape(shard_rows, -1)
    value_grad = shared[:, :, 1].transpose(1, 0, 2).reshape(shard_rows, -1)
    mixer_total, feed_total = results["feed", chips - 1][1].reshape(2, width)
    return (
        layer_out,
        input_grad,
        mixer_total,
        query_grad,
        key_grad,
        value_grad,
        output_grad,
        feed_total,
        gate_grad,
        up_grad,
        down_grad,
    )


def solution(mesh):
    placed = (
        P("rep", None, "fsdp", None),
        P("rep", None, "fsdp", None),
        P(),
        P("fsdp", None),
        P("fsdp", None),
        P("fsdp", None),
        P("fsdp", None),
        P(),
        P("fsdp", None),
        P("fsdp", None),
        P("fsdp", None),
        P("rep", None, None),
        P("rep", None, None),
        P("rep", None, None),
    )
    return jax.shard_map(
        local,
        mesh=mesh,
        in_specs=placed,
        out_specs=(
            P("rep", None, "fsdp", None),
            P("rep", None, "fsdp", None),
            P(),
            P("fsdp", None),
            P("fsdp", None),
            P("fsdp", None),
            P("fsdp", None),
            P(),
            P("fsdp", None),
            P("fsdp", None),
            P("fsdp", None),
        ),
        check_vma=False,
    )
```

```python
import functools

import jax
import jax.numpy as jnp
from jax import lax
from jax.experimental import pallas as pl
from jax.experimental.pallas import tpu as pltpu
from jax.sharding import PartitionSpec as P

HEADS = 32
KV_HEADS = 4
HEAD_DIM = 64
MICRO = 2
SEGS = 3


epsilon = 1e-05
FREE = pl.CostEstimate(flops=0, transcendentals=0, bytes_accessed=0)


def positions(order_row, doc_row, prefix_row, length):
    count = order_row.shape[0]
    block_width = length // count
    index = jnp.arange(length, dtype=jnp.int32)
    slot = index // block_width
    block = jnp.sum(
        jnp.where(
            slot[:, None] == jnp.arange(count, dtype=jnp.int32)[None, :], order_row[None, :], 0
        ),
        axis=1,
        dtype=jnp.int32,
    )
    place = block * block_width + index % block_width
    labels = jnp.arange(SEGS, dtype=jnp.int32)
    starts = jnp.sum(
        (doc_row[None, :] < labels[:, None]).astype(jnp.int32), axis=1, dtype=jnp.int32
    )
    member = jnp.sum(
        (place[:, None] >= starts[None, 1:]).astype(jnp.int32), axis=1, dtype=jnp.int32
    )
    picked = member[:, None] == labels[None, :]
    start_of = jnp.sum(jnp.where(picked, starts[None, :], 0), axis=1, dtype=jnp.int32)
    limit = jnp.sum(
        jnp.where(picked, starts[None, :] + prefix_row[None, :], 0), axis=1, dtype=jnp.int32
    )
    return (place, member, place - start_of, limit)


def angles_for(relative):
    halfway = HEAD_DIM // 2
    frequency = 10000.0 ** (-(2.0 * jnp.arange(halfway, dtype=jnp.float32)) / HEAD_DIM)
    return relative.astype(jnp.float32)[:, None] * frequency[None, :]


def rms_scale(values, gain):
    return values * lax.rsqrt(jnp.mean(values * values, axis=1, keepdims=True) + epsilon) * gain


def gated(gate_part, up_part):
    return jax.nn.silu(gate_part) * up_part


def contract_rows(left, right):
    return lax.dot_general(
        left, right, (((0,), (0,)), ((), ())), preferred_element_type=jnp.float32
    )


def times_transpose(left, right):
    return lax.dot_general(
        left, right, (((1,), (1,)), ((), ())), preferred_element_type=jnp.float32
    )


def dot_rows(left, right):
    return jnp.dot(left, right, preferred_element_type=jnp.float32)


def turn(field, cosine, sine):
    lane = lax.broadcasted_iota(jnp.int32, field.shape, 1) % HEAD_DIM
    half = HEAD_DIM // 2
    swapped = jnp.where(
        lane < half, pltpu.roll(field, 2 * HEAD_DIM - half, 1), pltpu.roll(field, half, 1)
    )
    return field * cosine + swapped * sine


def seen(columns, rows):
    place_q, member_q = columns[:, 0:1], columns[:, 1:2]
    place_k, member_k, limit_k = rows[0:1, :], rows[1:2, :], rows[2:3, :]
    return (member_q == member_k) & ((place_k <= place_q) | (place_k < limit_k))


def attend_kernel(raw_ref, cos_ref, sin_ref, column_ref, row_ref, out_ref, query_ref, kv_ref, log_ref):
    scale = HEAD_DIM ** (-0.5)
    cosine, sine = cos_ref[...], sin_ref[...]
    visible = seen(column_ref[...], row_ref[...])
    wide = 2 * HEAD_DIM
    pair_count = raw_ref.shape[1] // wide - 1
    first = lax.broadcasted_iota(jnp.int32, cosine.shape, 1) < HEAD_DIM
    kv = raw_ref[:, pair_count * wide :]
    keys_values = jnp.where(first, turn(kv, cosine, sine), kv)
    swapped = pltpu.roll(keys_values, HEAD_DIM, 1)
    keys = jnp.where(first, keys_values, swapped).astype(jnp.bfloat16)
    values = jnp.where(first, swapped, keys_values).astype(jnp.bfloat16)
    kv_ref[...] = keys_values.astype(jnp.bfloat16)
    logs = jnp.zeros(cosine.shape, jnp.float32)
    lanes = lax.broadcasted_iota(jnp.int32, cosine.shape, 1)
    for pair in range(pair_count):
        at = slice(pair * wide, (pair + 1) * wide)
        query = turn(raw_ref[:, at], cosine, sine).astype(jnp.bfloat16)
        query_ref[:, at] = query
        results = []
        for member in range(2):
            chosen = first if member == 0 else jnp.logical_not(first)
            one = jnp.where(chosen, query, jnp.zeros_like(query))
            scores = (
                lax.dot_general(
                    one, keys, (((1,), (1,)), ((), ())), preferred_element_type=jnp.float32
                )
                * scale
            )
            scores = jnp.where(visible, scores, -1000000000.0)
            peak = jnp.max(scores, axis=1, keepdims=True)
            raised = jnp.exp(scores - peak)
            totals = jnp.sum(raised, axis=1, keepdims=True)
            probs = (raised * (1.0 / totals)).astype(jnp.bfloat16)
            results.append(dot_rows(probs, values))
            logs = jnp.where(lanes == 2 * pair + member, peak + jnp.log(totals), logs)
        out_ref[:, at] = jnp.where(first, results[0], results[1]).astype(jnp.bfloat16)
    log_ref[...] = logs


def attend_back_kernel(
    query_ref, kv_ref, grad_ref, log_ref, cos_ref, sin_ref, column_ref, row_ref, out_ref
):
    scale = HEAD_DIM ** (-0.5)
    cosine, sine = cos_ref[...], sin_ref[...]
    visible = seen(column_ref[...], row_ref[...])
    wide = 2 * HEAD_DIM
    pair_count = query_ref.shape[1] // wide
    first = lax.broadcasted_iota(jnp.int32, cosine.shape, 1) < HEAD_DIM
    lanes = lax.broadcasted_iota(jnp.int32, cosine.shape, 1)
    keys_values = kv_ref[...]
    swapped = pltpu.roll(keys_values.astype(jnp.float32), HEAD_DIM, 1).astype(jnp.bfloat16)
    keys = jnp.where(first, keys_values, swapped)
    values = jnp.where(first, swapped, keys_values)
    logs = log_ref[...]
    grad_keys = jnp.zeros(cosine.shape, jnp.float32)
    grad_values = jnp.zeros(cosine.shape, jnp.float32)
    for pair in range(pair_count):
        at = slice(pair * wide, (pair + 1) * wide)
        query, grad = query_ref[:, at], grad_ref[:, at]
        results = []
        for member in range(2):
            chosen = first if member == 0 else jnp.logical_not(first)
            one = jnp.where(chosen, query, jnp.zeros_like(query))
            grad_one = jnp.where(chosen, grad, jnp.zeros_like(grad))
            log_one = jnp.sum(
                jnp.where(lanes == 2 * pair + member, logs, 0.0), axis=1, keepdims=True
            )
            scores = (
                lax.dot_general(
                    one, keys, (((1,), (1,)), ((), ())), preferred_element_type=jnp.float32
                )
                * scale
            )
            probs = jnp.exp(jnp.where(visible, scores, -1000000000.0) - log_one)
            grad_probs = lax.dot_general(
                grad_one, values, (((1,), (1,)), ((), ())), preferred_element_type=jnp.float32
            )
            inner_sum = jnp.sum(probs * grad_probs, axis=1, keepdims=True)
            grad_scores = (probs * (grad_probs - inner_sum)).astype(jnp.bfloat16)
            results.append(dot_rows(grad_scores, keys) * scale)
            grad_keys = grad_keys + contract_rows(grad_scores, one)
            grad_values = grad_values + contract_rows(probs.astype(jnp.bfloat16), grad_one)
        joined = jnp.where(first, results[0], results[1])
        out_ref[:, at] = turn(joined, cosine, -sine).astype(jnp.bfloat16)
    grad_keys = (grad_keys + pltpu.roll(grad_keys, HEAD_DIM, 1)) * scale
    grad_values = grad_values + pltpu.roll(grad_values, HEAD_DIM, 1)
    last = jnp.where(first, turn(grad_keys, cosine, -sine), grad_values)
    out_ref[:, pair_count * wide :] = last.astype(jnp.bfloat16)


def whole(*_):
    return (0, 0)


def whole_specs(arrays):
    return [pl.BlockSpec(a.shape, whole) for a in arrays]


def attend(raw, cosine, sine, columns, rows):
    length, wide = raw.shape
    query_width = wide - 2 * HEAD_DIM
    heads = query_width // HEAD_DIM
    outs = [
        jax.ShapeDtypeStruct((length, query_width), jnp.bfloat16),
        jax.ShapeDtypeStruct((length, query_width), jnp.bfloat16),
        jax.ShapeDtypeStruct((length, 2 * HEAD_DIM), jnp.bfloat16),
        jax.ShapeDtypeStruct((length, 2 * HEAD_DIM), jnp.float32),
    ]
    args = (raw, cosine, sine, columns, rows)
    return pl.pallas_call(
        attend_kernel,
        grid=(1,),
        in_specs=whole_specs(args),
        out_specs=whole_specs(outs),
        out_shape=outs,
        compiler_params=pltpu.CompilerParams(vmem_limit_bytes=48 * 1024 * 1024),
        cost_estimate=FREE,
        name="attend",
    )(*args)


def attend_back(query, kv, grad, logs, cosine, sine, columns, rows):
    length, query_width = query.shape
    heads = query_width // HEAD_DIM
    out = jax.ShapeDtypeStruct((length, query_width + 2 * HEAD_DIM), jnp.bfloat16)
    args = (query, kv, grad, logs, cosine, sine, columns, rows)
    return pl.pallas_call(
        attend_back_kernel,
        grid=(1,),
        in_specs=whole_specs(args),
        out_specs=pl.BlockSpec(out.shape, whole),
        out_shape=out,
        compiler_params=pltpu.CompilerParams(vmem_limit_bytes=48 * 1024 * 1024),
        cost_estimate=FREE,
        name="attend_back",
    )(*args)


def total_of(refs):
    total = refs[0][...].astype(jnp.float32)
    for ref in refs[1:]:
        total = total + ref[...].astype(jnp.float32)
    return total


def norm_kernel(gain_ref, *refs):
    low_ref, full_ref = refs[-2:]
    rows = total_of(refs[:-2])
    scale = lax.rsqrt(jnp.mean(rows * rows, axis=1, keepdims=True) + epsilon)
    full_ref[...] = rows
    low_ref[...] = (rows * scale * gain_ref[...].astype(jnp.float32)).astype(low_ref.dtype)


def norm_rows(gain, *parts):
    shape = parts[0].shape
    args = (gain.reshape(1, -1),) + parts
    outs = [jax.ShapeDtypeStruct(shape, jnp.bfloat16), jax.ShapeDtypeStruct(shape, jnp.float32)]
    return pl.pallas_call(
        norm_kernel,
        grid=(1,),
        in_specs=whole_specs(args),
        out_specs=whole_specs(outs),
        out_shape=outs,
        compiler_params=pltpu.CompilerParams(vmem_limit_bytes=32 * 1024 * 1024),
        cost_estimate=FREE,
        name="norm_rows",
    )(*args)


def norm_back_kernel(gain_ref, rows_ref, base_ref, *refs):
    low_ref, full_ref, gain_grad_ref = refs[-3:]
    rows, grad = rows_ref[...], total_of(refs[:-3])
    scale = lax.rsqrt(jnp.mean(rows * rows, axis=1, keepdims=True) + epsilon)
    gain_grad_ref[...] = jnp.sum(grad * rows * scale, axis=0, keepdims=True)
    inside = grad * gain_ref[...].astype(jnp.float32)
    slope = jnp.mean(inside * rows, axis=1, keepdims=True)
    result = base_ref[...].astype(jnp.float32) + scale * inside - rows * (scale**3 * slope)
    full_ref[...] = result
    low_ref[...] = result.astype(low_ref.dtype)


def norm_back(gain, rows, base, *parts):
    shape = rows.shape
    args = (gain.reshape(1, -1), rows, base) + parts
    outs = [
        jax.ShapeDtypeStruct(shape, jnp.bfloat16),
        jax.ShapeDtypeStruct(shape, jnp.float32),
        jax.ShapeDtypeStruct((1, shape[1]), jnp.float32),
    ]
    return pl.pallas_call(
        norm_back_kernel,
        grid=(1,),
        in_specs=whole_specs(args),
        out_specs=whole_specs(outs),
        out_shape=outs,
        compiler_params=pltpu.CompilerParams(vmem_limit_bytes=32 * 1024 * 1024),
        cost_estimate=FREE,
        name="norm_back",
    )(*args)


def pick_kernel(place_ref, gate_ref, up_ref, out_ref):
    for at in range(0, gate_ref.shape[1], 128):
        out_ref[0, :, 2 * at : 2 * at + 128] = gate_ref[:, at : at + 128]
        out_ref[0, :, 2 * at + 128 : 2 * at + 256] = up_ref[:, at : at + 128]


def pick_blocks(me, side, gate, up, chips, picks, halved):
    rows, total = gate.shape
    width = total // chips
    if halved:
        rows = rows // 2
    if width % 128:
        both = jnp.concatenate(
            [a.reshape(a.shape[0], chips, width).transpose(1, 0, 2) for a in (gate, up)], axis=2
        )
        if halved:
            both = lax.dynamic_slice_in_dim(both, side * rows, rows, 1)
        return jnp.stack(
            [lax.dynamic_index_in_dim(both, me // 2 ^ j, 0, keepdims=False) for j in picks]
        )
    first = picks[0]
    column = pl.BlockSpec(
        (rows, width), lambda s, place: (place[1] if halved else 0, place[0] // 2 ^ (s + first))
    )
    return pl.pallas_call(
        pick_kernel,
        grid_spec=pltpu.PrefetchScalarGridSpec(
            num_scalar_prefetch=1,
            grid=(len(picks),),
            in_specs=[column, column],
            out_specs=pl.BlockSpec((1, rows, 2 * width), lambda s, place: (s, 0, 0)),
        ),
        out_shape=jax.ShapeDtypeStruct((len(picks), rows, 2 * width), gate.dtype),
        compiler_params=pltpu.CompilerParams(vmem_limit_bytes=16 * 1024 * 1024),
        cost_estimate=FREE,
        name="pick_blocks",
    )(jnp.stack([me, side]), gate, up)


def tile_of(width):
    return 128 if width % 128 == 0 else width


def forward_kernel(place_ref, rows_ref, *refs, marks, shard):
    inner_ref, both_ref, weight_ref = refs[len(marks) :]
    for group, piece_ref in zip(marks, refs):
        count = piece_ref.shape[0] // len(group)
        for at, (p, flip) in enumerate(group):
            start = (place_ref[0] ^ p) * shard
            if flip is not None:
                start = start + (place_ref[1] ^ flip) * count
            weight_ref[pl.ds(pl.multiple_of(start, count), count), :] = piece_ref[
                at * count : (at + 1) * count, :
            ]
    both = dot_rows(rows_ref[...], weight_ref[...])
    half = both.shape[1] // 2
    gate, upward = both[:, :half], both[:, half:]
    both_ref[...] = both
    inner_ref[...] = (gate / (1.0 + jnp.exp(-gate)) * upward).astype(inner_ref.dtype)


def feed_forward(me, side, rows, pieces):
    count, width = rows.shape
    columns = pieces[0][1].shape[1]
    hidden = columns // 2
    tile = tile_of(hidden)
    marks = [mark for mark, _ in pieces]
    arrays = [piece for _, piece in pieces]
    outs = [
        jax.ShapeDtypeStruct((count, hidden), jnp.bfloat16),
        jax.ShapeDtypeStruct((count, columns), jnp.float32),
        jax.ShapeDtypeStruct((width, columns), jnp.bfloat16),
    ]
    return pl.pallas_call(
        functools.partial(
            forward_kernel, marks=marks, shard=width // lax.axis_size("fsdp")
        ),
        grid_spec=pltpu.PrefetchScalarGridSpec(
            num_scalar_prefetch=1,
            grid=(hidden // tile,),
            in_specs=[pl.BlockSpec((count, width), lambda s, place: (0, 0))]
            + [pl.BlockSpec((a.shape[0], 2 * tile), lambda s, place: (0, s)) for a in arrays],
            out_specs=[
                pl.BlockSpec((count, tile), lambda s, place: (0, s)),
                pl.BlockSpec((count, 2 * tile), lambda s, place: (0, s)),
                pl.BlockSpec((width, 2 * tile), lambda s, place: (0, s)),
            ],
        ),
        out_shape=outs,
        compiler_params=pltpu.CompilerParams(vmem_limit_bytes=48 * 1024 * 1024),
        cost_estimate=FREE,
        name="feed_forward",
    )(jnp.stack([me, side]), rows, *arrays)


def backward_kernel(grad_ref, weight_ref, both_ref, out_ref):
    grad = times_transpose(grad_ref[...], weight_ref[...])
    half = both_ref.shape[1] // 2
    gate, upward = both_ref[:, :half], both_ref[:, half:]
    sigmoid = 1.0 / (1.0 + jnp.exp(-gate))
    silu = gate * sigmoid
    out_ref[:, :half] = (
        grad * upward * (sigmoid + silu * (1.0 - sigmoid))
    ).astype(out_ref.dtype)
    out_ref[:, half:] = (grad * silu).astype(out_ref.dtype)


def feed_backward(grad_rows, weight, both):
    count, width = grad_rows.shape
    hidden = weight.shape[0]
    tile = tile_of(hidden)
    return pl.pallas_call(
        backward_kernel,
        grid=(hidden // tile,),
        in_specs=[
            pl.BlockSpec((count, width), lambda s: (0, 0)),
            pl.BlockSpec((tile, width), lambda s: (s, 0)),
            pl.BlockSpec((count, 2 * tile), lambda s: (0, s)),
        ],
        out_specs=pl.BlockSpec((count, 2 * tile), lambda s: (0, s)),
        out_shape=jax.ShapeDtypeStruct((count, 2 * hidden), jnp.bfloat16),
        compiler_params=pltpu.CompilerParams(vmem_limit_bytes=40 * 1024 * 1024),
        cost_estimate=FREE,
        name="feed_backward",
    )(grad_rows, weight, both)


def product_kernel(left_ref, right_ref, out_ref, *, kind):
    multiply = {"rows": dot_rows, "transpose": times_transpose, "outer": contract_rows}[kind]
    out_ref[...] = multiply(left_ref[...], right_ref[...]).astype(out_ref.dtype)


def product(kind, left, right, dtype):
    rows = left.shape[1 if kind == "outer" else 0]
    columns = right.shape[0 if kind == "transpose" else 1]
    tile = 256 if columns % 256 == 0 else 128
    right_spec = (
        pl.BlockSpec((tile, right.shape[1]), lambda s: (s, 0))
        if kind == "transpose"
        else pl.BlockSpec((right.shape[0], tile), lambda s: (0, s))
    )
    return pl.pallas_call(
        functools.partial(product_kernel, kind=kind),
        grid=(columns // tile,),
        in_specs=[pl.BlockSpec(left.shape, lambda s: (0, 0)), right_spec],
        out_specs=pl.BlockSpec((rows, tile), lambda s: (0, s)),
        out_shape=jax.ShapeDtypeStruct((rows, columns), dtype),
        compiler_params=pltpu.CompilerParams(vmem_limit_bytes=40 * 1024 * 1024),
        cost_estimate=FREE,
        name="product_" + kind,
    )(left, right)


def outer_kernel(place_ref, left_ref, right_ref, left_other_ref, right_other_ref, *out_refs):
    total = contract_rows(left_ref[...], right_ref[...])
    total = total + contract_rows(left_other_ref[...], right_other_ref[...])
    for at, out_ref in enumerate(out_refs):

        @pl.when(pl.program_id(0) == at)
        def _():
            out_ref[...] = total.astype(out_ref.dtype)


def outer_blocks(me, left, right, left_other, right_other, picks):
    tokens, width = right.shape
    rows = left.shape[1] // lax.axis_size("fsdp")
    first = picks[0]
    jump = picks[1] - first if len(picks) > 1 else 1
    column = pl.BlockSpec((tokens, rows), lambda s, place: (0, place[0] ^ (first + jump * s)))
    full = pl.BlockSpec((tokens, width), lambda s, place: (0, 0))
    block = pl.BlockSpec((rows, width), lambda s, place: (0, 0))
    return pl.pallas_call(
        outer_kernel,
        grid_spec=pltpu.PrefetchScalarGridSpec(
            num_scalar_prefetch=1,
            grid=(len(picks),),
            in_specs=[column, full, column, full],
            out_specs=[block] * len(picks),
        ),
        out_shape=[jax.ShapeDtypeStruct((rows, width), jnp.bfloat16)] * len(picks),
        compiler_params=pltpu.CompilerParams(vmem_limit_bytes=48 * 1024 * 1024),
        cost_estimate=FREE,
        name="outer_blocks",
    )(me.reshape(1), left, right, left_other, right_other)


def place_kernel(place_ref, near_ref, far_ref, out_ref):
    @pl.when(pl.program_id(1) == 0)
    def _():
        out_ref[...] = near_ref[...]

    @pl.when(pl.program_id(1) == 1)
    def _():
        out_ref[...] = far_ref[...]


def place_blocks(me, near, far):
    chips, rows, width = near.shape
    block = pl.BlockSpec((1, rows, width), lambda j, b, place: (j, 0, 0))
    return pl.pallas_call(
        place_kernel,
        grid_spec=pltpu.PrefetchScalarGridSpec(
            num_scalar_prefetch=1,
            grid=(chips, 2),
            in_specs=[block, block],
            out_specs=pl.BlockSpec(
                (1, rows, width), lambda j, b, place: (place[0] ^ (2 * j + b), 0, 0)
            ),
        ),
        out_shape=jax.ShapeDtypeStruct((2 * chips, rows, width), near.dtype),
        compiler_params=pltpu.CompilerParams(vmem_limit_bytes=16 * 1024 * 1024),
        cost_estimate=FREE,
        name="place_blocks",
    )(me.reshape(1), near, far).reshape(2 * chips * rows, width)


def spread_first(place_ref, piece_ref, gate_ref, up_ref):
    for at in range(0, gate_ref.shape[1], 128):
        gate_ref[:, at : at + 128] = piece_ref[:, 2 * at : 2 * at + 128].astype(jnp.float32)
        up_ref[:, at : at + 128] = piece_ref[:, 2 * at + 128 : 2 * at + 256].astype(jnp.float32)


def spread_next(place_ref, piece_ref, gate_in, up_in, gate_ref, up_ref):
    spread_first(place_ref, piece_ref, gate_ref, up_ref)


def spread(me, j, piece, chips, held):
    rows, both = piece.shape
    width = both // 2
    out = jax.ShapeDtypeStruct((rows, width * chips), jnp.float32)
    column = pl.BlockSpec((rows, width), lambda s, place: (0, place[0] // 2 ^ j))
    anywhere = pl.BlockSpec(memory_space=pl.ANY)
    return pl.pallas_call(
        spread_next if held else spread_first,
        grid_spec=pltpu.PrefetchScalarGridSpec(
            num_scalar_prefetch=1,
            grid=(1,),
            in_specs=[pl.BlockSpec((rows, both), lambda s, place: (0, 0))]
            + [anywhere] * len(held),
            out_specs=[column, column],
        ),
        out_shape=[out, out],
        input_output_aliases={2: 0, 3: 1} if held else {},
        compiler_params=pltpu.CompilerParams(vmem_limit_bytes=24 * 1024 * 1024),
        cost_estimate=FREE,
        name="spread",
    )(me.reshape(1), piece, *held)


class Flow:
    def __init__(self, token):
        self.token = token

    def after(self, *arrays):
        return lax.optimization_barrier((self.token,) + tuple(arrays))[1:]

    def until(self, *arrays):
        held = lax.optimization_barrier((self.token,) + tuple(arrays))
        self.token = held[0]
        return held[1:]


class Chain:
    def __init__(self, flow, copies, index):
        self.flow, self.copies, self.index = flow, copies, index
        half = copies // 2
        ends = [(s, copies - 1 - s) for s in range(half - 1)]
        self.stages = [([(a, a + 1), (b, b - 1)], None) for a, b in ends]
        self.stages.append(([(half - 1, half), (half, half - 1)], None))
        self.stages += [([(a + 1, a), (b - 1, b)], (a, b)) for a, b in reversed(ends)]
        self.waiting, self.moving, self.results = [], [], {}

    def add(self, name, *parts):
        self.waiting.append((name, parts))

    def start(self, parts, stage):
        return [lax.ppermute(part, "rep", self.stages[stage][0]) for part in parts]

    def step(self):
        moving, self.moving = self.moving, []
        if self.waiting:
            name, parts = self.waiting.pop(0)
            parts = self.flow.after(*parts)
            self.moving.append((name, parts, self.start(parts, 0), 0))
        if not moving:
            return
        arrived = iter(self.flow.until(*[array for item in moving for array in item[2]]))
        summed = []
        for name, parts, came, stage in moving:
            came = [next(arrived) for _ in came]
            outer = self.stages[stage][1]
            if outer is None:
                parts = [
                    (a.astype(jnp.float32) + b.astype(jnp.float32)).astype(a.dtype)
                    for a, b in zip(parts, came)
                ]
            else:
                here = (self.index == outer[0]) | (self.index == outer[1])
                parts = [jnp.where(here, b, a) for a, b in zip(parts, came)]
            if stage + 1 == len(self.stages):
                self.results[name] = parts
            else:
                summed.append((name, parts, stage + 1))
        for name, parts, stage in summed:
            self.moving.append((name, parts, self.start(parts, stage), stage))

    def finish(self):
        while self.waiting or self.moving:
            self.step()


def local(
    tokens,
    cotangent,
    mixer_gain,
    query_weight,
    key_weight,
    value_weight,
    output_weight,
    feed_gain,
    gate_weight,
    up_weight,
    down_weight,
    doc_ids,
    prefix_len,
    block_order,
):
    tok_count, width = tokens.shape[2:]
    devices = lax.axis_size("fsdp")
    chips = devices // 2
    copies = lax.axis_size("rep")
    me = lax.axis_index("fsdp")
    core = me % 2
    copy_index = lax.axis_index("rep")
    side = copy_index % 2
    length = tok_count * devices
    shard_rows = width // devices
    half_shard = shard_rows // 2
    query_width = HEADS // chips * HEAD_DIM
    sharing = max(1, chips // KV_HEADS)
    down_rows = down_weight.shape[0]
    hidden_width = 2 * down_rows
    low = jnp.bfloat16
    full = jnp.float32
    flow = Flow(jnp.zeros((8, 128), full) + copy_index.astype(full))
    chain = Chain(flow, copies, copy_index)

    def swap(array, bits):
        return lax.ppermute(array, "fsdp", [(d, d ^ bits) for d in range(devices)])

    def swap_copies(array, bits):
        return lax.ppermute(array, "rep", [(d, d ^ bits) for d in range(copies)])

    def one_of(array, index, axis=0):
        return lax.dynamic_index_in_dim(array, index, axis, keepdims=False)

    def both_cores(mine, other):
        return place_blocks(core, mine[None], other[None])

    def gather_start(own):
        return (own, swap(own, 2), swap(own, 4)) if chips == 4 else (own,)

    def gather_end(parts):
        if chips == 4:
            own, along_x, along_y = parts
            mid = own.shape[0] // 2
            return [own, along_x, along_y, swap(along_y[:mid], 2), swap(along_x[mid:], 4)]
        (own,) = parts
        bits = 2
        while bits < devices:
            own = jnp.concatenate([own, swap(own, bits)], axis=0)
            bits = 2 * bits
        return [own]

    def joined(parts):
        return jnp.concatenate(parts, axis=0) if len(parts) > 1 else parts[0]

    def scatter_start(partial):
        if chips != 4:
            return (partial,)
        mine, to_x, to_y, across = jnp.split(partial, 4, axis=0)
        mid = mine.shape[0] // 2
        across = across.astype(low)
        return mine, to_x, to_y, swap(across[:mid], 2), swap(across[mid:], 4)

    def scatter_end(parts):
        if chips == 4:
            mine, to_x, to_y, from_x, from_y = parts
            mid = mine.shape[0] // 2
            to_x = jnp.concatenate([to_x[:mid], to_x[mid:] + from_y.astype(full)], axis=0)
            to_y = jnp.concatenate([to_y[:mid] + from_x.astype(full), to_y[mid:]], axis=0)
            came_x, came_y = swap(to_x.astype(low), 2), swap(to_y.astype(low), 4)
            return mine, came_x, came_y
        (partial,) = parts
        bits = devices // 2
        while bits > 1:
            rows = partial.shape[0] // 2
            partial = partial[:rows] + swap(partial[rows:].astype(low), bits).astype(full)
            bits = bits // 2
        return (partial,)

    def swap_cores(array, pieces):
        rows = array.shape[0] // pieces
        return [swap(array[at * rows : (at + 1) * rows], 1) for at in range(pieces)]

    def by_core(array):
        mine, other = one_of(array, core), one_of(array, 1 - core)
        return jnp.concatenate([mine, swap(other, 1)], axis=0)

    def by_token(rows):
        mine, other = rows[:tok_count], swap(rows[tok_count:], 1)
        return jnp.where(core == 0, jnp.stack([mine, other]), jnp.stack([other, mine]))[None]

    own_tokens = by_core(tokens[0])
    query_blocks = query_weight.reshape(shard_rows, chips, query_width).transpose(1, 0, 2)
    key_value = [
        jnp.repeat(a.reshape(shard_rows, KV_HEADS, HEAD_DIM).transpose(1, 0, 2), sharing, axis=0)
        for a in (key_weight, value_weight)
    ]
    mixer_blocks = jnp.concatenate([query_blocks] + key_value, axis=2)
    mixer_near = [one_of(mixer_blocks, me // 2 ^ j) for j in range(chips)]
    output_far = swap(output_weight, 1)
    own_tokens, output_far, *mixer_near = flow.until(own_tokens, output_far, *mixer_near)
    normed_own, inputs = norm_rows(mixer_gain, own_tokens)
    normed_own, gate_weight, up_weight = flow.until(normed_own, gate_weight, up_weight)
    normed_parts = gather_start(normed_own)
    mixer_near = [swap(piece, 2 * j) if j else piece for j, piece in enumerate(mixer_near)]

    feed_own = pick_blocks(me, side, gate_weight, up_weight, chips, range(1), False)[0]
    feed_away = pick_blocks(me, side, gate_weight, up_weight, chips, range(1, chips), True)
    feed_own, feed_away, *held = flow.until(feed_own, feed_away, *mixer_near, *normed_parts)
    mixer_near, normed_parts = jnp.stack(held[:chips]), held[chips:]
    held = flow.until(*swap_cores(mixer_near, 2), *gather_end(normed_parts))
    mixer_far, normed = joined(held[:2]), joined(held[2:])
    split = (chips + 1) // 2 + 1
    away = [swap(flow.after(feed_away[j - 1])[0], 2 * j) for j in range(1, chips)]
    (block_order,) = flow.after(block_order)
    info = positions(
        one_of(block_order[0], core), one_of(doc_ids[0], core), one_of(prefix_len[0], core), length
    )
    facts = jnp.stack(info).reshape(4, devices, tok_count)
    facts = jnp.stack([one_of(facts, me ^ p, 1) for p in range(devices)], axis=1)
    place, member, relative, limit = facts.reshape(4, length)
    rows = jnp.concatenate([jnp.stack([place, member, limit]), jnp.zeros((5, length), jnp.int32)])
    columns = jnp.stack([place, member], axis=1)
    angle = angles_for(relative)
    cosine, sine = jnp.cos(angle), jnp.sin(angle)
    cosine = jnp.concatenate([cosine] * 4, axis=1)
    sine = jnp.concatenate([-sine, sine, -sine, sine], axis=1)

    output_rows = both_cores(output_weight, output_far)
    mixer_columns = place_blocks(me, mixer_near, mixer_far)
    (normed,) = flow.after(normed)
    raw = product("rows", normed, mixer_columns, full)
    attended, query, kv, logs = attend(raw, cosine, sine, columns, rows)
    branch = product("rows", attended, output_rows, full)
    normed_other = swap_cores(normed, 2)
    held = flow.until(branch, *away, *normed_other)
    branch, away, normed_other = held[0], held[1:chips], joined(held[chips:])
    away = joined(away)
    other, away_far = swap_copies(away, 1), swap(away, 1)
    feed_own_far = swap(*flow.after(feed_own), 1)
    parts = flow.until(*scatter_end(scatter_start(flow.after(branch)[0])))
    normed_two_own, hidden = norm_rows(feed_gain, inputs, *parts)
    (normed_two_own,) = flow.until(normed_two_own)
    normed_two_parts = flow.until(*gather_start(normed_two_own))
    held = flow.until(other, away_far, feed_own_far, *gather_end(normed_two_parts))
    other, away_far, feed_own_far, normed_two = held[0], held[1], held[2], joined(held[3:])
    grad_rows = by_core(*flow.after(cotangent[0]))
    other_far, grad_rows = flow.until(swap(other, 1), grad_rows)
    (own, down_weight) = flow.after(grad_rows, down_weight)
    down_far = swap(down_weight, 1)
    cotangent_rows = (
        [own] + [swap(own, 2 * j) for j in range(1, chips)]
        if chips == 4
        else gather_end(gather_start(own))
    )
    normed_two_other = swap(flow.after(normed_two)[0], 1)
    feed_pieces = [([(0, None)], feed_own), ([(1, None)], feed_own_far)]
    for kind, array in enumerate((away, away_far, other, other_far)):
        feed_pieces.append(([(2 * j + kind % 2, kind // 2) for j in range(1, chips)], array))
    inner, both, feed_columns, normed_two_other, down_far, *held = flow.until(
        *feed_forward(me, side, normed_two, feed_pieces),
        normed_two_other,
        down_far,
        *cotangent_rows,
    )
    all_grad_rows = joined(held)
    down_all = both_cores(down_weight, down_far)

    down_partial = product("outer", inner, all_grad_rows, low).reshape(2, down_rows, width)
    came = swap_cores(one_of(down_partial, 1 - core), 2)
    down_all, *came = flow.until(down_all, *came)
    mine = [
        lax.dynamic_slice_in_dim(
            down_partial.reshape(2 * down_rows, width),
            core * down_rows + piece * (down_rows // 2),
            down_rows // 2,
            0,
        )
        for piece in range(2)
    ]
    down_parts = flow.until(
        *[(x.astype(full) + y.astype(full)).astype(low) for x, y in zip(mine, came)]
    )
    for piece in range(2):
        chain.add(("down", piece), down_parts[piece])
    chain.step()

    (grad_both,) = flow.until(feed_backward(*flow.after(all_grad_rows), down_all, both))
    grad_both_other = swap(grad_both, 1)
    partial_two = product("transpose", grad_both, feed_columns, full)
    (partial_two,) = flow.until(partial_two)
    chain.step()
    grad_both_other, *parts = flow.until(
        grad_both_other, *scatter_end(scatter_start(*flow.after(partial_two)))
    )
    picks = range(0, devices, 2)
    pieces = outer_blocks(
        me, normed_two, *flow.after(grad_both), normed_two_other, grad_both_other, picks
    )
    grad_branch_own, grad_hidden, feed_part = norm_back(
        feed_gain, hidden, grad_rows, *parts
    )
    held = flow.until(*pieces, *gather_start(grad_branch_own))
    pieces, parts = held[:chips], held[chips:]
    chain.add(("feed", 0), pieces[0])
    chain.step()
    grad_branch = joined(gather_end(flow.after(*parts)))
    output_partial = product("outer", attended, grad_branch, low)
    output_partial = output_partial.reshape(2, shard_rows, width)
    came = swap_cores(one_of(output_partial, 1 - core), 2)
    grad_attended = product("transpose", grad_branch, output_rows, low)
    grad_mixer = attend_back(query, kv, grad_attended, logs, cosine, sine, columns, rows)
    partial = product("transpose", grad_mixer, mixer_columns, full)
    grad_mixer_other = swap_cores(grad_mixer, 2)
    partial, grad_mixer, held, *came = flow.until(
        partial, grad_mixer, output_partial, *came, *grad_mixer_other
    )
    grad_mixer_other, came = joined(came[2:]), came[:2]
    output_part = (one_of(held, core).astype(full) + joined(came).astype(full)).astype(low)
    chain.add("output", output_part)
    chain.step()
    moved = {j: swap(flow.after(pieces[j])[0], 2 * j) for j in range(1, split)}
    mixer_pieces = outer_blocks(
        me, normed, *flow.after(grad_mixer), normed_other, grad_mixer_other, picks
    )
    held = flow.until(*mixer_pieces, *[moved[j] for j in range(1, split)])
    mixer_pieces, early = held[:chips], held[chips:]
    for j, piece in enumerate(early, 1):
        chain.add(("feed", j), piece)
    chain.step()
    parts = scatter_end(scatter_start(flow.after(partial)[0]))
    input_grad, _, mixer_part = norm_back(
        mixer_gain, inputs, flow.after(grad_hidden)[0], *flow.until(*parts)
    )
    (input_grad,) = flow.until(input_grad)
    chain.step()
    for _ in range(split - 3):
        chain.step()
    gains = jnp.concatenate([mixer_part, feed_part]).reshape(2, 8, width // 8)
    gains, *mixer_pieces = flow.after(gains, *mixer_pieces)
    bits = 1
    while bits < devices:
        gains = gains + swap(gains, bits)
        bits = 2 * bits
    gains, *mixer_pieces = flow.until(
        gains, *[swap(mixer_pieces[j], 2 * j) if j else mixer_pieces[j] for j in range(chips)]
    )
    chain.add("mixer", jnp.stack(mixer_pieces), gains)
    chain.step()
    late = [swap(flow.after(pieces[j])[0], 2 * j) for j in range(split, chips)]
    down = product("rows", *flow.after(inner), down_all, full)
    down, *late = flow.until(down, *late)
    for j, piece in enumerate(late, split):
        chain.add(("feed", j), piece)
    chain.step()
    for _ in range(chips - split - 1):
        chain.step()
    parts = flow.until(*scatter_start(flow.after(down)[0]))
    chain.step()
    parts = flow.until(*scatter_end(flow.after(*parts)))
    layer_out = by_token((hidden + sum(part.astype(full) for part in parts)).astype(low))
    input_grad = by_token(input_grad)
    chain.finish()
    results = chain.results
    down_grad = jnp.concatenate([results["down", piece][0] for piece in range(2)], axis=0)
    down_grad = down_grad.astype(full)
    output_grad = results["output"][0].astype(full)
    done = [results["feed", j][0] for j in range(chips)]
    if hidden_width % 128:
        stacked = jnp.stack(done)
        ordered = jnp.stack([one_of(stacked, me // 2 ^ j) for j in range(chips)])
        ordered = ordered.astype(full).reshape(chips, shard_rows, 2, hidden_width)
        gate_grad, up_grad = ordered.transpose(2, 1, 0, 3).reshape(2, shard_rows, -1)
    else:
        held = ()
        for j, piece in enumerate(done):
            held = spread(me, j, piece, chips, held)
        gate_grad, up_grad = held
    mixer_grads = results["mixer"][0]
    mixer_grads = jnp.stack([one_of(mixer_grads, me // 2 ^ j) for j in range(chips)])
    mixer_grads = mixer_grads.astype(full)
    query_grad = mixer_grads[:, :, :query_width].transpose(1, 0, 2).reshape(shard_rows, -1)
    shared = (
        mixer_grads[:, :, query_width:]
        .reshape(KV_HEADS, sharing, shard_rows, 2, HEAD_DIM)
        .sum(axis=1)
    )
    key_grad = shared[:, :, 0].transpose(1, 0, 2).reshape(shard_rows, -1)
    value_grad = shared[:, :, 1].transpose(1, 0, 2).reshape(shard_rows, -1)
    mixer_total, feed_total = results["mixer"][1].reshape(2, width)
    return (
        layer_out,
        input_grad,
        mixer_total,
        query_grad,
        key_grad,
        value_grad,
        output_grad,
        feed_total,
        gate_grad,
        up_grad,
        down_grad,
    )


def solution(mesh):
    placed = (
        P("rep", None, "fsdp", None),
        P("rep", None, "fsdp", None),
        P(),
        P("fsdp", None),
        P("fsdp", None),
        P("fsdp", None),
        P("fsdp", None),
        P(),
        P("fsdp", None),
        P("fsdp", None),
        P("fsdp", None),
        P("rep", None, None),
        P("rep", None, None),
        P("rep", None, None),
    )
    return jax.shard_map(
        local,
        mesh=mesh,
        in_specs=placed,
        out_specs=(
            P("rep", None, "fsdp", None),
            P("rep", None, "fsdp", None),
            P(),
            P("fsdp", None),
            P("fsdp", None),
            P("fsdp", None),
            P("fsdp", None),
            P(),
            P("fsdp", None),
            P("fsdp", None),
            P("fsdp", None),
        ),
        check_vma=False,
    )
```

```python
import functools

import jax
import jax.numpy as jnp
from jax import lax
from jax.experimental import pallas as pl
from jax.experimental.pallas import tpu as pltpu
from jax.sharding import PartitionSpec as P

HEADS = 32
KV_HEADS = 4
HEAD_DIM = 64
MICRO = 2
SEGS = 3


epsilon = 1e-05
FREE = pl.CostEstimate(flops=0, transcendentals=0, bytes_accessed=0)


def positions(order_row, doc_row, prefix_row, length):
    count = order_row.shape[0]
    block_width = length // count
    index = jnp.arange(length, dtype=jnp.int32)
    slot = index // block_width
    block = jnp.sum(
        jnp.where(
            slot[:, None] == jnp.arange(count, dtype=jnp.int32)[None, :], order_row[None, :], 0
        ),
        axis=1,
        dtype=jnp.int32,
    )
    place = block * block_width + index % block_width
    labels = jnp.arange(SEGS, dtype=jnp.int32)
    starts = jnp.sum(
        (doc_row[None, :] < labels[:, None]).astype(jnp.int32), axis=1, dtype=jnp.int32
    )
    member = jnp.sum(
        (place[:, None] >= starts[None, 1:]).astype(jnp.int32), axis=1, dtype=jnp.int32
    )
    picked = member[:, None] == labels[None, :]
    start_of = jnp.sum(jnp.where(picked, starts[None, :], 0), axis=1, dtype=jnp.int32)
    limit = jnp.sum(
        jnp.where(picked, starts[None, :] + prefix_row[None, :], 0), axis=1, dtype=jnp.int32
    )
    return (place, member, place - start_of, limit)


def angles_for(relative):
    halfway = HEAD_DIM // 2
    frequency = 10000.0 ** (-(2.0 * jnp.arange(halfway, dtype=jnp.float32)) / HEAD_DIM)
    return relative.astype(jnp.float32)[:, None] * frequency[None, :]


def rms_scale(values, gain):
    return values * lax.rsqrt(jnp.mean(values * values, axis=1, keepdims=True) + epsilon) * gain


def gated(gate_part, up_part):
    return jax.nn.silu(gate_part) * up_part


def contract_rows(left, right):
    return lax.dot_general(
        left, right, (((0,), (0,)), ((), ())), preferred_element_type=jnp.float32
    )


def times_transpose(left, right):
    return lax.dot_general(
        left, right, (((1,), (1,)), ((), ())), preferred_element_type=jnp.float32
    )


def dot_rows(left, right):
    return jnp.dot(left, right, preferred_element_type=jnp.float32)


def turn(field, cosine, sine):
    lane = lax.broadcasted_iota(jnp.int32, field.shape, 1) % HEAD_DIM
    half = HEAD_DIM // 2
    swapped = jnp.where(
        lane < half, pltpu.roll(field, 2 * HEAD_DIM - half, 1), pltpu.roll(field, half, 1)
    )
    return field * cosine + swapped * sine


def seen(columns, rows):
    place_q, member_q = columns[:, 0:1], columns[:, 1:2]
    place_k, member_k, limit_k = rows[0:1, :], rows[1:2, :], rows[2:3, :]
    return (member_q == member_k) & ((place_k <= place_q) | (place_k < limit_k))


def attend_kernel(raw_ref, cos_ref, sin_ref, column_ref, row_ref, out_ref, query_ref, kv_ref, log_ref):
    scale = HEAD_DIM ** (-0.5)
    cosine, sine = cos_ref[...], sin_ref[...]
    visible = seen(column_ref[...], row_ref[...])
    wide = 2 * HEAD_DIM
    pair_count = raw_ref.shape[1] // wide - 1
    first = lax.broadcasted_iota(jnp.int32, cosine.shape, 1) < HEAD_DIM
    kv = raw_ref[:, pair_count * wide :]
    keys_values = jnp.where(first, turn(kv, cosine, sine), kv)
    swapped = pltpu.roll(keys_values, HEAD_DIM, 1)
    keys = jnp.where(first, keys_values, swapped).astype(jnp.bfloat16)
    values = jnp.where(first, swapped, keys_values).astype(jnp.bfloat16)
    kv_ref[...] = keys_values.astype(jnp.bfloat16)
    logs = jnp.zeros(cosine.shape, jnp.float32)
    lanes = lax.broadcasted_iota(jnp.int32, cosine.shape, 1)
    for pair in range(pair_count):
        at = slice(pair * wide, (pair + 1) * wide)
        query = turn(raw_ref[:, at], cosine, sine).astype(jnp.bfloat16)
        query_ref[:, at] = query
        results = []
        for member in range(2):
            chosen = first if member == 0 else jnp.logical_not(first)
            one = jnp.where(chosen, query, jnp.zeros_like(query))
            scores = (
                lax.dot_general(
                    one, keys, (((1,), (1,)), ((), ())), preferred_element_type=jnp.float32
                )
                * scale
            )
            scores = jnp.where(visible, scores, -1000000000.0)
            peak = jnp.max(scores, axis=1, keepdims=True)
            raised = jnp.exp(scores - peak)
            totals = jnp.sum(raised, axis=1, keepdims=True)
            probs = (raised * (1.0 / totals)).astype(jnp.bfloat16)
            results.append(dot_rows(probs, values))
            logs = jnp.where(lanes == 2 * pair + member, peak + jnp.log(totals), logs)
        out_ref[:, at] = jnp.where(first, results[0], results[1]).astype(jnp.bfloat16)
    log_ref[...] = logs


def attend_back_kernel(
    query_ref, kv_ref, grad_ref, log_ref, cos_ref, sin_ref, column_ref, row_ref, out_ref
):
    scale = HEAD_DIM ** (-0.5)
    cosine, sine = cos_ref[...], sin_ref[...]
    visible = seen(column_ref[...], row_ref[...])
    wide = 2 * HEAD_DIM
    pair_count = query_ref.shape[1] // wide
    first = lax.broadcasted_iota(jnp.int32, cosine.shape, 1) < HEAD_DIM
    lanes = lax.broadcasted_iota(jnp.int32, cosine.shape, 1)
    keys_values = kv_ref[...]
    swapped = pltpu.roll(keys_values.astype(jnp.float32), HEAD_DIM, 1).astype(jnp.bfloat16)
    keys = jnp.where(first, keys_values, swapped)
    values = jnp.where(first, swapped, keys_values)
    logs = log_ref[...]
    grad_keys = jnp.zeros(cosine.shape, jnp.float32)
    grad_values = jnp.zeros(cosine.shape, jnp.float32)
    for pair in range(pair_count):
        at = slice(pair * wide, (pair + 1) * wide)
        query, grad = query_ref[:, at], grad_ref[:, at]
        results = []
        for member in range(2):
            chosen = first if member == 0 else jnp.logical_not(first)
            one = jnp.where(chosen, query, jnp.zeros_like(query))
            grad_one = jnp.where(chosen, grad, jnp.zeros_like(grad))
            log_one = jnp.sum(
                jnp.where(lanes == 2 * pair + member, logs, 0.0), axis=1, keepdims=True
            )
            scores = (
                lax.dot_general(
                    one, keys, (((1,), (1,)), ((), ())), preferred_element_type=jnp.float32
                )
                * scale
            )
            probs = jnp.exp(jnp.where(visible, scores, -1000000000.0) - log_one)
            grad_probs = lax.dot_general(
                grad_one, values, (((1,), (1,)), ((), ())), preferred_element_type=jnp.float32
            )
            inner_sum = jnp.sum(probs * grad_probs, axis=1, keepdims=True)
            grad_scores = (probs * (grad_probs - inner_sum)).astype(jnp.bfloat16)
            results.append(dot_rows(grad_scores, keys) * scale)
            grad_keys = grad_keys + contract_rows(grad_scores, one)
            grad_values = grad_values + contract_rows(probs.astype(jnp.bfloat16), grad_one)
        joined = jnp.where(first, results[0], results[1])
        out_ref[:, at] = turn(joined, cosine, -sine).astype(jnp.bfloat16)
    grad_keys = (grad_keys + pltpu.roll(grad_keys, HEAD_DIM, 1)) * scale
    grad_values = grad_values + pltpu.roll(grad_values, HEAD_DIM, 1)
    last = jnp.where(first, turn(grad_keys, cosine, -sine), grad_values)
    out_ref[:, pair_count * wide :] = last.astype(jnp.bfloat16)


def whole(*_):
    return (0, 0)


def whole_specs(arrays):
    return [pl.BlockSpec(a.shape, whole) for a in arrays]


def attend(raw, cosine, sine, columns, rows):
    length, wide = raw.shape
    query_width = wide - 2 * HEAD_DIM
    heads = query_width // HEAD_DIM
    outs = [
        jax.ShapeDtypeStruct((length, query_width), jnp.bfloat16),
        jax.ShapeDtypeStruct((length, query_width), jnp.bfloat16),
        jax.ShapeDtypeStruct((length, 2 * HEAD_DIM), jnp.bfloat16),
        jax.ShapeDtypeStruct((length, 2 * HEAD_DIM), jnp.float32),
    ]
    args = (raw, cosine, sine, columns, rows)
    return pl.pallas_call(
        attend_kernel,
        grid=(1,),
        in_specs=whole_specs(args),
        out_specs=whole_specs(outs),
        out_shape=outs,
        compiler_params=pltpu.CompilerParams(vmem_limit_bytes=48 * 1024 * 1024),
        cost_estimate=FREE,
        name="attend",
    )(*args)


def attend_back(query, kv, grad, logs, cosine, sine, columns, rows):
    length, query_width = query.shape
    heads = query_width // HEAD_DIM
    out = jax.ShapeDtypeStruct((length, query_width + 2 * HEAD_DIM), jnp.bfloat16)
    args = (query, kv, grad, logs, cosine, sine, columns, rows)
    return pl.pallas_call(
        attend_back_kernel,
        grid=(1,),
        in_specs=whole_specs(args),
        out_specs=pl.BlockSpec(out.shape, whole),
        out_shape=out,
        compiler_params=pltpu.CompilerParams(vmem_limit_bytes=48 * 1024 * 1024),
        cost_estimate=FREE,
        name="attend_back",
    )(*args)


def total_of(refs):
    total = refs[0][...].astype(jnp.float32)
    for ref in refs[1:]:
        total = total + ref[...].astype(jnp.float32)
    return total


def norm_kernel(gain_ref, *refs):
    low_ref, full_ref = refs[-2:]
    rows = total_of(refs[:-2])
    scale = lax.rsqrt(jnp.mean(rows * rows, axis=1, keepdims=True) + epsilon)
    full_ref[...] = rows
    low_ref[...] = (rows * scale * gain_ref[...].astype(jnp.float32)).astype(low_ref.dtype)


def norm_rows(gain, *parts):
    shape = parts[0].shape
    args = (gain.reshape(1, -1),) + parts
    outs = [jax.ShapeDtypeStruct(shape, jnp.bfloat16), jax.ShapeDtypeStruct(shape, jnp.float32)]
    return pl.pallas_call(
        norm_kernel,
        grid=(1,),
        in_specs=whole_specs(args),
        out_specs=whole_specs(outs),
        out_shape=outs,
        compiler_params=pltpu.CompilerParams(vmem_limit_bytes=32 * 1024 * 1024),
        cost_estimate=FREE,
        name="norm_rows",
    )(*args)


def norm_back_kernel(gain_ref, rows_ref, base_ref, *refs):
    low_ref, full_ref, gain_grad_ref = refs[-3:]
    rows, grad = rows_ref[...], total_of(refs[:-3])
    scale = lax.rsqrt(jnp.mean(rows * rows, axis=1, keepdims=True) + epsilon)
    gain_grad_ref[...] = jnp.sum(grad * rows * scale, axis=0, keepdims=True)
    inside = grad * gain_ref[...].astype(jnp.float32)
    slope = jnp.mean(inside * rows, axis=1, keepdims=True)
    result = base_ref[...].astype(jnp.float32) + scale * inside - rows * (scale**3 * slope)
    full_ref[...] = result
    low_ref[...] = result.astype(low_ref.dtype)


def norm_back(gain, rows, base, *parts):
    shape = rows.shape
    args = (gain.reshape(1, -1), rows, base) + parts
    outs = [
        jax.ShapeDtypeStruct(shape, jnp.bfloat16),
        jax.ShapeDtypeStruct(shape, jnp.float32),
        jax.ShapeDtypeStruct((1, shape[1]), jnp.float32),
    ]
    return pl.pallas_call(
        norm_back_kernel,
        grid=(1,),
        in_specs=whole_specs(args),
        out_specs=whole_specs(outs),
        out_shape=outs,
        compiler_params=pltpu.CompilerParams(vmem_limit_bytes=32 * 1024 * 1024),
        cost_estimate=FREE,
        name="norm_back",
    )(*args)


def pick_kernel(place_ref, gate_ref, up_ref, out_ref):
    for at in range(0, gate_ref.shape[1], 128):
        out_ref[0, :, 2 * at : 2 * at + 128] = gate_ref[:, at : at + 128]
        out_ref[0, :, 2 * at + 128 : 2 * at + 256] = up_ref[:, at : at + 128]


def pick_blocks(me, side, gate, up, chips, picks, halved):
    rows, total = gate.shape
    width = total // chips
    if halved:
        rows = rows // 2
    if width % 128:
        both = jnp.concatenate(
            [a.reshape(a.shape[0], chips, width).transpose(1, 0, 2) for a in (gate, up)], axis=2
        )
        if halved:
            both = lax.dynamic_slice_in_dim(both, side * rows, rows, 1)
        return jnp.stack(
            [lax.dynamic_index_in_dim(both, me // 2 ^ j, 0, keepdims=False) for j in picks]
        )
    first = picks[0]
    column = pl.BlockSpec(
        (rows, width), lambda s, place: (place[1] if halved else 0, place[0] // 2 ^ (s + first))
    )
    return pl.pallas_call(
        pick_kernel,
        grid_spec=pltpu.PrefetchScalarGridSpec(
            num_scalar_prefetch=1,
            grid=(len(picks),),
            in_specs=[column, column],
            out_specs=pl.BlockSpec((1, rows, 2 * width), lambda s, place: (s, 0, 0)),
        ),
        out_shape=jax.ShapeDtypeStruct((len(picks), rows, 2 * width), gate.dtype),
        compiler_params=pltpu.CompilerParams(vmem_limit_bytes=16 * 1024 * 1024),
        cost_estimate=FREE,
        name="pick_blocks",
    )(jnp.stack([me, side]), gate, up)


def tile_of(width):
    return 128 if width % 128 == 0 else width


def forward_kernel(place_ref, rows_ref, *refs, marks, shard):
    inner_ref, both_ref, weight_ref = refs[len(marks) :]
    for group, piece_ref in zip(marks, refs):
        count = piece_ref.shape[0] // len(group)
        for at, (p, flip) in enumerate(group):
            start = (place_ref[0] ^ p) * shard
            if flip is not None:
                start = start + (place_ref[1] ^ flip) * count
            weight_ref[pl.ds(pl.multiple_of(start, count), count), :] = piece_ref[
                at * count : (at + 1) * count, :
            ]
    both = dot_rows(rows_ref[...], weight_ref[...])
    half = both.shape[1] // 2
    gate, upward = both[:, :half], both[:, half:]
    both_ref[...] = both
    inner_ref[...] = (gate / (1.0 + jnp.exp(-gate)) * upward).astype(inner_ref.dtype)


def feed_forward(me, side, rows, pieces):
    count, width = rows.shape
    columns = pieces[0][1].shape[1]
    hidden = columns // 2
    tile = tile_of(hidden)
    marks = [mark for mark, _ in pieces]
    arrays = [piece for _, piece in pieces]
    outs = [
        jax.ShapeDtypeStruct((count, hidden), jnp.bfloat16),
        jax.ShapeDtypeStruct((count, columns), jnp.float32),
        jax.ShapeDtypeStruct((width, columns), jnp.bfloat16),
    ]
    return pl.pallas_call(
        functools.partial(
            forward_kernel, marks=marks, shard=width // lax.axis_size("fsdp")
        ),
        grid_spec=pltpu.PrefetchScalarGridSpec(
            num_scalar_prefetch=1,
            grid=(hidden // tile,),
            in_specs=[pl.BlockSpec((count, width), lambda s, place: (0, 0))]
            + [pl.BlockSpec((a.shape[0], 2 * tile), lambda s, place: (0, s)) for a in arrays],
            out_specs=[
                pl.BlockSpec((count, tile), lambda s, place: (0, s)),
                pl.BlockSpec((count, 2 * tile), lambda s, place: (0, s)),
                pl.BlockSpec((width, 2 * tile), lambda s, place: (0, s)),
            ],
        ),
        out_shape=outs,
        compiler_params=pltpu.CompilerParams(vmem_limit_bytes=48 * 1024 * 1024),
        cost_estimate=FREE,
        name="feed_forward",
    )(jnp.stack([me, side]), rows, *arrays)


def backward_kernel(grad_ref, weight_ref, both_ref, out_ref):
    grad = times_transpose(grad_ref[...], weight_ref[...])
    half = both_ref.shape[1] // 2
    gate, upward = both_ref[:, :half], both_ref[:, half:]
    sigmoid = 1.0 / (1.0 + jnp.exp(-gate))
    silu = gate * sigmoid
    out_ref[:, :half] = (
        grad * upward * (sigmoid + silu * (1.0 - sigmoid))
    ).astype(out_ref.dtype)
    out_ref[:, half:] = (grad * silu).astype(out_ref.dtype)


def feed_backward(grad_rows, weight, both):
    count, width = grad_rows.shape
    hidden = weight.shape[0]
    tile = tile_of(hidden)
    return pl.pallas_call(
        backward_kernel,
        grid=(hidden // tile,),
        in_specs=[
            pl.BlockSpec((count, width), lambda s: (0, 0)),
            pl.BlockSpec((tile, width), lambda s: (s, 0)),
            pl.BlockSpec((count, 2 * tile), lambda s: (0, s)),
        ],
        out_specs=pl.BlockSpec((count, 2 * tile), lambda s: (0, s)),
        out_shape=jax.ShapeDtypeStruct((count, 2 * hidden), jnp.bfloat16),
        compiler_params=pltpu.CompilerParams(vmem_limit_bytes=40 * 1024 * 1024),
        cost_estimate=FREE,
        name="feed_backward",
    )(grad_rows, weight, both)


def product_kernel(left_ref, right_ref, out_ref, *, kind):
    multiply = {"rows": dot_rows, "transpose": times_transpose, "outer": contract_rows}[kind]
    out_ref[...] = multiply(left_ref[...], right_ref[...]).astype(out_ref.dtype)


def product(kind, left, right, dtype):
    rows = left.shape[1 if kind == "outer" else 0]
    columns = right.shape[0 if kind == "transpose" else 1]
    tile = 256 if columns % 256 == 0 else 128
    right_spec = (
        pl.BlockSpec((tile, right.shape[1]), lambda s: (s, 0))
        if kind == "transpose"
        else pl.BlockSpec((right.shape[0], tile), lambda s: (0, s))
    )
    return pl.pallas_call(
        functools.partial(product_kernel, kind=kind),
        grid=(columns // tile,),
        in_specs=[pl.BlockSpec(left.shape, lambda s: (0, 0)), right_spec],
        out_specs=pl.BlockSpec((rows, tile), lambda s: (0, s)),
        out_shape=jax.ShapeDtypeStruct((rows, columns), dtype),
        compiler_params=pltpu.CompilerParams(vmem_limit_bytes=40 * 1024 * 1024),
        cost_estimate=FREE,
        name="product_" + kind,
    )(left, right)


def down_kernel(place_ref, left_ref, right_ref, *refs):
    out_refs, total_ref = refs[:-1], refs[-1]
    total_ref[...] = contract_rows(left_ref[...], right_ref[...])
    rows = out_refs[0].shape[0]
    for at, out_ref in enumerate(out_refs):
        core = place_ref[0] if at < 2 else 1 - place_ref[0]
        start = pl.multiple_of(core * (2 * rows) + at % 2 * rows, 16)
        out_ref[...] = total_ref[pl.ds(start, rows), :].astype(out_ref.dtype)


def down_products(core, left, right):
    rows, width = left.shape[1], right.shape[1]
    part, tile = rows // 4, 256
    return pl.pallas_call(
        down_kernel,
        grid_spec=pltpu.PrefetchScalarGridSpec(
            num_scalar_prefetch=1,
            grid=(width // tile,),
            in_specs=[
                pl.BlockSpec(left.shape, lambda s, place: (0, 0)),
                pl.BlockSpec((right.shape[0], tile), lambda s, place: (0, s)),
            ],
            out_specs=[pl.BlockSpec((part, tile), lambda s, place: (0, s))] * 4,
            scratch_shapes=[pltpu.VMEM((rows, tile), jnp.float32)],
        ),
        out_shape=[jax.ShapeDtypeStruct((part, width), jnp.bfloat16)] * 4,
        compiler_params=pltpu.CompilerParams(vmem_limit_bytes=40 * 1024 * 1024),
        cost_estimate=FREE,
        name="down_products",
    )(core.reshape(1), left, right)


def outer_kernel(place_ref, left_ref, right_ref, left_other_ref, right_other_ref, *out_refs):
    total = contract_rows(left_ref[...], right_ref[...])
    total = total + contract_rows(left_other_ref[...], right_other_ref[...])
    for at, out_ref in enumerate(out_refs):

        @pl.when(pl.program_id(0) == at)
        def _():
            out_ref[...] = total.astype(out_ref.dtype)


def outer_blocks(me, left, right, left_other, right_other, picks):
    tokens, width = right.shape
    rows = left.shape[1] // lax.axis_size("fsdp")
    first = picks[0]
    jump = picks[1] - first if len(picks) > 1 else 1
    column = pl.BlockSpec((tokens, rows), lambda s, place: (0, place[0] ^ (first + jump * s)))
    full = pl.BlockSpec((tokens, width), lambda s, place: (0, 0))
    block = pl.BlockSpec((rows, width), lambda s, place: (0, 0))
    return pl.pallas_call(
        outer_kernel,
        grid_spec=pltpu.PrefetchScalarGridSpec(
            num_scalar_prefetch=1,
            grid=(len(picks),),
            in_specs=[column, full, column, full],
            out_specs=[block] * len(picks),
        ),
        out_shape=[jax.ShapeDtypeStruct((rows, width), jnp.bfloat16)] * len(picks),
        compiler_params=pltpu.CompilerParams(vmem_limit_bytes=48 * 1024 * 1024),
        cost_estimate=FREE,
        name="outer_blocks",
    )(me.reshape(1), left, right, left_other, right_other)


def place_kernel(place_ref, near_ref, far_ref, out_ref):
    @pl.when(pl.program_id(1) == 0)
    def _():
        out_ref[...] = near_ref[...]

    @pl.when(pl.program_id(1) == 1)
    def _():
        out_ref[...] = far_ref[...]


def place_blocks(me, near, far):
    chips, rows, width = near.shape
    block = pl.BlockSpec((1, rows, width), lambda j, b, place: (j, 0, 0))
    return pl.pallas_call(
        place_kernel,
        grid_spec=pltpu.PrefetchScalarGridSpec(
            num_scalar_prefetch=1,
            grid=(chips, 2),
            in_specs=[block, block],
            out_specs=pl.BlockSpec(
                (1, rows, width), lambda j, b, place: (place[0] ^ (2 * j + b), 0, 0)
            ),
        ),
        out_shape=jax.ShapeDtypeStruct((2 * chips, rows, width), near.dtype),
        compiler_params=pltpu.CompilerParams(vmem_limit_bytes=16 * 1024 * 1024),
        cost_estimate=FREE,
        name="place_blocks",
    )(me.reshape(1), near, far).reshape(2 * chips * rows, width)


def spread_first(place_ref, piece_ref, gate_ref, up_ref):
    for at in range(0, gate_ref.shape[1], 128):
        gate_ref[:, at : at + 128] = piece_ref[:, 2 * at : 2 * at + 128].astype(jnp.float32)
        up_ref[:, at : at + 128] = piece_ref[:, 2 * at + 128 : 2 * at + 256].astype(jnp.float32)


def spread_next(place_ref, piece_ref, gate_in, up_in, gate_ref, up_ref):
    spread_first(place_ref, piece_ref, gate_ref, up_ref)


def spread(me, j, piece, chips, held):
    rows, both = piece.shape
    width = both // 2
    out = jax.ShapeDtypeStruct((rows, width * chips), jnp.float32)
    column = pl.BlockSpec((rows, width), lambda s, place: (0, place[0] // 2 ^ j))
    anywhere = pl.BlockSpec(memory_space=pl.ANY)
    return pl.pallas_call(
        spread_next if held else spread_first,
        grid_spec=pltpu.PrefetchScalarGridSpec(
            num_scalar_prefetch=1,
            grid=(1,),
            in_specs=[pl.BlockSpec((rows, both), lambda s, place: (0, 0))]
            + [anywhere] * len(held),
            out_specs=[column, column],
        ),
        out_shape=[out, out],
        input_output_aliases={2: 0, 3: 1} if held else {},
        compiler_params=pltpu.CompilerParams(vmem_limit_bytes=24 * 1024 * 1024),
        cost_estimate=FREE,
        name="spread",
    )(me.reshape(1), piece, *held)


class Flow:
    def __init__(self, token):
        self.token = token

    def after(self, *arrays):
        return lax.optimization_barrier((self.token,) + tuple(arrays))[1:]

    def until(self, *arrays):
        held = lax.optimization_barrier((self.token,) + tuple(arrays))
        self.token = held[0]
        return held[1:]


class Chain:
    def __init__(self, flow, copies, index):
        self.flow, self.copies, self.index = flow, copies, index
        half = copies // 2
        ends = [(s, copies - 1 - s) for s in range(half - 1)]
        self.stages = [([(a, a + 1), (b, b - 1)], None) for a, b in ends]
        self.stages.append(([(half - 1, half), (half, half - 1)], None))
        self.stages += [([(a + 1, a), (b - 1, b)], (a, b)) for a, b in reversed(ends)]
        self.waiting, self.moving, self.results = [], [], {}

    def add(self, name, *parts):
        self.waiting.append((name, parts))

    def start(self, parts, stage):
        return [lax.ppermute(part, "rep", self.stages[stage][0]) for part in parts]

    def step(self):
        moving, self.moving = self.moving, []
        if self.waiting:
            name, parts = self.waiting.pop(0)
            parts = self.flow.after(*parts)
            self.moving.append((name, parts, self.start(parts, 0), 0))
        if not moving:
            return
        arrived = iter(self.flow.until(*[array for item in moving for array in item[2]]))
        summed = []
        for name, parts, came, stage in moving:
            came = [next(arrived) for _ in came]
            outer = self.stages[stage][1]
            if outer is None:
                parts = [
                    (a.astype(jnp.float32) + b.astype(jnp.float32)).astype(a.dtype)
                    for a, b in zip(parts, came)
                ]
            else:
                here = (self.index == outer[0]) | (self.index == outer[1])
                parts = [jnp.where(here, b, a) for a, b in zip(parts, came)]
            if stage + 1 == len(self.stages):
                self.results[name] = parts
            else:
                summed.append((name, parts, stage + 1))
        for name, parts, stage in summed:
            self.moving.append((name, parts, self.start(parts, stage), stage))

    def finish(self):
        while self.waiting or self.moving:
            self.step()


def local(
    tokens,
    cotangent,
    mixer_gain,
    query_weight,
    key_weight,
    value_weight,
    output_weight,
    feed_gain,
    gate_weight,
    up_weight,
    down_weight,
    doc_ids,
    prefix_len,
    block_order,
):
    tok_count, width = tokens.shape[2:]
    devices = lax.axis_size("fsdp")
    chips = devices // 2
    copies = lax.axis_size("rep")
    me = lax.axis_index("fsdp")
    core = me % 2
    copy_index = lax.axis_index("rep")
    side = copy_index % 2
    length = tok_count * devices
    shard_rows = width // devices
    half_shard = shard_rows // 2
    query_width = HEADS // chips * HEAD_DIM
    sharing = max(1, chips // KV_HEADS)
    down_rows = down_weight.shape[0]
    hidden_width = 2 * down_rows
    low = jnp.bfloat16
    full = jnp.float32
    flow = Flow(jnp.zeros((8, 128), full) + copy_index.astype(full))
    chain = Chain(flow, copies, copy_index)

    def swap(array, bits):
        return lax.ppermute(array, "fsdp", [(d, d ^ bits) for d in range(devices)])

    def swap_copies(array, bits):
        return lax.ppermute(array, "rep", [(d, d ^ bits) for d in range(copies)])

    def one_of(array, index, axis=0):
        return lax.dynamic_index_in_dim(array, index, axis, keepdims=False)

    def both_cores(mine, other):
        return place_blocks(core, mine[None], other[None])

    def gather_start(own):
        return (own, swap(own, 2), swap(own, 4)) if chips == 4 else (own,)

    def gather_end(parts):
        if chips == 4:
            own, along_x, along_y = parts
            mid = own.shape[0] // 2
            return [own, along_x, along_y, swap(along_y[:mid], 2), swap(along_x[mid:], 4)]
        (own,) = parts
        bits = 2
        while bits < devices:
            own = jnp.concatenate([own, swap(own, bits)], axis=0)
            bits = 2 * bits
        return [own]

    def joined(parts):
        return jnp.concatenate(parts, axis=0) if len(parts) > 1 else parts[0]

    def scatter_start(partial):
        if chips != 4:
            return (partial,)
        mine, to_x, to_y, across = jnp.split(partial, 4, axis=0)
        mid = mine.shape[0] // 2
        across = across.astype(low)
        return mine, to_x, to_y, swap(across[:mid], 2), swap(across[mid:], 4)

    def scatter_end(parts):
        if chips == 4:
            mine, to_x, to_y, from_x, from_y = parts
            mid = mine.shape[0] // 2
            to_x = jnp.concatenate([to_x[:mid], to_x[mid:] + from_y.astype(full)], axis=0)
            to_y = jnp.concatenate([to_y[:mid] + from_x.astype(full), to_y[mid:]], axis=0)
            came_x, came_y = swap(to_x.astype(low), 2), swap(to_y.astype(low), 4)
            return mine, came_x, came_y
        (partial,) = parts
        bits = devices // 2
        while bits > 1:
            rows = partial.shape[0] // 2
            partial = partial[:rows] + swap(partial[rows:].astype(low), bits).astype(full)
            bits = bits // 2
        return (partial,)

    def swap_cores(array, pieces):
        rows = array.shape[0] // pieces
        return [swap(array[at * rows : (at + 1) * rows], 1) for at in range(pieces)]

    def by_core(array):
        mine, other = one_of(array, core), one_of(array, 1 - core)
        return jnp.concatenate([mine, swap(other, 1)], axis=0)

    def by_token(rows):
        mine, other = rows[:tok_count], swap(rows[tok_count:], 1)
        return jnp.where(core == 0, jnp.stack([mine, other]), jnp.stack([other, mine]))[None]

    own_tokens = by_core(tokens[0])
    query_blocks = query_weight.reshape(shard_rows, chips, query_width).transpose(1, 0, 2)
    key_value = [
        jnp.repeat(a.reshape(shard_rows, KV_HEADS, HEAD_DIM).transpose(1, 0, 2), sharing, axis=0)
        for a in (key_weight, value_weight)
    ]
    mixer_blocks = jnp.concatenate([query_blocks] + key_value, axis=2)
    mixer_near = [one_of(mixer_blocks, me // 2 ^ j) for j in range(chips)]
    output_far = swap(output_weight, 1)
    own_tokens, output_far, *mixer_near = flow.until(own_tokens, output_far, *mixer_near)
    normed_own, inputs = norm_rows(mixer_gain, own_tokens)
    normed_own, gate_weight, up_weight = flow.until(normed_own, gate_weight, up_weight)
    normed_parts = gather_start(normed_own)
    mixer_near = [swap(piece, 2 * j) if j else piece for j, piece in enumerate(mixer_near)]

    feed_own = pick_blocks(me, side, gate_weight, up_weight, chips, range(1), False)[0]
    feed_away = pick_blocks(me, side, gate_weight, up_weight, chips, range(1, chips), True)
    feed_own, feed_away, *held = flow.until(feed_own, feed_away, *mixer_near, *normed_parts)
    mixer_near, normed_parts = jnp.stack(held[:chips]), held[chips:]
    held = flow.until(*swap_cores(mixer_near, 2), *gather_end(normed_parts))
    mixer_far, normed = joined(held[:2]), joined(held[2:])
    split = (chips + 1) // 2 + 1
    away = [swap(flow.after(feed_away[j - 1])[0], 2 * j) for j in range(1, chips)]
    (block_order,) = flow.after(block_order)
    info = positions(
        one_of(block_order[0], core), one_of(doc_ids[0], core), one_of(prefix_len[0], core), length
    )
    facts = jnp.stack(info).reshape(4, devices, tok_count)
    facts = jnp.stack([one_of(facts, me ^ p, 1) for p in range(devices)], axis=1)
    place, member, relative, limit = facts.reshape(4, length)
    rows = jnp.concatenate([jnp.stack([place, member, limit]), jnp.zeros((5, length), jnp.int32)])
    columns = jnp.stack([place, member], axis=1)
    angle = angles_for(relative)
    cosine, sine = jnp.cos(angle), jnp.sin(angle)
    cosine = jnp.concatenate([cosine] * 4, axis=1)
    sine = jnp.concatenate([-sine, sine, -sine, sine], axis=1)

    output_rows = both_cores(output_weight, output_far)
    mixer_columns = place_blocks(me, mixer_near, mixer_far)
    (normed,) = flow.after(normed)
    raw = product("rows", normed, mixer_columns, full)
    attended, query, kv, logs = attend(raw, cosine, sine, columns, rows)
    branch = product("rows", attended, output_rows, full)
    normed_other = swap_cores(normed, 2)
    held = flow.until(branch, *away, *normed_other)
    branch, away, normed_other = held[0], held[1:chips], joined(held[chips:])
    away = joined(away)
    other, away_far = swap_copies(away, 1), swap(away, 1)
    feed_own_far = swap(*flow.after(feed_own), 1)
    parts = flow.until(*scatter_end(scatter_start(flow.after(branch)[0])))
    normed_two_own, hidden = norm_rows(feed_gain, inputs, *parts)
    (normed_two_own,) = flow.until(normed_two_own)
    normed_two_parts = flow.until(*gather_start(normed_two_own))
    held = flow.until(other, away_far, feed_own_far, *gather_end(normed_two_parts))
    other, away_far, feed_own_far, normed_two = held[0], held[1], held[2], joined(held[3:])
    grad_rows = by_core(*flow.after(cotangent[0]))
    other_far, grad_rows = flow.until(swap(other, 1), grad_rows)
    (own, down_weight) = flow.after(grad_rows, down_weight)
    down_far = swap(down_weight, 1)
    cotangent_rows = (
        [own] + [swap(own, 2 * j) for j in range(1, chips)]
        if chips == 4
        else gather_end(gather_start(own))
    )
    normed_two_other = swap(flow.after(normed_two)[0], 1)
    feed_pieces = [([(0, None)], feed_own), ([(1, None)], feed_own_far)]
    for kind, array in enumerate((away, away_far, other, other_far)):
        feed_pieces.append(([(2 * j + kind % 2, kind // 2) for j in range(1, chips)], array))
    inner, both, feed_columns, normed_two_other, down_far, *held = flow.until(
        *feed_forward(me, side, normed_two, feed_pieces),
        normed_two_other,
        down_far,
        *cotangent_rows,
    )
    all_grad_rows = joined(held)
    down_all = both_cores(down_weight, down_far)

    *mine, first, second = down_products(core, inner, all_grad_rows)
    down_all, *came = flow.until(down_all, swap(first, 1), swap(second, 1))
    down_parts = flow.until(
        *[(x.astype(full) + y.astype(full)).astype(low) for x, y in zip(mine, came)]
    )
    for piece in range(2):
        chain.add(("down", piece), down_parts[piece])
    chain.step()

    (grad_both,) = flow.until(feed_backward(*flow.after(all_grad_rows), down_all, both))
    grad_both_other = swap(grad_both, 1)
    partial_two = product("transpose", grad_both, feed_columns, full)
    (partial_two,) = flow.until(partial_two)
    chain.step()
    grad_both_other, *parts = flow.until(
        grad_both_other, *scatter_end(scatter_start(*flow.after(partial_two)))
    )
    picks = range(0, devices, 2)
    pieces = outer_blocks(
        me, normed_two, *flow.after(grad_both), normed_two_other, grad_both_other, picks
    )
    grad_branch_own, grad_hidden, feed_part = norm_back(
        feed_gain, hidden, grad_rows, *parts
    )
    held = flow.until(*pieces, *gather_start(grad_branch_own))
    pieces, parts = held[:chips], held[chips:]
    chain.add(("feed", 0), pieces[0])
    chain.step()
    grad_branch = joined(gather_end(flow.after(*parts)))
    output_partial = product("outer", attended, grad_branch, low)
    output_partial = output_partial.reshape(2, shard_rows, width)
    came = swap_cores(one_of(output_partial, 1 - core), 2)
    grad_attended = product("transpose", grad_branch, output_rows, low)
    grad_mixer = attend_back(query, kv, grad_attended, logs, cosine, sine, columns, rows)
    partial = product("transpose", grad_mixer, mixer_columns, full)
    grad_mixer_other = swap_cores(grad_mixer, 2)
    partial, grad_mixer, held, *came = flow.until(
        partial, grad_mixer, output_partial, *came, *grad_mixer_other
    )
    grad_mixer_other, came = joined(came[2:]), came[:2]
    output_part = (one_of(held, core).astype(full) + joined(came).astype(full)).astype(low)
    chain.add("output", output_part)
    chain.step()
    moved = {j: swap(flow.after(pieces[j])[0], 2 * j) for j in range(1, split)}
    mixer_pieces = outer_blocks(
        me, normed, *flow.after(grad_mixer), normed_other, grad_mixer_other, picks
    )
    held = flow.until(*mixer_pieces, *[moved[j] for j in range(1, split)])
    mixer_pieces, early = held[:chips], held[chips:]
    for j, piece in enumerate(early, 1):
        chain.add(("feed", j), piece)
    chain.step()
    parts = scatter_end(scatter_start(flow.after(partial)[0]))
    input_grad, _, mixer_part = norm_back(
        mixer_gain, inputs, flow.after(grad_hidden)[0], *flow.until(*parts)
    )
    (input_grad,) = flow.until(input_grad)
    chain.step()
    for _ in range(split - 3):
        chain.step()
    gains = jnp.concatenate([mixer_part, feed_part]).reshape(2, 8, width // 8)
    gains, *mixer_pieces = flow.after(gains, *mixer_pieces)
    bits = 1
    while bits < devices:
        gains = gains + swap(gains, bits)
        bits = 2 * bits
    gains, *mixer_pieces = flow.until(
        gains, *[swap(mixer_pieces[j], 2 * j) if j else mixer_pieces[j] for j in range(chips)]
    )
    chain.add("mixer", jnp.stack(mixer_pieces), gains)
    chain.step()
    late = [swap(flow.after(pieces[j])[0], 2 * j) for j in range(split, chips)]
    down = product("rows", *flow.after(inner), down_all, full)
    down, *late = flow.until(down, *late)
    for j, piece in enumerate(late, split):
        chain.add(("feed", j), piece)
    chain.step()
    for _ in range(chips - split - 1):
        chain.step()
    parts = flow.until(*scatter_start(flow.after(down)[0]))
    chain.step()
    parts = flow.until(*scatter_end(flow.after(*parts)))
    layer_out = by_token((hidden + sum(part.astype(full) for part in parts)).astype(low))
    input_grad = by_token(input_grad)
    chain.finish()
    results = chain.results
    down_grad = jnp.concatenate([results["down", piece][0] for piece in range(2)], axis=0)
    down_grad = down_grad.astype(full)
    output_grad = results["output"][0].astype(full)
    done = [results["feed", j][0] for j in range(chips)]
    if hidden_width % 128:
        stacked = jnp.stack(done)
        ordered = jnp.stack([one_of(stacked, me // 2 ^ j) for j in range(chips)])
        ordered = ordered.astype(full).reshape(chips, shard_rows, 2, hidden_width)
        gate_grad, up_grad = ordered.transpose(2, 1, 0, 3).reshape(2, shard_rows, -1)
    else:
        held = ()
        for j, piece in enumerate(done):
            held = spread(me, j, piece, chips, held)
        gate_grad, up_grad = held
    mixer_grads = results["mixer"][0]
    mixer_grads = jnp.stack([one_of(mixer_grads, me // 2 ^ j) for j in range(chips)])
    mixer_grads = mixer_grads.astype(full)
    query_grad = mixer_grads[:, :, :query_width].transpose(1, 0, 2).reshape(shard_rows, -1)
    shared = (
        mixer_grads[:, :, query_width:]
        .reshape(KV_HEADS, sharing, shard_rows, 2, HEAD_DIM)
        .sum(axis=1)
    )
    key_grad = shared[:, :, 0].transpose(1, 0, 2).reshape(shard_rows, -1)
    value_grad = shared[:, :, 1].transpose(1, 0, 2).reshape(shard_rows, -1)
    mixer_total, feed_total = results["mixer"][1].reshape(2, width)
    return (
        layer_out,
        input_grad,
        mixer_total,
        query_grad,
        key_grad,
        value_grad,
        output_grad,
        feed_total,
        gate_grad,
        up_grad,
        down_grad,
    )


def solution(mesh):
    placed = (
        P("rep", None, "fsdp", None),
        P("rep", None, "fsdp", None),
        P(),
        P("fsdp", None),
        P("fsdp", None),
        P("fsdp", None),
        P("fsdp", None),
        P(),
        P("fsdp", None),
        P("fsdp", None),
        P("fsdp", None),
        P("rep", None, None),
        P("rep", None, None),
        P("rep", None, None),
    )
    return jax.shard_map(
        local,
        mesh=mesh,
        in_specs=placed,
        out_specs=(
            P("rep", None, "fsdp", None),
            P("rep", None, "fsdp", None),
            P(),
            P("fsdp", None),
            P("fsdp", None),
            P("fsdp", None),
            P("fsdp", None),
            P(),
            P("fsdp", None),
            P("fsdp", None),
            P("fsdp", None),
        ),
        check_vma=False,
    )
```
